32 devices in a mesh: gx: 8 (over z, core), gy: 4 (over y, x).
Axes of the slice: x: 2, y: 2, z: 4, core: 2. Of those that a mesh axis runs over, the one named last changes fastest.
Arguments:
- populations: float32 [19, 128, 32, 256], P(None, 'gx', 'gy'), may hold values from 0 to 0.5, as said below
- relax_rate: float32 [128, 32, 256], P('gx', 'gy'), may hold values from 0.6 to 1.6
- solid_mask: int32 [128, 32, 256], P('gx', 'gy'), may hold values 0 or 1
- singular_values: float32 [64], replicated, may hold values from 1 to 4
- basis: float32 [64, 3, 64, 16, 128], P(None, None, 'gx', 'gy'), may hold values from -60 to 60
- snapshots: float32 [15, 3, 64, 16, 128], P(None, None, 'gx', 'gy'), may hold values from -60 to 60
Outputs:
- populations_out: float32 [19, 128, 32, 256], P(None, 'gx', 'gy')
- upper_factor: float32 [80, 80], replicated
- new_basis: float32 [80, 3, 64, 16, 128], P(None, None, 'gx', 'gy')
The draws below stay inside these ranges and needn't reach their ends.
Inputs may be any that keep to these rules, and one draw needn't show every extreme that they name: `populations`: each entry is w_i times a factor between 0.7 and 1.3.
All inputs are finite; a program needn't handle non-finite values. No bound on the sum of `solid_mask` on one device may be relied on, other than what follows from the above.
Results may differ from the reference program's by a relative error of at most 0.00012.
Values sent between devices are 32-bit elements; how exact they have to be, the bound alone decides.
No kernel may reach another device: no remote copies, remote signals or barrier semaphores. Data moves between devices by JAX's collectives and lax.ppermute only.
A program may use at most 128 MiB of HBM per device.

```python
import math
import jax
import jax.numpy as jnp
from jax import lax

NVEL = 19
SUBSTEPS = 2
RANK = 64
SNAPS = 16
COLS = 80
NX = 128
NY = 32
NZ = 256
NXC = 64
NYC = 16
NZC = 128
ROWS_ALL = 393216


weight_table = [1.0 / 3.0] + [1.0 / 18.0] * 6 + [1.0 / 36.0] * 12


def draw_populations(key, part):
    shape = (NVEL, NX, NY, NZ)
    weights = jnp.array(weight_table, jnp.float32)[:, None, None, None]
    factor = 1.0 + 0.3 * jax.random.uniform(key, shape, jnp.float32, -1.0, 1.0)
    return weights * factor


def scaled_rows(key, count):
    shape = (count, 3, NXC, NYC, NZC)
    ix = jnp.arange(NXC, dtype=jnp.float32)[:, None, None] / (NXC - 1)
    iy = jnp.arange(NYC, dtype=jnp.float32)[None, :, None] / (NYC - 1)
    spread = 10.0 ** ((ix + iy) * 0.5)
    first = jax.random.fold_in(key, 11)
    values = jnp.clip(jax.random.normal(first, shape, jnp.float32), -6.0, 6.0)
    return values * spread


def draw_basis(key, part):
    return scaled_rows(jax.random.fold_in(key, 101), RANK)


def draw_snapshots(key, part):
    return scaled_rows(jax.random.fold_in(key, 202), SNAPS - 1)


def touch_ends(values, rng, low, largest):
    extent = values.shape
    spot = [jax.random.randint(jax.random.fold_in(rng, axis), (), 0, extent[axis]) for axis in range(len(extent))]
    values = values.at[tuple(spot)].set(low)
    longest = extent.index(max(extent))
    spot[longest] = (spot[longest] + 1) % extent[longest]
    return values.at[tuple(spot)].set(largest)


def block_levels(own_key, shape, shards, low, high):
    level = 1.0
    for dim, shards_of in shards:
        steps = jax.random.uniform(jax.random.fold_in(jax.random.fold_in(own_key, 6), dim), (shards_of,), jnp.float32, low / len(shards), high / len(shards))
        level = level * jnp.repeat(jnp.exp(steps), shape[dim] // shards_of).reshape((-1,) + (1,) * (len(shape) - 1 - dim))
    return level


def setup_inputs(seed: int = 0) -> dict:
    splits = jax.random.split(jax.random.key(seed), 7)
    return {
        "populations": draw_populations(jax.random.fold_in(splits[6], 71), 0),
        "relax_rate": jnp.clip(0.6 + 1.0 * jax.random.uniform(splits[1], (NX, NY, NZ), jnp.float32) ** block_levels(splits[1], (NX, NY, NZ), ((0, 8), (1, 4)), -0.2, 0.2), 0.6, 1.6),
        "solid_mask": touch_ends((jax.random.randint(splits[2], (NX, NY, NZ), 0, 8) < 1).astype(jnp.int32), jax.random.fold_in(splits[2], 1), 0, 1),
        "singular_values": jnp.clip(jnp.exp(jax.random.uniform(splits[3], (RANK,), jnp.float32, math.log(1.0), math.log(4.0))), 1.0, 4.0),
        "basis": draw_basis(jax.random.fold_in(splits[6], 71), 0),
        "snapshots": draw_snapshots(jax.random.fold_in(splits[6], 71), 0),
    }


velocity_table = [(0, 0, 0), (1, 0, 0), (-1, 0, 0), (0, 1, 0), (0, -1, 0), (0, 0, 1), (0, 0, -1), (1, 1, 0), (-1, -1, 0), (1, -1, 0), (-1, 1, 0), (1, 0, 1), (-1, 0, -1), (1, 0, -1), (-1, 0, 1), (0, 1, 1), (0, -1, -1), (0, 1, -1), (0, -1, 1)]
weight_table = [1.0 / 3.0] + [1.0 / 18.0] * 6 + [1.0 / 36.0] * 12
reverse_table = [0, 2, 1, 4, 3, 6, 5, 8, 7, 10, 9, 12, 11, 14, 13, 16, 15, 18, 17]
speed_scale = 10.0

def moments(field):
    highest = lax.Precision.HIGHEST
    density = jnp.sum(field, axis=0)
    comps = []
    for axis_id in range(3):
        column = jnp.array([v[axis_id] for v in velocity_table], jnp.float32)
        comps.append(jnp.tensordot(column, field, axes=1, precision=highest) / density)
    return (density, comps)

def collide(field, relax_rate, solid_mask):
    density, comps = moments(field)
    usq = comps[0] * comps[0] + comps[1] * comps[1] + comps[2] * comps[2]
    result = []
    for index in range(19):
        vel = velocity_table[index]
        along = vel[0] * comps[0] + vel[1] * comps[1] + vel[2] * comps[2]
        equil = weight_table[index] * density * (1.0 + 3.0 * along + 4.5 * along * along - 1.5 * usq)
        relaxed = field[index] + relax_rate * (equil - field[index])
        result.append(jnp.where(solid_mask > 0, field[reverse_table[index]], relaxed))
    return result

def reference(populations, relax_rate, solid_mask, singular_values, basis, snapshots):
    field = populations
    for step in range(SUBSTEPS):
        post = collide(field, relax_rate, solid_mask)
        field = jnp.stack([jnp.roll(post[i], velocity_table[i], axis=(0, 1, 2)) for i in range(19)])
    density, comps = moments(field)
    fluid = (solid_mask == 0).astype(jnp.float32)
    vel = jnp.stack([c * fluid for c in comps])
    coarse = speed_scale * jnp.mean(vel.reshape(3, NXC, 2, NYC, 2, NZC, 2), axis=(2, 4, 6))
    stacked = jnp.concatenate([singular_values[:, None, None, None, None] * basis, snapshots, coarse[None]], axis=0)
    flat = stacked.reshape(COLS, ROWS_ALL)
    scaled = flat * (1.0 / ROWS_ALL ** 0.5)
    gram = lax.dot_general(scaled.astype(jnp.float32), scaled.astype(jnp.float32), (((1,), (1,)), ((), ())), precision=lax.Precision.HIGHEST, preferred_element_type=jnp.float32)
    lower = jnp.linalg.cholesky(gram)
    rotated = lax.linalg.triangular_solve(lower, flat, left_side=True, lower=True)
    return (field, lower.T, rotated.reshape(COLS, 3, NXC, NYC, NZC))
```

```python
import jax
import jax.numpy as jnp
from jax import lax
from jax.experimental import pallas as pl
from jax.experimental.pallas import tpu as pltpu
from jax.sharding import PartitionSpec as P

velocity_table = [
    (0, 0, 0),
    (1, 0, 0),
    (-1, 0, 0),
    (0, 1, 0),
    (0, -1, 0),
    (0, 0, 1),
    (0, 0, -1),
    (1, 1, 0),
    (-1, -1, 0),
    (1, -1, 0),
    (-1, 1, 0),
    (1, 0, 1),
    (-1, 0, -1),
    (1, 0, -1),
    (-1, 0, 1),
    (0, 1, 1),
    (0, -1, -1),
    (0, 1, -1),
    (0, -1, 1),
]
NVEL = 19
PAIRS = [(i, i + 1) for i in range(1, NVEL, 2)]
W_REST, W_FACE, W_EDGE = 1.0 / 3.0, 1.0 / 18.0, 1.0 / 36.0
UP_X = [i for i in range(NVEL) if velocity_table[i][0] == 1]
DOWN_X = [i for i in range(NVEL) if velocity_table[i][0] == -1]
UP_Y = [i for i in range(NVEL) if velocity_table[i][1] == 1]
DOWN_Y = [i for i in range(NVEL) if velocity_table[i][1] == -1]
SPEED_SCALE = 10.0
HIGHEST = lax.Precision.HIGHEST
F32 = jnp.float32
BF16 = jnp.bfloat16


def params(mib=40):
    return pltpu.CompilerParams(vmem_limit_bytes=mib << 20)


def shifted(value, axis, steps):
    count = lax.axis_size(axis)
    return lax.ppermute(value, axis, [(s, (s + steps) % count) for s in range(count)])


def moments(f):
    plus = [f[a] + f[b] for a, b in PAIRS]
    minus = [f[a] - f[b] for a, b in PAIRS]
    rho = f[0] + plus[0]
    for p in plus[1:]:
        rho = rho + p
    mx, my, mz, m7, m9, m11, m13, m15, m17 = minus
    jx = (mx + m7) + (m9 + m11) + m13
    jy = (my + m7) + (m15 + m17) - m9
    jz = (mz + m11) + (m15 - m13) - m17
    r = 1.0 / rho
    return rho, (jx * r, jy * r, jz * r)


def collide(f, omega, solid):
    rho, u = moments(f)
    base = 1.0 - 1.5 * (u[0] * u[0] + u[1] * u[1] + u[2] * u[2])
    keep = 1.0 - omega
    wr = omega * rho
    post = [None] * NVEL
    post[0] = jnp.where(solid, f[0], keep * f[0] + (W_REST * wr) * base)
    w_face, w_edge = W_FACE * wr, W_EDGE * wr
    for a, b in PAIRS:
        vel = velocity_table[a]
        along = None
        for axis in range(3):
            if vel[axis] == 1:
                along = u[axis] if along is None else along + u[axis]
            elif vel[axis] == -1:
                along = along - u[axis]
        w = w_face if a < 7 else w_edge
        even = w * (base + 4.5 * (along * along))
        odd = w * (3.0 * along)
        post[a] = jnp.where(solid, f[b], keep * f[a] + (even + odd))
        post[b] = jnp.where(solid, f[a], keep * f[b] + (even - odd))
    return post


def emit_post(post, x, nx, post_ref, xup_ref, xdn_ref, yup_ref, ydn_ref):
    ny = post_ref.shape[2]
    for i in range(NVEL):
        cz = velocity_table[i][2]
        value = post[i] if cz == 0 else pltpu.roll(post[i], cz % post[i].shape[1], 1)
        post_ref[i, x] = value
        cx = velocity_table[i][0]
        row = lax.rem(x + (cx + nx), nx)
        if i in UP_Y:
            yup_ref[pl.ds(UP_Y.index(i) * nx + row, 1), :] = value[ny - 1 : ny, :]
        if i in DOWN_Y:
            ydn_ref[pl.ds(DOWN_Y.index(i) * nx + row, 1), :] = value[0:1, :]


def emit_faces(nx, post_ref, xup_ref, xdn_ref):
    for k, i in enumerate(UP_X):
        xup_ref[k] = post_ref[i, nx - 1]
    for k, i in enumerate(DOWN_X):
        xdn_ref[k] = post_ref[i, 0]


def first_kernel(f_ref, om_ref, so_ref, post_ref, xup_ref, xdn_ref, yup_ref, ydn_ref):
    nx = f_ref.shape[1]

    def step(x, carry):
        post = collide([f_ref[i, x] for i in range(NVEL)], om_ref[x], so_ref[x] > 0)
        emit_post(post, x, nx, post_ref, xup_ref, xdn_ref, yup_ref, ydn_ref)
        return carry

    lax.fori_loop(0, nx, step, 0)
    emit_faces(nx, post_ref, xup_ref, xdn_ref)


def streamed(x, nx, post_ref, xup_ref, xdn_ref, yup_ref, ydn_ref):
    ny = post_ref.shape[2]
    row_id = lax.broadcasted_iota(jnp.int32, (ny, post_ref.shape[3]), 0)
    f = []
    for i in range(NVEL):
        cx, cy, _ = velocity_table[i]
        if cx == 1:
            value = jnp.where(x == 0, xup_ref[UP_X.index(i)], post_ref[i, lax.rem(x + nx - 1, nx)])
        elif cx == -1:
            value = jnp.where(
                x == nx - 1, xdn_ref[DOWN_X.index(i)], post_ref[i, lax.rem(x + 1, nx)]
            )
        else:
            value = post_ref[i, x]
        if cy == 1:
            edge = yup_ref[pl.ds(UP_Y.index(i) * nx + x, 1), :]
            value = jnp.where(row_id == 0, edge, pltpu.roll(value, 1, 0))
        elif cy == -1:
            edge = ydn_ref[pl.ds(DOWN_Y.index(i) * nx + x, 1), :]
            value = jnp.where(row_id == ny - 1, edge, pltpu.roll(value, ny - 1, 0))
        f.append(value)
    return f


def second_kernel(
    p_ref, xu_ref, xd_ref, yu_ref, yd_ref, om_ref, so_ref, post_ref, xup_ref, xdn_ref, yup_ref, ydn_ref
):
    nx = p_ref.shape[1]

    def step(x, carry):
        f = streamed(x, nx, p_ref, xu_ref, xd_ref, yu_ref, yd_ref)
        post = collide(f, om_ref[x], so_ref[x] > 0)
        emit_post(post, x, nx, post_ref, xup_ref, xdn_ref, yup_ref, ydn_ref)
        return carry

    lax.fori_loop(0, nx, step, 0)
    emit_faces(nx, post_ref, xup_ref, xdn_ref)


def pack_kernel(xu_ref, xd_ref, yup_ref, ydn_ref, ou_ref, od_ref):
    nx = yup_ref.shape[0] // len(UP_Y)
    ny = xu_ref.shape[1]
    ou_ref[...] = yup_ref[...]
    od_ref[...] = ydn_ref[...]
    for ids, out, row in ((UP_Y, ou_ref, ny - 1), (DOWN_Y, od_ref, 0)):
        for k, i in enumerate(ids):
            if velocity_table[i][0] == 1:
                out[k * nx : k * nx + 1, :] = xu_ref[UP_X.index(i), row : row + 1, :]
            elif velocity_table[i][0] == -1:
                at = k * nx + nx - 1
                out[at : at + 1, :] = xd_ref[DOWN_X.index(i), row : row + 1, :]


def gram_kernel(s_ref, basis_ref, snap_ref, a_ref, h_ref, g_ref):
    rank = basis_ref.shape[0]
    depth = basis_ref.shape[1]
    extra = snap_ref.shape[0]
    cols = a_ref.shape[1]
    basis = basis_ref.reshape(rank * depth, 128)
    snaps = snap_ref.reshape(extra * depth, 128)
    scale = jnp.broadcast_to(s_ref[...], (rank, 128))
    zero = jnp.zeros((cols - rank - extra, 128), F32)

    def step(q, acc):
        for t in range(2):
            r = 2 * q + t
            a_ref[r, 0:rank, :] = basis[pl.ds(r, rank, stride=depth), :] * scale
            a_ref[r, rank : rank + extra, :] = snaps[pl.ds(r, extra, stride=depth), :]
            a_ref[r, rank + extra : cols, :] = zero
        rows = jnp.concatenate([a_ref[2 * q], a_ref[2 * q + 1]], axis=1)
        high = rows.astype(BF16)
        low = (rows - high.astype(F32)).astype(BF16)
        both = jnp.concatenate([high, low], axis=0)
        h_ref[q] = both
        return acc + lax.dot_general(
            both, high, (((1,), (1,)), ((), ())), preferred_element_type=F32
        )

    acc = lax.fori_loop(0, depth // 2, step, jnp.zeros((2 * cols, cols), F32))
    cross = acc[cols:, :]
    eye = (
        lax.broadcasted_iota(jnp.int32, (cols, cols), 0)
        == lax.broadcasted_iota(jnp.int32, (cols, cols), 1)
    ).astype(F32)
    flipped = lax.dot_general(
        eye, cross, (((1,), (1,)), ((), ())), precision=HIGHEST, preferred_element_type=F32
    )
    g_ref[...] = acc[:cols, :] + cross + flipped


def factor_kernel(inv_rows, g_ref, u_ref, li_ref, w_ref):
    cols = g_ref.shape[0]
    known = cols - 1
    row_id = lax.broadcasted_iota(jnp.int32, (cols, cols), 0)
    col_id = lax.broadcasted_iota(jnp.int32, (cols, cols), 1)
    left = g_ref[...] * inv_rows
    right = (row_id == col_id).astype(F32)
    down = lax.broadcasted_iota(jnp.int32, (cols, 1), 0)
    for j in range(known):
        column = left[:, j : j + 1]
        pivot = lax.rsqrt(left[j : j + 1, j : j + 1])
        scaled = column * pivot
        step = jnp.where(down > j, scaled, 0.0)
        top = left[j : j + 1, :] * pivot
        aug = right[j : j + 1, :] * pivot
        here = down == j
        left = jnp.where(here, top, left - step * top)
        right = jnp.where(here, aug, right - step * aug)
    keep = jnp.logical_and(row_id <= col_id, col_id < known)
    u_ref[...] = jnp.where(keep, left, 0.0)
    inverse = jnp.where(jnp.logical_and(row_id >= col_id, row_id < known), right, 0.0)
    li_ref[...] = inverse
    high = inverse.astype(BF16)
    w_ref[0] = high
    w_ref[1] = (inverse - high.astype(F32)).astype(BF16)


def rotate_kernel(w_ref, h_ref, o_ref):
    cols = w_ref.shape[1]
    depth = o_ref.shape[1]
    out = o_ref.reshape(cols * depth, 128)
    whigh, wlow = w_ref[0], w_ref[1]

    def step(q, carry):
        high = h_ref[q, 0:cols, :]
        low = h_ref[q, cols:, :]
        dims = (((1,), (0,)), ((), ()))
        res = lax.dot_general(whigh, high, dims, preferred_element_type=F32)
        res = res + lax.dot_general(wlow, high, dims, preferred_element_type=F32)
        res = res + lax.dot_general(whigh, low, dims, preferred_element_type=F32)
        out[pl.ds(2 * q, cols, stride=depth), :] = res[:, :128]
        out[pl.ds(2 * q + 1, cols, stride=depth), :] = res[:, 128:]
        return carry

    lax.fori_loop(0, depth // 2, step, 0)


def final_kernel(
    p_ref, xu_ref, xd_ref, yu_ref, yd_ref, so_ref, a_ref, f_ref, c_ref, v_ref, vel_ref
):
    nx, ny, nz = p_ref.shape[1:]
    nxc, nyc = nx // 2, ny // 2

    def step(xc, carry):
        total = [None] * 3
        for t in range(2):
            x = 2 * xc + t
            f = streamed(x, nx, p_ref, xu_ref, xd_ref, yu_ref, yd_ref)
            for i in range(NVEL):
                f_ref[i, x] = f[i]
            _, u = moments(f)
            fluid = (so_ref[x] == 0).astype(F32)
            for k in range(3):
                part = u[k] * fluid
                total[k] = part if t == 0 else total[k] + part
        for k in range(3):
            at = pl.multiple_of((k * nxc + xc) * ny, ny)
            for t in range(nz // 128):
                vel_ref[t, pl.ds(at, ny), :] = total[k][:, t * 128 : (t + 1) * 128]
        return carry

    lax.fori_loop(0, nxc, step, 0)
    depth = 3 * nxc * nyc
    pairs = []
    for t in range(nz // 128):
        half = vel_ref.at[t]
        pairs.append(half[pl.ds(0, depth, stride=2), :] + half[pl.ds(1, depth, stride=2), :])
    pairs = jnp.concatenate(pairs, axis=1)
    pick = (
        lax.broadcasted_iota(jnp.int32, (nz, nz // 2), 0) // 2
        == lax.broadcasted_iota(jnp.int32, (nz, nz // 2), 1)
    ).astype(F32)
    coarse = lax.dot_general(
        pairs, pick, (((1,), (0,)), ((), ())), precision=HIGHEST, preferred_element_type=F32
    )
    c_ref[...] = coarse * (SPEED_SCALE / 8.0)
    cols = a_ref.shape[1]

    def inner(r, acc):
        return acc + a_ref[r] * c_ref[pl.ds(r, 1), :]

    acc = lax.fori_loop(0, depth, inner, jnp.zeros((cols, 128), F32))
    dots = jnp.sum(acc, axis=1, keepdims=True)
    own = jnp.sum(c_ref[...] * c_ref[...])
    down = lax.broadcasted_iota(jnp.int32, (cols, 1), 0)
    dots = jnp.where(down == cols - 1, own, dots)
    across = lax.broadcasted_iota(jnp.int32, (cols, 128), 1)
    diag = jnp.where(across == lax.broadcasted_iota(jnp.int32, (cols, 128), 0), dots, 0.0)
    line = jnp.sum(diag, axis=0, keepdims=True)
    v_ref[...] = jnp.broadcast_to(line, v_ref.shape)


def last_kernel(inv_rows, v_ref, li_ref, u_ref, a_ref, c_ref, q_ref, uo_ref, o_ref, row_ref, sem):
    cols = li_ref.shape[0]
    known = cols - 1
    depth = c_ref.shape[0]
    line = jnp.sum(v_ref[...], axis=0, keepdims=True)[:, :cols] * inv_rows
    across = lax.broadcasted_iota(jnp.int32, (1, cols), 1)
    norm = jnp.sum(jnp.where(across == known, line, 0.0), axis=1, keepdims=True)
    inverse = li_ref[...]
    coef = jnp.sum(inverse * jnp.where(across == known, 0.0, line), axis=1, keepdims=True)
    pivot = lax.rsqrt(norm - jnp.sum(coef * coef, axis=0, keepdims=True))
    left = norm - jnp.sum(coef * coef, axis=0, keepdims=True)
    col_id = lax.broadcasted_iota(jnp.int32, (cols, cols), 1)
    row_id = lax.broadcasted_iota(jnp.int32, (cols, cols), 0)
    edge = jnp.where(row_id == known, left * pivot, coef)
    uo_ref[...] = jnp.where(col_id == known, edge, u_ref[...])
    weight = jnp.sum(inverse * coef, axis=0, keepdims=True) * (-pivot)
    diag = jnp.where(row_id == col_id, weight, 0.0)
    tall = jnp.sum(diag, axis=1, keepdims=True)
    tall = jnp.broadcast_to(tall, (cols, 128))

    def step(r, carry):
        part = jnp.sum(a_ref[r] * tall, axis=0, keepdims=True)
        row_ref[pl.ds(r, 1), :] = part + c_ref[pl.ds(r, 1), :] * pivot
        return carry

    lax.fori_loop(0, depth, step, 0)
    copy = pltpu.make_async_copy(row_ref, o_ref.at[known], sem)
    copy.start()
    copy.wait()


def shape(dims, dtype=F32):
    return jax.ShapeDtypeStruct(dims, dtype)


def halo_x(xup, xdn):
    return shifted(xup, "gx", 1), shifted(xdn, "gx", -1)


def halo_y(xu, xd, yup, ydn):
    send_up, send_dn = pl.pallas_call(
        pack_kernel, out_shape=(shape(yup.shape), shape(ydn.shape)), name="pack", compiler_params=params(8)
    )(xu, xd, yup, ydn)
    return shifted(send_up, "gy", 1), shifted(send_dn, "gy", -1)


def sum_everywhere(value):
    for axis in ("gy", "gx"):
        count = lax.axis_size(axis)
        bit = 1
        while bit < count:
            value = value + lax.ppermute(value, axis, [(s, s ^ bit) for s in range(count)])
            bit *= 2
    return value


def on_device(populations, relax_rate, solid_mask, singular_values, basis, snapshots):
    _, nx, ny, nz = populations.shape
    rank, extra = basis.shape[0], snapshots.shape[0]
    cols = rank + extra + 1
    tail = basis.shape[1:]
    depth = tail[0] * tail[1] * tail[2]
    n_dev = lax.axis_size("gx") * lax.axis_size("gy")
    inv_rows = 1.0 / (depth * tail[3] * n_dev)
    edges = len(UP_Y) * nx
    post_shapes = (
        shape((NVEL, nx, ny, nz)),
        shape((len(UP_X), ny, nz)),
        shape((len(DOWN_X), ny, nz)),
        shape((edges, nz)),
        shape((edges, nz)),
    )
    post, xup, xdn, yup, ydn = pl.pallas_call(
        first_kernel, out_shape=post_shapes, name="first", compiler_params=params(16)
    )(populations, relax_rate, solid_mask)
    xu, xd = halo_x(xup, xdn)
    rows, halves, gram = pl.pallas_call(
        gram_kernel,
        out_shape=(
            shape((depth, cols, 128)),
            shape((depth // 2, 2 * cols, 256), BF16),
            shape((cols, cols)),
        ),
        name="gram",
        compiler_params=params(24),
    )(
        singular_values.reshape(rank, 1),
        basis.reshape(rank, depth, 128),
        snapshots.reshape(extra, depth, 128),
    )
    yu, yd = halo_y(xu, xd, yup, ydn)
    gram = sum_everywhere(gram)
    post, xup, xdn, yup, ydn = pl.pallas_call(
        second_kernel, out_shape=post_shapes, name="second", compiler_params=params(16)
    )(post, xu, xd, yu, yd, relax_rate, solid_mask)
    xu, xd = halo_x(xup, xdn)
    upper, inverse, split = pl.pallas_call(
        lambda *refs: factor_kernel(inv_rows, *refs),
        out_shape=(shape((cols, cols)), shape((cols, cols)), shape((2, cols, cols), BF16)),
        name="factor",
        compiler_params=params(8),
    )(gram)
    yu, yd = halo_y(xu, xd, yup, ydn)
    rotated = pl.pallas_call(
        rotate_kernel, out_shape=shape((cols, depth, 128)), name="rotate", compiler_params=params(16)
    )(split, halves)
    field, coarse, line = pl.pallas_call(
        final_kernel,
        out_shape=(shape((NVEL, nx, ny, nz)), shape((depth, 128)), shape((n_dev, 128))),
        scratch_shapes=[pltpu.VMEM((nz // 128, 3 * (nx // 2) * ny, 128), F32)],
        name="final",
        compiler_params=params(24),
    )(post, xu, xd, yu, yd, solid_mask, rows)
    lines = lax.all_to_all(line, ("gx", "gy"), 0, 0, tiled=True)
    vmem = pl.BlockSpec(memory_space=pltpu.VMEM)
    hbm = pl.BlockSpec(memory_space=pl.ANY)
    upper, rotated = pl.pallas_call(
        lambda *refs: last_kernel(inv_rows, *refs),
        out_shape=(shape((cols, cols)), shape((cols, depth, 128))),
        in_specs=[vmem] * 5 + [hbm],
        out_specs=(vmem, hbm),
        scratch_shapes=[pltpu.VMEM((depth, 128), F32), pltpu.SemaphoreType.DMA],
        input_output_aliases={5: 1},
        name="last",
        compiler_params=params(16),
    )(lines, inverse, upper, rows, coarse, rotated)
    return field, upper, rotated.reshape((cols,) + tail)


def solution(mesh):
    return jax.shard_map(
        on_device,
        mesh=mesh,
        in_specs=(
            P(None, "gx", "gy", None),
            P("gx", "gy", None),
            P("gx", "gy", None),
            P(),
            P(None, None, "gx", "gy", None),
            P(None, None, "gx", "gy", None),
        ),
        out_specs=(P(None, "gx", "gy", None), P(), P(None, None, "gx", "gy", None)),
        check_vma=False,
    )
```

```python
import jax
import jax.numpy as jnp
from jax import lax
from jax.experimental import pallas as pl
from jax.experimental.pallas import tpu as pltpu
from jax.sharding import PartitionSpec as P

velocity_table = [
    (0, 0, 0),
    (1, 0, 0),
    (-1, 0, 0),
    (0, 1, 0),
    (0, -1, 0),
    (0, 0, 1),
    (0, 0, -1),
    (1, 1, 0),
    (-1, -1, 0),
    (1, -1, 0),
    (-1, 1, 0),
    (1, 0, 1),
    (-1, 0, -1),
    (1, 0, -1),
    (-1, 0, 1),
    (0, 1, 1),
    (0, -1, -1),
    (0, 1, -1),
    (0, -1, 1),
]
NVEL = 19
PAIRS = [(i, i + 1) for i in range(1, NVEL, 2)]
W_REST, W_FACE, W_EDGE = 1.0 / 3.0, 1.0 / 18.0, 1.0 / 36.0
UP_X = [i for i in range(NVEL) if velocity_table[i][0] == 1]
DOWN_X = [i for i in range(NVEL) if velocity_table[i][0] == -1]
UP_Y = [i for i in range(NVEL) if velocity_table[i][1] == 1]
DOWN_Y = [i for i in range(NVEL) if velocity_table[i][1] == -1]
SPEED_SCALE = 10.0
HIGHEST = lax.Precision.HIGHEST
F32 = jnp.float32
BF16 = jnp.bfloat16
VMEM = pl.BlockSpec(memory_space=pltpu.VMEM)
ANY = pl.BlockSpec(memory_space=pl.ANY)
HBM = pl.BlockSpec(memory_space=pltpu.HBM)


def params(mib=40):
    return pltpu.CompilerParams(vmem_limit_bytes=mib << 20)


def shifted(value, axis, steps):
    count = lax.axis_size(axis)
    return lax.ppermute(value, axis, [(s, (s + steps) % count) for s in range(count)])


def moments(f):
    plus = [f[a] + f[b] for a, b in PAIRS]
    minus = [f[a] - f[b] for a, b in PAIRS]
    rho = f[0] + plus[0]
    for p in plus[1:]:
        rho = rho + p
    mx, my, mz, m7, m9, m11, m13, m15, m17 = minus
    jx = (mx + m7) + (m9 + m11) + m13
    jy = (my + m7) + (m15 + m17) - m9
    jz = (mz + m11) + (m15 - m13) - m17
    r = 1.0 / rho
    return rho, (jx * r, jy * r, jz * r)


def collide(f, omega, solid):
    rho, u = moments(f)
    base = 1.0 - 1.5 * (u[0] * u[0] + u[1] * u[1] + u[2] * u[2])
    keep = 1.0 - omega
    wr = omega * rho
    post = [None] * NVEL
    post[0] = jnp.where(solid, f[0], keep * f[0] + (W_REST * wr) * base)
    w_face, w_edge = W_FACE * wr, W_EDGE * wr
    for a, b in PAIRS:
        vel = velocity_table[a]
        along = None
        for axis in range(3):
            if vel[axis] == 1:
                along = u[axis] if along is None else along + u[axis]
            elif vel[axis] == -1:
                along = along - u[axis]
        w = w_face if a < 7 else w_edge
        even = w * (base + 4.5 * (along * along))
        odd = w * (3.0 * along)
        post[a] = jnp.where(solid, f[b], keep * f[a] + (even + odd))
        post[b] = jnp.where(solid, f[a], keep * f[b] + (even - odd))
    return post


def emit_post(post, x, nx, post_ref, xup_ref, xdn_ref, yup_ref, ydn_ref):
    ny = post_ref.shape[2]
    for i in range(NVEL):
        cz = velocity_table[i][2]
        value = post[i] if cz == 0 else pltpu.roll(post[i], cz % post[i].shape[1], 1)
        post_ref[i, x] = value
        cx = velocity_table[i][0]
        row = lax.rem(x + (cx + nx), nx)
        if i in UP_Y:
            yup_ref[pl.ds(UP_Y.index(i) * nx + row, 1), :] = value[ny - 1 : ny, :]
        if i in DOWN_Y:
            ydn_ref[pl.ds(DOWN_Y.index(i) * nx + row, 1), :] = value[0:1, :]


def emit_faces(nx, post_ref, xup_ref, xdn_ref):
    for k, i in enumerate(UP_X):
        xup_ref[k] = post_ref[i, nx - 1]
    for k, i in enumerate(DOWN_X):
        xdn_ref[k] = post_ref[i, 0]


def first_kernel(
    f_hbm, om_hbm, so_hbm, post_ref, xup_ref, xdn_ref, yup_ref, ydn_ref, om_ref, so_ref, f_ref, sem
):
    nx = f_ref.shape[1]
    parts = sem.shape[0] - 2
    rows = nx // parts

    def load(k):
        at = pl.ds(k * rows, rows)
        return pltpu.make_async_copy(f_hbm.at[:, at], f_ref.at[:, at], sem.at[k])

    loads = [load(k) for k in range(parts)]
    omega = pltpu.make_async_copy(om_hbm, om_ref, sem.at[parts])
    solid = pltpu.make_async_copy(so_hbm, so_ref, sem.at[parts + 1])
    loads[0].start()
    omega.start()
    solid.start()
    for k in range(1, parts):
        loads[k].start()

    def step(x, carry):
        post = collide([f_ref[i, x] for i in range(NVEL)], om_ref[x], so_ref[x] > 0)
        emit_post(post, x, nx, post_ref, xup_ref, xdn_ref, yup_ref, ydn_ref)
        return carry

    for k in range(parts):
        loads[k].wait()
        if k == 0:
            omega.wait()
            solid.wait()
        lax.fori_loop(k * rows, (k + 1) * rows, step, 0)
    emit_faces(nx, post_ref, xup_ref, xdn_ref)


def streamed(x, nx, post_ref, xup_ref, xdn_ref, yup_ref, ydn_ref):
    ny = post_ref.shape[2]
    row_id = lax.broadcasted_iota(jnp.int32, (ny, post_ref.shape[3]), 0)
    f = []
    for i in range(NVEL):
        cx, cy, _ = velocity_table[i]
        if cx == 1:
            value = jnp.where(x == 0, xup_ref[UP_X.index(i)], post_ref[i, lax.rem(x + nx - 1, nx)])
        elif cx == -1:
            value = jnp.where(
                x == nx - 1, xdn_ref[DOWN_X.index(i)], post_ref[i, lax.rem(x + 1, nx)]
            )
        else:
            value = post_ref[i, x]
        if cy == 1:
            edge = yup_ref[pl.ds(UP_Y.index(i) * nx + x, 1), :]
            value = jnp.where(row_id == 0, edge, pltpu.roll(value, 1, 0))
        elif cy == -1:
            edge = ydn_ref[pl.ds(DOWN_Y.index(i) * nx + x, 1), :]
            value = jnp.where(row_id == ny - 1, edge, pltpu.roll(value, ny - 1, 0))
        f.append(value)
    return f


def second_kernel(
    p_ref,
    xu_ref,
    xd_ref,
    yu_ref,
    yd_ref,
    om_ref,
    so_ref,
    gate_ref,
    post_ref,
    xup_ref,
    xdn_ref,
    yup_ref,
    ydn_ref,
):
    nx = p_ref.shape[1]

    def step(x, carry):
        f = streamed(x, nx, p_ref, xu_ref, xd_ref, yu_ref, yd_ref)
        post = collide(f, om_ref[x], so_ref[x] > 0)
        emit_post(post, x, nx, post_ref, xup_ref, xdn_ref, yup_ref, ydn_ref)
        return carry

    lax.fori_loop(0, nx, step, 0)
    emit_faces(nx, post_ref, xup_ref, xdn_ref)


def pack_kernel(xu_ref, xd_ref, yup_ref, ydn_ref, gate_ref, ou_ref, od_ref):
    nx = yup_ref.shape[0] // len(UP_Y)
    ny = xu_ref.shape[1]
    ou_ref[...] = yup_ref[...]
    od_ref[...] = ydn_ref[...]
    for ids, out, row in ((UP_Y, ou_ref, ny - 1), (DOWN_Y, od_ref, 0)):
        for k, i in enumerate(ids):
            if velocity_table[i][0] == 1:
                out[k * nx : k * nx + 1, :] = xu_ref[UP_X.index(i), row : row + 1, :]
            elif velocity_table[i][0] == -1:
                at = k * nx + nx - 1
                out[at : at + 1, :] = xd_ref[DOWN_X.index(i), row : row + 1, :]


def gram_kernel(s_ref, basis_ref, snap_ref, gate_ref, a_ref, h_ref, g_ref):
    rank = basis_ref.shape[0]
    depth = basis_ref.shape[1]
    extra = snap_ref.shape[0]
    cols = a_ref.shape[1]
    same = lax.broadcasted_iota(jnp.int32, (rank, rank), 0) == lax.broadcasted_iota(
        jnp.int32, (rank, rank), 1
    )
    scale = jnp.sum(jnp.where(same, s_ref[...], 0.0), axis=1, keepdims=True)
    scale = jnp.broadcast_to(scale, (rank, 128))
    zero = jnp.zeros((cols - rank - extra, 8, 128), F32)

    def step(q, carry):
        r = pl.multiple_of(q * 8, 8)
        top = jnp.swapaxes(basis_ref[:, pl.ds(r, 8), :], 0, 1)
        low = jnp.concatenate([snap_ref[:, pl.ds(r, 8), :], zero], axis=0)
        low = jnp.swapaxes(low, 0, 1)
        for t in range(8):
            rows = jnp.concatenate([top[t] * scale, low[t]], axis=0)
            a_ref[r + t] = rows
            at = pl.ds(pl.multiple_of((r + t) * 128, 128), 128)
            high = rows.astype(BF16)
            h_ref[0:cols, at] = high
            h_ref[cols : 2 * cols, at] = (rows - high.astype(F32)).astype(BF16)
        return carry

    lax.fori_loop(0, depth // 8, step, 0)
    acc = lax.dot_general(
        h_ref[...], h_ref[0:cols, :], (((1,), (1,)), ((), ())), preferred_element_type=F32
    )
    cross = acc[cols:, :]
    eye = (
        lax.broadcasted_iota(jnp.int32, (cols, cols), 0)
        == lax.broadcasted_iota(jnp.int32, (cols, cols), 1)
    ).astype(F32)
    flipped = lax.dot_general(
        eye, cross, (((1,), (1,)), ((), ())), precision=HIGHEST, preferred_element_type=F32
    )
    g_ref[...] = acc[:cols, :] + cross + flipped


def factor_kernel(inv_rows, g_ref, u_ref, li_ref, w_ref):
    cols = g_ref.shape[0]
    known = cols - 1
    blocks = cols // 8
    pad = jnp.zeros((8, 128 - cols), F32)
    sub = lax.broadcasted_iota(jnp.int32, (8, 128), 0)
    lane = lax.broadcasted_iota(jnp.int32, (8, 128), 1)
    left = [
        jnp.concatenate([g_ref[8 * b : 8 * b + 8, :] * inv_rows, pad], axis=1) for b in range(blocks)
    ]
    right = [(sub + 8 * b == lane).astype(F32) for b in range(blocks)]
    for p in range(blocks):
        live = range(p, blocks)
        width = min(8, known - 8 * p)
        col = [
            {
                b: jnp.broadcast_to(left[b][:, 8 * p + t : 8 * p + t + 1], (8, 128))
                for b in live
            }
            for t in range(width)
        ]
        for t in range(width):
            pivot = lax.rsqrt(jnp.broadcast_to(col[t][p][t : t + 1, :], (8, 128)))
            lcol = {b: col[t][b] * pivot for b in live}
            lcol[p] = jnp.where(sub > t, lcol[p], 0.0)
            for v in range(t + 1, width):
                m = jnp.broadcast_to(lcol[p][v : v + 1, :], (8, 128))
                for b in live:
                    col[v][b] = col[v][b] - lcol[b] * m
            top = jnp.broadcast_to(left[p][t : t + 1, :], (8, 128)) * pivot
            aug = jnp.broadcast_to(right[p][t : t + 1, :], (8, 128)) * pivot
            for b in live:
                left[b] = left[b] - lcol[b] * top
                right[b] = right[b] - lcol[b] * aug
            left[p] = jnp.where(sub == t, top, left[p])
            right[p] = jnp.where(sub == t, aug, right[p])
    fill = jnp.zeros((8, 128), F32)
    for b in range(blocks):
        row = sub + 8 * b
        upper = jnp.where(jnp.logical_and(row <= lane, lane < known), left[b], 0.0)
        inverse = jnp.where(jnp.logical_and(row >= lane, row < known), right[b], 0.0)
        u_ref[8 * b : 8 * b + 8, :] = upper[:, :cols]
        li_ref[8 * b : 8 * b + 8, :] = inverse[:, :cols]
        high = inverse.astype(BF16).astype(F32)
        wide = jnp.concatenate([high, fill], axis=1)
        rest = jnp.concatenate([inverse - high, fill], axis=1)
        wide = wide + pltpu.roll(rest, cols, 1) + pltpu.roll(wide, 2 * cols, 1)
        w_ref[8 * b : 8 * b + 8, :] = wide[:, : 3 * cols]


def rotate_kernel(w_ref, h_ref, o_ref, out_ref, sem):
    cols = w_ref.shape[0]
    depth = out_ref.shape[1]
    weight = w_ref[...].astype(BF16)

    def copy(q):
        at = pl.ds(pl.multiple_of(q * 8, 8), 8)
        return pltpu.make_async_copy(out_ref.at[:, at, :], o_ref.at[:, at, :], sem.at[q])

    def step(q, carry):
        at = pl.ds(pl.multiple_of(q * 1024, 1024), 1024)
        high = h_ref[0:cols, at]
        low = h_ref[cols : 2 * cols, at]
        res = lax.dot_general(
            weight,
            jnp.concatenate([high, high, low], axis=0),
            (((1,), (0,)), ((), ())),
            preferred_element_type=F32,
        )
        res = jnp.stack([res[:, t * 128 : (t + 1) * 128] for t in range(8)], axis=0)
        out_ref[:, pl.ds(pl.multiple_of(q * 8, 8), 8), :] = jnp.swapaxes(res, 0, 1)
        copy(q).start()
        return carry

    lax.fori_loop(0, depth // 8, step, 0)

    def finish(q, carry):
        copy(q).wait()
        return carry

    lax.fori_loop(0, depth // 8, finish, 0)


def final_kernel(
    p_ref, xu_ref, xd_ref, yu_ref, yd_ref, so_ref, a_ref, f_hbm, c_ref, v_ref, vel_ref, f_ref, sem
):
    nx, ny, nz = p_ref.shape[1:]
    nxc, nyc = nx // 2, ny // 2

    def copy(xc):
        at = pl.ds(2 * xc, 2)
        return pltpu.make_async_copy(f_ref.at[:, at], f_hbm.at[:, at], sem.at[xc])

    def finish(xc, carry):
        copy(xc).wait()
        return carry

    def step(xc, carry):
        total = [None] * 3
        for t in range(2):
            x = 2 * xc + t
            f = streamed(x, nx, p_ref, xu_ref, xd_ref, yu_ref, yd_ref)
            for i in range(NVEL):
                f_ref[i, x] = f[i]
            _, u = moments(f)
            fluid = (so_ref[x] == 0).astype(F32)
            for k in range(3):
                part = u[k] * fluid
                total[k] = part if t == 0 else total[k] + part
        for k in range(3):
            at = pl.multiple_of((k * nxc + xc) * ny, ny)
            for t in range(nz // 128):
                vel_ref[t, pl.ds(at, ny), :] = total[k][:, t * 128 : (t + 1) * 128]
        copy(xc).start()
        return carry

    lax.fori_loop(0, nxc, step, 0)
    depth = 3 * nxc * nyc
    pairs = []
    for t in range(nz // 128):
        half = vel_ref.at[t]
        pairs.append(half[pl.ds(0, depth, stride=2), :] + half[pl.ds(1, depth, stride=2), :])
    pairs = jnp.concatenate(pairs, axis=1)
    pick = (
        lax.broadcasted_iota(jnp.int32, (nz, nz // 2), 0) // 2
        == lax.broadcasted_iota(jnp.int32, (nz, nz // 2), 1)
    ).astype(F32)
    coarse = lax.dot_general(
        pairs, pick, (((1,), (0,)), ((), ())), precision=HIGHEST, preferred_element_type=F32
    )
    c_ref[...] = coarse * (SPEED_SCALE / 8.0)
    cols = a_ref.shape[1]

    def inner(r, acc):
        return acc + a_ref[r] * c_ref[pl.ds(r, 1), :]

    acc = lax.fori_loop(0, depth, inner, jnp.zeros((cols, 128), F32), unroll=8)
    dots = jnp.sum(acc, axis=1, keepdims=True)
    own = jnp.sum(c_ref[...] * c_ref[...])
    down = lax.broadcasted_iota(jnp.int32, (cols, 1), 0)
    dots = jnp.where(down == cols - 1, own, dots)
    across = lax.broadcasted_iota(jnp.int32, (cols, 128), 1)
    diag = jnp.where(across == lax.broadcasted_iota(jnp.int32, (cols, 128), 0), dots, 0.0)
    line = jnp.sum(diag, axis=0, keepdims=True)
    v_ref[...] = jnp.broadcast_to(line, v_ref.shape)
    lax.fori_loop(0, nxc, finish, 0)


def last_kernel(inv_rows, v_ref, li_ref, u_ref, a_ref, c_ref, q_ref, uo_ref, o_ref, row_ref, sem):
    cols = li_ref.shape[0]
    known = cols - 1
    depth = c_ref.shape[0]
    line = jnp.sum(v_ref[...], axis=0, keepdims=True)[:, :cols] * inv_rows
    across = lax.broadcasted_iota(jnp.int32, (1, cols), 1)
    norm = jnp.sum(jnp.where(across == known, line, 0.0), axis=1, keepdims=True)
    inverse = li_ref[...]
    coef = jnp.sum(inverse * jnp.where(across == known, 0.0, line), axis=1, keepdims=True)
    pivot = lax.rsqrt(norm - jnp.sum(coef * coef, axis=0, keepdims=True))
    left = norm - jnp.sum(coef * coef, axis=0, keepdims=True)
    col_id = lax.broadcasted_iota(jnp.int32, (cols, cols), 1)
    row_id = lax.broadcasted_iota(jnp.int32, (cols, cols), 0)
    edge = jnp.where(row_id == known, left * pivot, coef)
    uo_ref[...] = jnp.where(col_id == known, edge, u_ref[...])
    weight = jnp.sum(inverse * coef, axis=0, keepdims=True) * (-pivot)
    diag = jnp.where(row_id == col_id, weight, 0.0)
    tall = jnp.sum(diag, axis=1, keepdims=True)
    tall = jnp.broadcast_to(tall, (cols, 128))

    def step(r, carry):
        part = jnp.sum(a_ref[r] * tall, axis=0, keepdims=True)
        row_ref[pl.ds(r, 1), :] = part + c_ref[pl.ds(r, 1), :] * pivot
        return carry

    lax.fori_loop(0, depth, step, 0, unroll=8)
    copy = pltpu.make_async_copy(row_ref, o_ref.at[known], sem)
    copy.start()
    copy.wait()


def shape(dims, dtype=F32):
    return jax.ShapeDtypeStruct(dims, dtype)


def halo_x(xup, xdn):
    return shifted(xup, "gx", 1), shifted(xdn, "gx", -1)


def halo_y(xu, xd, yup, ydn, gate):
    send_up, send_dn = pl.pallas_call(
        pack_kernel,
        out_shape=(shape(yup.shape), shape(ydn.shape)),
        in_specs=[VMEM] * 4 + [ANY],
        name="pack",
        compiler_params=params(2),
    )(xu, xd, yup, ydn, gate)
    return shifted(send_up, "gy", 1), shifted(send_dn, "gy", -1)


def rounds():
    steps = []
    for axis in ("gx", "gy"):
        bit = 1
        while bit < lax.axis_size(axis):
            steps.append((axis, bit))
            bit *= 2
    return steps


def exchange(value, steps):
    for axis, bit in steps:
        pairs = [(s, s ^ bit) for s in range(lax.axis_size(axis))]
        value = value + lax.ppermute(value, axis, pairs)
    return value


def on_device(populations, relax_rate, solid_mask, singular_values, basis, snapshots):
    _, nx, ny, nz = populations.shape
    rank, extra = basis.shape[0], snapshots.shape[0]
    cols = rank + extra + 1
    tail = basis.shape[1:]
    depth = tail[0] * tail[1] * tail[2]
    n_dev = lax.axis_size("gx") * lax.axis_size("gy")
    inv_rows = 1.0 / (depth * tail[3] * n_dev)
    edges = len(UP_Y) * nx
    post_shapes = (
        shape((NVEL, nx, ny, nz)),
        shape((len(UP_X), ny, nz)),
        shape((len(DOWN_X), ny, nz)),
        shape((edges, nz)),
        shape((edges, nz)),
    )
    post, xup, xdn, yup, ydn, omega, solid = pl.pallas_call(
        first_kernel,
        out_shape=post_shapes + (shape((nx, ny, nz)), shape((nx, ny, nz), jnp.int32)),
        in_specs=[HBM] * 3,
        scratch_shapes=[pltpu.VMEM((NVEL, nx, ny, nz), F32), pltpu.SemaphoreType.DMA((6,))],
        name="first",
        compiler_params=params(6),
    )(populations, relax_rate, solid_mask)
    xu, xd = halo_x(xup, xdn)
    rows, halves, gram = pl.pallas_call(
        gram_kernel,
        out_shape=(
            pltpu.VMEM((depth, cols, 128), F32),
            pltpu.VMEM((2 * cols, depth * 128), BF16),
            shape((cols, cols)),
        ),
        in_specs=[VMEM] * 3 + [ANY],
        name="gram",
        compiler_params=params(4),
    )(
        singular_values.reshape(1, rank),
        basis.reshape(rank, depth, 128),
        snapshots.reshape(extra, depth, 128),
        omega,
    )
    yu, yd = halo_y(xu, xd, yup, ydn, gram)
    steps = rounds()
    gram = exchange(gram, steps[:2])
    post, xup, xdn, yup, ydn = pl.pallas_call(
        second_kernel,
        out_shape=post_shapes,
        in_specs=[VMEM] * 7 + [ANY],
        name="second",
        compiler_params=params(4),
    )(post, xu, xd, yu, yd, omega, solid, gram)
    xu, xd = halo_x(xup, xdn)
    gram = exchange(gram, steps[2:4])
    yu, yd = halo_y(xu, xd, yup, ydn, gram)
    gram = exchange(gram, steps[4:])
    field, coarse, line = pl.pallas_call(
        final_kernel,
        out_shape=(shape((NVEL, nx, ny, nz)), shape((depth, 128)), shape((n_dev, 128))),
        in_specs=[VMEM] * 7,
        out_specs=(ANY, VMEM, VMEM),
        scratch_shapes=[
            pltpu.VMEM((nz // 128, 3 * (nx // 2) * ny, 128), F32),
            pltpu.VMEM((NVEL, nx, ny, nz), F32),
            pltpu.SemaphoreType.DMA((nx // 2,)),
        ],
        name="final",
        compiler_params=params(6),
    )(post, xu, xd, yu, yd, solid, rows)
    lines = lax.all_to_all(line, ("gx", "gy"), 0, 0, tiled=True)
    upper, inverse, split = pl.pallas_call(
        lambda *refs: factor_kernel(inv_rows, *refs),
        out_shape=(shape((cols, cols)), shape((cols, cols)), shape((cols, 3 * cols))),
        name="factor",
        compiler_params=params(4),
    )(gram)
    rotated = pl.pallas_call(
        rotate_kernel,
        out_shape=shape((cols, depth, 128)),
        in_specs=[VMEM] * 2,
        out_specs=ANY,
        scratch_shapes=[
            pltpu.VMEM((cols, depth, 128), F32),
            pltpu.SemaphoreType.DMA((depth // 8,)),
        ],
        name="rotate",
        compiler_params=params(8),
    )(split, halves)
    upper, rotated = pl.pallas_call(
        lambda *refs: last_kernel(inv_rows, *refs),
        out_shape=(shape((cols, cols)), shape((cols, depth, 128))),
        in_specs=[VMEM] * 5 + [ANY],
        out_specs=(VMEM, ANY),
        scratch_shapes=[pltpu.VMEM((depth, 128), F32), pltpu.SemaphoreType.DMA],
        input_output_aliases={5: 1},
        name="last",
        compiler_params=params(4),
    )(lines, inverse, upper, rows, coarse, rotated)
    return field, upper, rotated.reshape((cols,) + tail)


def solution(mesh):
    return jax.shard_map(
        on_device,
        mesh=mesh,
        in_specs=(
            P(None, "gx", "gy", None),
            P("gx", "gy", None),
            P("gx", "gy", None),
            P(),
            P(None, None, "gx", "gy", None),
            P(None, None, "gx", "gy", None),
        ),
        out_specs=(P(None, "gx", "gy", None), P(), P(None, None, "gx", "gy", None)),
        check_vma=False,
    )
```

```python
import jax
import jax.numpy as jnp
from jax import lax
from jax.experimental import pallas as pl
from jax.experimental.pallas import tpu as pltpu
from jax.sharding import PartitionSpec as P

velocity_table = [
    (0, 0, 0),
    (1, 0, 0),
    (-1, 0, 0),
    (0, 1, 0),
    (0, -1, 0),
    (0, 0, 1),
    (0, 0, -1),
    (1, 1, 0),
    (-1, -1, 0),
    (1, -1, 0),
    (-1, 1, 0),
    (1, 0, 1),
    (-1, 0, -1),
    (1, 0, -1),
    (-1, 0, 1),
    (0, 1, 1),
    (0, -1, -1),
    (0, 1, -1),
    (0, -1, 1),
]
NVEL = 19
PAIRS = [(i, i + 1) for i in range(1, NVEL, 2)]
W_REST, W_FACE, W_EDGE = 1.0 / 3.0, 1.0 / 18.0, 1.0 / 36.0
UP_X = [i for i in range(NVEL) if velocity_table[i][0] == 1]
DOWN_X = [i for i in range(NVEL) if velocity_table[i][0] == -1]
UP_Y = [i for i in range(NVEL) if velocity_table[i][1] == 1]
DOWN_Y = [i for i in range(NVEL) if velocity_table[i][1] == -1]
SPEED_SCALE = 10.0
HIGHEST = lax.Precision.HIGHEST
F32 = jnp.float32
BF16 = jnp.bfloat16
VMEM = pl.BlockSpec(memory_space=pltpu.VMEM)
ANY = pl.BlockSpec(memory_space=pl.ANY)
HBM = pl.BlockSpec(memory_space=pltpu.HBM)


def params(mib=40):
    return pltpu.CompilerParams(vmem_limit_bytes=mib << 20)


def ring_pairs(axis):
    count = lax.axis_size(axis)
    partner = [(s, s ^ 1) for s in range(count)]
    other = [(s, (s + 1 if s % 2 else s - 1) % count) for s in range(count)]
    return partner, other


def swap(values, axis):
    partner, other = ring_pairs(axis)
    return lax.ppermute(values[0], axis, partner), lax.ppermute(values[1], axis, other)


def by_parity(axis, place):
    odd = lax.rem(lax.axis_index(axis), 2)

    @pl.when(odd == 0)
    def _():
        place(0)

    @pl.when(odd == 1)
    def _():
        place(1)


def moments(f):
    plus = [f[a] + f[b] for a, b in PAIRS]
    minus = [f[a] - f[b] for a, b in PAIRS]
    rho = f[0] + plus[0]
    for p in plus[1:]:
        rho = rho + p
    mx, my, mz, m7, m9, m11, m13, m15, m17 = minus
    jx = (mx + m7) + (m9 + m11) + m13
    jy = (my + m7) + (m15 + m17) - m9
    jz = (mz + m11) + (m15 - m13) - m17
    r = 1.0 / rho
    return rho, (jx * r, jy * r, jz * r)


def collide(f, omega, solid):
    rho, u = moments(f)
    base = 1.0 - 1.5 * (u[0] * u[0] + u[1] * u[1] + u[2] * u[2])
    keep = 1.0 - omega
    wr = omega * rho
    post = [None] * NVEL
    post[0] = jnp.where(solid, f[0], keep * f[0] + (W_REST * wr) * base)
    w_face, w_edge = W_FACE * wr, W_EDGE * wr
    for a, b in PAIRS:
        vel = velocity_table[a]
        along = None
        for axis in range(3):
            if vel[axis] == 1:
                along = u[axis] if along is None else along + u[axis]
            elif vel[axis] == -1:
                along = along - u[axis]
        w = w_face if a < 7 else w_edge
        even = w * (base + 4.5 * (along * along))
        odd = w * (3.0 * along)
        post[a] = jnp.where(solid, f[b], keep * f[a] + (even + odd))
        post[b] = jnp.where(solid, f[a], keep * f[b] + (even - odd))
    return post


def emit_post(post, x, nx, post_ref, yup_ref, ydn_ref):
    ny = post_ref.shape[2]
    for i in range(NVEL):
        cz = velocity_table[i][2]
        value = post[i] if cz == 0 else pltpu.roll(post[i], cz % post[i].shape[1], 1)
        post_ref[i, x] = value
        cx = velocity_table[i][0]
        row = lax.rem(x + (cx + nx), nx)
        if i in UP_Y:
            yup_ref[pl.ds(UP_Y.index(i) * nx + row, 1), :] = value[ny - 1 : ny, :]
        if i in DOWN_Y:
            ydn_ref[pl.ds(DOWN_Y.index(i) * nx + row, 1), :] = value[0:1, :]


def emit_faces(nx, post_ref, faces):
    def place(odd):
        for k, i in enumerate(UP_X):
            faces[odd][k] = post_ref[i, nx - 1]
        for k, i in enumerate(DOWN_X):
            faces[1 - odd][k] = post_ref[i, 0]

    by_parity("gx", place)


def sort_halos(xa_ref, xb_ref, ya_ref, yb_ref, xup_ref, xdn_ref, yup_ref, ydn_ref):
    def place_x(odd):
        xup_ref[...] = (xb_ref, xa_ref)[odd][...]
        xdn_ref[...] = (xa_ref, xb_ref)[odd][...]

    def place_y(odd):
        yup_ref[...] = (yb_ref, ya_ref)[odd][...]
        ydn_ref[...] = (ya_ref, yb_ref)[odd][...]

    by_parity("gx", place_x)
    by_parity("gy", place_y)


def first_kernel(
    f_hbm, om_hbm, so_hbm, post_ref, xa_ref, xb_ref, yup_ref, ydn_ref, om_ref, so_ref, f_ref, sem
):
    nx = f_ref.shape[1]
    parts = sem.shape[0] - 2
    rows = nx // parts

    def load(k):
        at = pl.ds(k * rows, rows)
        return pltpu.make_async_copy(f_hbm.at[:, at], f_ref.at[:, at], sem.at[k])

    loads = [load(k) for k in range(parts)]
    omega = pltpu.make_async_copy(om_hbm, om_ref, sem.at[parts])
    solid = pltpu.make_async_copy(so_hbm, so_ref, sem.at[parts + 1])
    loads[0].start()
    omega.start()
    solid.start()
    for k in range(1, parts):
        loads[k].start()

    def step(x, carry):
        post = collide([f_ref[i, x] for i in range(NVEL)], om_ref[x], so_ref[x] > 0)
        emit_post(post, x, nx, post_ref, yup_ref, ydn_ref)
        return carry

    for k in range(parts):
        loads[k].wait()
        if k == 0:
            omega.wait()
            solid.wait()
        lax.fori_loop(k * rows, (k + 1) * rows, step, 0)
    emit_faces(nx, post_ref, (xa_ref, xb_ref))


def streamed(x, nx, post_ref, xup_ref, xdn_ref, yup_ref, ydn_ref):
    ny = post_ref.shape[2]
    row_id = lax.broadcasted_iota(jnp.int32, (ny, post_ref.shape[3]), 0)
    f = []
    for i in range(NVEL):
        cx, cy, _ = velocity_table[i]
        if cx == 1:
            value = jnp.where(x == 0, xup_ref[UP_X.index(i)], post_ref[i, lax.rem(x + nx - 1, nx)])
        elif cx == -1:
            value = jnp.where(
                x == nx - 1, xdn_ref[DOWN_X.index(i)], post_ref[i, lax.rem(x + 1, nx)]
            )
        else:
            value = post_ref[i, x]
        if cy == 1:
            edge = yup_ref[pl.ds(UP_Y.index(i) * nx + x, 1), :]
            value = jnp.where(row_id == 0, edge, pltpu.roll(value, 1, 0))
        elif cy == -1:
            edge = ydn_ref[pl.ds(DOWN_Y.index(i) * nx + x, 1), :]
            value = jnp.where(row_id == ny - 1, edge, pltpu.roll(value, ny - 1, 0))
        f.append(value)
    return f


def second_kernel(
    p_ref,
    ra_ref,
    rb_ref,
    sa_ref,
    sb_ref,
    om_ref,
    so_ref,
    gate_ref,
    post_ref,
    xa_ref,
    xb_ref,
    yup_ref,
    ydn_ref,
    *halos,
):
    nx = p_ref.shape[1]
    sort_halos(ra_ref, rb_ref, sa_ref, sb_ref, *halos)

    def step(x, carry):
        f = streamed(x, nx, p_ref, *halos)
        post = collide(f, om_ref[x], so_ref[x] > 0)
        emit_post(post, x, nx, post_ref, yup_ref, ydn_ref)
        return carry

    lax.fori_loop(0, nx, step, 0)
    emit_faces(nx, post_ref, (xa_ref, xb_ref))


def pack_kernel(xa_ref, xb_ref, yup_ref, ydn_ref, gate_ref, oa_ref, ob_ref):
    nx = yup_ref.shape[0] // len(UP_Y)
    ny = xa_ref.shape[1]

    def corners(ids, out, row, odd):
        xu_ref, xd_ref = ((xb_ref, xa_ref), (xa_ref, xb_ref))[odd]
        for k, i in enumerate(ids):
            if velocity_table[i][0] == 1:
                out[k * nx : k * nx + 1, :] = xu_ref[UP_X.index(i), row : row + 1, :]
            elif velocity_table[i][0] == -1:
                at = k * nx + nx - 1
                out[at : at + 1, :] = xd_ref[DOWN_X.index(i), row : row + 1, :]

    def place(odd):
        up, down = (oa_ref, ob_ref)[odd], (ob_ref, oa_ref)[odd]
        up[...] = yup_ref[...]
        down[...] = ydn_ref[...]
        by_parity("gx", lambda x_odd: corners(UP_Y, up, ny - 1, x_odd))
        by_parity("gx", lambda x_odd: corners(DOWN_Y, down, 0, x_odd))

    by_parity("gy", place)


def gram_kernel(
    s_ref, basis_hbm, snap_hbm, gate_ref, a_ref, h_hbm, g_ref, basis_ref, snap_ref, h_ref, ins, outs
):
    rank = basis_ref.shape[0]
    depth = basis_ref.shape[1]
    extra = snap_ref.shape[0]
    cols = a_ref.shape[1]
    same = lax.broadcasted_iota(jnp.int32, (rank, rank), 0) == lax.broadcasted_iota(
        jnp.int32, (rank, rank), 1
    )
    scale = jnp.sum(jnp.where(same, s_ref[...], 0.0), axis=1, keepdims=True)
    scale = jnp.broadcast_to(scale, (rank, 128))
    zero = jnp.zeros((cols - rank - extra, 8, 128), F32)

    def load(q):
        at = pl.ds(pl.multiple_of(q * 8, 8), 8)
        return (
            pltpu.make_async_copy(basis_hbm.at[:, at], basis_ref.at[:, at], ins.at[0, q]),
            pltpu.make_async_copy(snap_hbm.at[:, at], snap_ref.at[:, at], ins.at[1, q]),
        )

    def save(q):
        at = pl.ds(pl.multiple_of(q * 1024, 1024), 1024)
        return pltpu.make_async_copy(h_ref.at[:, at], h_hbm.at[:, at], outs.at[q])

    def begin(q, carry):
        for copy in load(q):
            copy.start()
        return carry

    def finish(q, carry):
        save(q).wait()
        return carry

    lax.fori_loop(0, depth // 8, begin, 0)

    def step(q, carry):
        for copy in load(q):
            copy.wait()
        r = pl.multiple_of(q * 8, 8)
        top = jnp.swapaxes(basis_ref[:, pl.ds(r, 8), :], 0, 1)
        low = jnp.concatenate([snap_ref[:, pl.ds(r, 8), :], zero], axis=0)
        low = jnp.swapaxes(low, 0, 1)
        for t in range(8):
            rows = jnp.concatenate([top[t] * scale, low[t]], axis=0)
            a_ref[r + t] = rows
            at = pl.ds(pl.multiple_of((r + t) * 128, 128), 128)
            high = rows.astype(BF16)
            h_ref[0:cols, at] = high
            h_ref[cols : 2 * cols, at] = (rows - high.astype(F32)).astype(BF16)
        save(q).start()
        return carry

    lax.fori_loop(0, depth // 8, step, 0)
    acc = lax.dot_general(
        h_ref[...], h_ref[0:cols, :], (((1,), (1,)), ((), ())), preferred_element_type=F32
    )
    cross = acc[cols:, :]
    eye = (
        lax.broadcasted_iota(jnp.int32, (cols, cols), 0)
        == lax.broadcasted_iota(jnp.int32, (cols, cols), 1)
    ).astype(F32)
    flipped = lax.dot_general(
        eye, cross, (((1,), (1,)), ((), ())), precision=HIGHEST, preferred_element_type=F32
    )
    g_ref[...] = acc[:cols, :] + cross + flipped
    lax.fori_loop(0, depth // 8, finish, 0)


def factor_kernel(inv_rows, g_ref, u_ref, li_ref, w_ref):
    cols = g_ref.shape[0]
    known = cols - 1
    blocks = cols // 8
    pad = jnp.zeros((8, 128 - cols), F32)
    sub = lax.broadcasted_iota(jnp.int32, (8, 128), 0)
    lane = lax.broadcasted_iota(jnp.int32, (8, 128), 1)
    left = [
        jnp.concatenate([g_ref[8 * b : 8 * b + 8, :] * inv_rows, pad], axis=1) for b in range(blocks)
    ]
    right = [(sub + 8 * b == lane).astype(F32) for b in range(blocks)]
    for p in range(blocks):
        live = range(p, blocks)
        width = min(8, known - 8 * p)
        col = [
            {
                b: jnp.broadcast_to(left[b][:, 8 * p + t : 8 * p + t + 1], (8, 128))
                for b in live
            }
            for t in range(width)
        ]
        for t in range(width):
            pivot = lax.rsqrt(jnp.broadcast_to(col[t][p][t : t + 1, :], (8, 128)))
            lcol = {b: col[t][b] * pivot for b in live}
            lcol[p] = jnp.where(sub > t, lcol[p], 0.0)
            for v in range(t + 1, width):
                m = jnp.broadcast_to(lcol[p][v : v + 1, :], (8, 128))
                for b in live:
                    col[v][b] = col[v][b] - lcol[b] * m
            top = jnp.broadcast_to(left[p][t : t + 1, :], (8, 128)) * pivot
            aug = jnp.broadcast_to(right[p][t : t + 1, :], (8, 128)) * pivot
            for b in live:
                left[b] = left[b] - lcol[b] * top
                right[b] = right[b] - lcol[b] * aug
            left[p] = jnp.where(sub == t, top, left[p])
            right[p] = jnp.where(sub == t, aug, right[p])
    fill = jnp.zeros((8, 128), F32)
    for b in range(blocks):
        row = sub + 8 * b
        upper = jnp.where(jnp.logical_and(row <= lane, lane < known), left[b], 0.0)
        inverse = jnp.where(jnp.logical_and(row >= lane, row < known), right[b], 0.0)
        u_ref[8 * b : 8 * b + 8, :] = upper[:, :cols]
        li_ref[8 * b : 8 * b + 8, :] = inverse[:, :cols]
        high = inverse.astype(BF16).astype(F32)
        wide = jnp.concatenate([high, fill], axis=1)
        rest = jnp.concatenate([inverse - high, fill], axis=1)
        wide = wide + pltpu.roll(rest, cols, 1) + pltpu.roll(wide, 2 * cols, 1)
        w_ref[8 * b : 8 * b + 8, :] = wide[:, : 3 * cols]


def rotate_kernel(w_ref, h_hbm, o_ref, h_ref, out_ref, ins, sem):
    cols = w_ref.shape[0]
    depth = out_ref.shape[1]
    weight = w_ref[...].astype(BF16)

    def copy(q):
        at = pl.ds(pl.multiple_of(q * 8, 8), 8)
        return pltpu.make_async_copy(out_ref.at[:, at, :], o_ref.at[:, at, :], sem.at[q])

    def load(q):
        at = pl.ds(pl.multiple_of(q * 1024, 1024), 1024)
        return pltpu.make_async_copy(h_hbm.at[:, at], h_ref.at[:, at], ins.at[q])

    def begin(q, carry):
        load(q).start()
        return carry

    lax.fori_loop(0, depth // 8, begin, 0)

    def step(q, carry):
        load(q).wait()
        at = pl.ds(pl.multiple_of(q * 1024, 1024), 1024)
        high = h_ref[0:cols, at]
        low = h_ref[cols : 2 * cols, at]
        res = lax.dot_general(
            weight,
            jnp.concatenate([high, high, low], axis=0),
            (((1,), (0,)), ((), ())),
            preferred_element_type=F32,
        )
        res = jnp.stack([res[:, t * 128 : (t + 1) * 128] for t in range(8)], axis=0)
        out_ref[:, pl.ds(pl.multiple_of(q * 8, 8), 8), :] = jnp.swapaxes(res, 0, 1)
        copy(q).start()
        return carry

    lax.fori_loop(0, depth // 8, step, 0)

    def finish(q, carry):
        copy(q).wait()
        return carry

    lax.fori_loop(0, depth // 8, finish, 0)


def final_kernel(
    p_ref, ra_ref, rb_ref, sa_ref, sb_ref, so_ref, a_ref, gate_ref, f_hbm, c_ref, v_ref, vel_ref, f_ref, sem, *halos
):
    nx, ny, nz = p_ref.shape[1:]
    nxc, nyc = nx // 2, ny // 2
    sort_halos(ra_ref, rb_ref, sa_ref, sb_ref, *halos)

    def copy(xc):
        at = pl.ds(2 * xc, 2)
        return pltpu.make_async_copy(f_ref.at[:, at], f_hbm.at[:, at], sem.at[xc])

    def finish(xc, carry):
        copy(xc).wait()
        return carry

    def step(xc, carry):
        total = [None] * 3
        for t in range(2):
            x = 2 * xc + t
            f = streamed(x, nx, p_ref, *halos)
            for i in range(NVEL):
                f_ref[i, x] = f[i]
            _, u = moments(f)
            fluid = (so_ref[x] == 0).astype(F32)
            for k in range(3):
                part = u[k] * fluid
                total[k] = part if t == 0 else total[k] + part
        for k in range(3):
            at = pl.multiple_of((k * nxc + xc) * ny, ny)
            for t in range(nz // 128):
                vel_ref[t, pl.ds(at, ny), :] = total[k][:, t * 128 : (t + 1) * 128]
        copy(xc).start()
        return carry

    lax.fori_loop(0, nxc, step, 0)
    depth = 3 * nxc * nyc
    pairs = []
    for t in range(nz // 128):
        half = vel_ref.at[t]
        pairs.append(half[pl.ds(0, depth, stride=2), :] + half[pl.ds(1, depth, stride=2), :])
    pairs = jnp.concatenate(pairs, axis=1)
    pick = (
        lax.broadcasted_iota(jnp.int32, (nz, nz // 2), 0) // 2
        == lax.broadcasted_iota(jnp.int32, (nz, nz // 2), 1)
    ).astype(F32)
    coarse = lax.dot_general(
        pairs, pick, (((1,), (0,)), ((), ())), precision=HIGHEST, preferred_element_type=F32
    )
    c_ref[...] = coarse * (SPEED_SCALE / 8.0)
    cols = a_ref.shape[1]

    def inner(r, acc):
        return acc + a_ref[r] * c_ref[pl.ds(r, 1), :]

    acc = lax.fori_loop(0, depth, inner, jnp.zeros((cols, 128), F32), unroll=8)
    dots = jnp.sum(acc, axis=1, keepdims=True)
    own = jnp.sum(c_ref[...] * c_ref[...])
    down = lax.broadcasted_iota(jnp.int32, (cols, 1), 0)
    dots = jnp.where(down == cols - 1, own, dots)
    across = lax.broadcasted_iota(jnp.int32, (cols, 128), 1)
    diag = jnp.where(across == lax.broadcasted_iota(jnp.int32, (cols, 128), 0), dots, 0.0)
    line = jnp.sum(diag, axis=0, keepdims=True)
    v_ref[...] = jnp.broadcast_to(line, v_ref.shape)
    lax.fori_loop(0, nxc, finish, 0)


def last_kernel(
    inv_rows,
    v_ref,
    li_ref,
    u_ref,
    s_ref,
    c_ref,
    basis_hbm,
    snap_hbm,
    q_ref,
    uo_ref,
    o_ref,
    basis_ref,
    snap_ref,
    tall_ref,
    row_ref,
    ins,
    sem,
):
    cols = li_ref.shape[0]
    known = cols - 1
    rank, depth = basis_ref.shape[:2]
    extra = snap_ref.shape[0]
    parts = ins.shape[1]
    size = depth // parts
    loads = []
    for k in range(parts):
        at = pl.ds(k * size, size)
        loads.append(
            (
                pltpu.make_async_copy(basis_hbm.at[:, at], basis_ref.at[:, at], ins.at[0, k]),
                pltpu.make_async_copy(snap_hbm.at[:, at], snap_ref.at[:, at], ins.at[1, k]),
            )
        )
        for copy in loads[-1]:
            copy.start()
    line = jnp.sum(v_ref[...], axis=0, keepdims=True)[:, :cols] * inv_rows
    across = lax.broadcasted_iota(jnp.int32, (1, cols), 1)
    norm = jnp.sum(jnp.where(across == known, line, 0.0), axis=1, keepdims=True)
    inverse = li_ref[...]
    coef = jnp.sum(inverse * jnp.where(across == known, 0.0, line), axis=1, keepdims=True)
    left = norm - jnp.sum(coef * coef, axis=0, keepdims=True)
    pivot = lax.rsqrt(left)
    col_id = lax.broadcasted_iota(jnp.int32, (cols, cols), 1)
    row_id = lax.broadcasted_iota(jnp.int32, (cols, cols), 0)
    edge = jnp.where(row_id == known, left * pivot, coef)
    uo_ref[...] = jnp.where(col_id == known, edge, u_ref[...])
    weight = jnp.sum(inverse * coef, axis=0, keepdims=True) * (-pivot)
    scale = jnp.concatenate([s_ref[...], jnp.ones((1, cols - rank), F32)], axis=1)
    diag = jnp.where(row_id == col_id, weight * scale, 0.0)
    tall_ref[...] = jnp.broadcast_to(jnp.sum(diag, axis=1, keepdims=True), (cols, 128))

    def step(q, carry):
        at = pl.ds(pl.multiple_of(q * 16, 16), 16)
        total = [c_ref[at, :] * pivot] + [None] * 3
        for k in range(rank + extra):
            value = basis_ref[k, at, :] if k < rank else snap_ref[k - rank, at, :]
            value = value * tall_ref[k : k + 1, :]
            total[k % 4] = value if total[k % 4] is None else total[k % 4] + value
        row_ref[at, :] = (total[0] + total[1]) + (total[2] + total[3])
        return carry

    for k in range(parts):
        for copy in loads[k]:
            copy.wait()
        lax.fori_loop(k * size // 16, (k + 1) * size // 16, step, 0)
    copy = pltpu.make_async_copy(row_ref, o_ref.at[known], sem)
    copy.start()
    copy.wait()


def in_hbm(value):
    return pltpu.with_memory_space_constraint(value, pltpu.HBM)


def shape(dims, dtype=F32):
    return jax.ShapeDtypeStruct(dims, dtype)


def halo_y(xa, xb, yup, ydn, gate):
    sends = pl.pallas_call(
        pack_kernel,
        out_shape=(shape(yup.shape), shape(ydn.shape)),
        in_specs=[VMEM] * 4 + [ANY],
        name="pack",
        compiler_params=params(2),
    )(xa, xb, yup, ydn, gate)
    return swap(sends, "gy")


def rounds():
    steps = []
    for axis in ("gx", "gy"):
        bit = 1
        while bit < lax.axis_size(axis):
            steps.append((axis, bit))
            bit *= 2
    return steps


def exchange(value, steps):
    for axis, bit in steps:
        pairs = [(s, s ^ bit) for s in range(lax.axis_size(axis))]
        value = value + lax.ppermute(value, axis, pairs)
    return value


def on_device(populations, relax_rate, solid_mask, singular_values, basis, snapshots):
    _, nx, ny, nz = populations.shape
    rank, extra = basis.shape[0], snapshots.shape[0]
    cols = rank + extra + 1
    tail = basis.shape[1:]
    depth = tail[0] * tail[1] * tail[2]
    n_dev = lax.axis_size("gx") * lax.axis_size("gy")
    inv_rows = 1.0 / (depth * tail[3] * n_dev)
    edges = len(UP_Y) * nx
    post_shapes = (
        shape((NVEL, nx, ny, nz)),
        shape((len(UP_X), ny, nz)),
        shape((len(DOWN_X), ny, nz)),
        shape((edges, nz)),
        shape((edges, nz)),
    )
    halos = [pltpu.VMEM(post_shapes[k].shape, F32) for k in range(1, 5)]
    post, xa, xb, yup, ydn, omega, solid = pl.pallas_call(
        first_kernel,
        out_shape=post_shapes + (shape((nx, ny, nz)), shape((nx, ny, nz), jnp.int32)),
        in_specs=[HBM] * 3,
        scratch_shapes=[pltpu.VMEM((NVEL, nx, ny, nz), F32), pltpu.SemaphoreType.DMA((6,))],
        name="first",
        compiler_params=params(6),
    )(*[in_hbm(value) for value in (populations, relax_rate, solid_mask)])
    xa, xb = swap((xa, xb), "gx")
    weights = singular_values.reshape(1, rank)
    modes = in_hbm(basis.reshape(rank, depth, 128))
    earlier = in_hbm(snapshots.reshape(extra, depth, 128))
    blocks = depth // 8
    rows, halves, gram = pl.pallas_call(
        gram_kernel,
        out_shape=(
            shape((depth, cols, 128)),
            pltpu.HBM((2 * cols, depth * 128), BF16),
            shape((cols, cols)),
        ),
        in_specs=[VMEM, HBM, HBM, ANY],
        out_specs=(VMEM, HBM, VMEM),
        scratch_shapes=[
            pltpu.VMEM((rank, depth, 128), F32),
            pltpu.VMEM((extra, depth, 128), F32),
            pltpu.VMEM((2 * cols, depth * 128), BF16),
            pltpu.SemaphoreType.DMA((2, blocks)),
            pltpu.SemaphoreType.DMA((blocks,)),
        ],
        name="gram",
        compiler_params=params(12),
    )(weights, modes, earlier, omega)
    ya, yb = halo_y(xa, xb, yup, ydn, gram)
    steps = rounds()
    gram = exchange(gram, steps[:2])
    post, xa, xb, yup, ydn = pl.pallas_call(
        second_kernel,
        out_shape=post_shapes,
        in_specs=[VMEM] * 7 + [ANY],
        scratch_shapes=halos,
        name="second",
        compiler_params=params(4),
    )(post, xa, xb, ya, yb, omega, solid, gram)
    xa, xb = swap((xa, xb), "gx")
    gram = exchange(gram, steps[2:-1])
    ya, yb = halo_y(xa, xb, yup, ydn, gram)
    gram = exchange(gram, steps[-1:])
    upper, inverse, split = pl.pallas_call(
        lambda *refs: factor_kernel(inv_rows, *refs),
        out_shape=(shape((cols, cols)), shape((cols, cols)), shape((cols, 3 * cols))),
        name="factor",
        compiler_params=params(4),
    )(gram)
    field, coarse, line = pl.pallas_call(
        final_kernel,
        out_shape=(shape((NVEL, nx, ny, nz)), shape((depth, 128)), shape((n_dev, 128))),
        in_specs=[VMEM] * 7 + [ANY],
        out_specs=(ANY, VMEM, VMEM),
        scratch_shapes=[
            pltpu.VMEM((nz // 128, 3 * (nx // 2) * ny, 128), F32),
            pltpu.VMEM((NVEL, nx, ny, nz), F32),
            pltpu.SemaphoreType.DMA((nx // 2,)),
        ]
        + halos,
        name="final",
        compiler_params=params(6),
    )(post, xa, xb, ya, yb, solid, rows, inverse)
    lines = lax.all_to_all(line, ("gx", "gy"), 0, 0, tiled=True)
    rotated = pl.pallas_call(
        rotate_kernel,
        out_shape=shape((cols, depth, 128)),
        in_specs=[VMEM, HBM],
        out_specs=ANY,
        scratch_shapes=[
            pltpu.VMEM((2 * cols, depth * 128), BF16),
            pltpu.VMEM((cols, depth, 128), F32),
            pltpu.SemaphoreType.DMA((blocks,)),
            pltpu.SemaphoreType.DMA((blocks,)),
        ],
        name="rotate",
        compiler_params=params(12),
    )(split, in_hbm(halves))
    upper, rotated = pl.pallas_call(
        lambda *refs: last_kernel(inv_rows, *refs),
        out_shape=(shape((cols, cols)), shape((cols, depth, 128))),
        in_specs=[VMEM] * 5 + [HBM] * 2 + [ANY],
        out_specs=(VMEM, ANY),
        scratch_shapes=[
            pltpu.VMEM((rank, depth, 128), F32),
            pltpu.VMEM((extra, depth, 128), F32),
            pltpu.VMEM((cols, 128), F32),
            pltpu.VMEM((depth, 128), F32),
            pltpu.SemaphoreType.DMA((2, 3)),
            pltpu.SemaphoreType.DMA,
        ],
        input_output_aliases={7: 1},
        name="last",
        compiler_params=params(8),
    )(lines, inverse, upper, weights, coarse, modes, earlier, rotated)
    return field, upper, rotated.reshape((cols,) + tail)


def solution(mesh):
    return jax.shard_map(
        on_device,
        mesh=mesh,
        in_specs=(
            P(None, "gx", "gy", None),
            P("gx", "gy", None),
            P("gx", "gy", None),
            P(),
            P(None, None, "gx", "gy", None),
            P(None, None, "gx", "gy", None),
        ),
        out_specs=(P(None, "gx", "gy", None), P(), P(None, None, "gx", "gy", None)),
        check_vma=False,
    )
```

```python
import jax
import jax.numpy as jnp
from jax import lax
from jax.experimental import pallas as pl
from jax.experimental.pallas import tpu as pltpu
from jax.sharding import PartitionSpec as P

velocity_table = [
    (0, 0, 0),
    (1, 0, 0),
    (-1, 0, 0),
    (0, 1, 0),
    (0, -1, 0),
    (0, 0, 1),
    (0, 0, -1),
    (1, 1, 0),
    (-1, -1, 0),
    (1, -1, 0),
    (-1, 1, 0),
    (1, 0, 1),
    (-1, 0, -1),
    (1, 0, -1),
    (-1, 0, 1),
    (0, 1, 1),
    (0, -1, -1),
    (0, 1, -1),
    (0, -1, 1),
]
NVEL = 19
PAIRS = [(i, i + 1) for i in range(1, NVEL, 2)]
W_REST, W_FACE, W_EDGE = 1.0 / 3.0, 1.0 / 18.0, 1.0 / 36.0
UP_X = [i for i in range(NVEL) if velocity_table[i][0] == 1]
DOWN_X = [i for i in range(NVEL) if velocity_table[i][0] == -1]
UP_Y = [i for i in range(NVEL) if velocity_table[i][1] == 1]
DOWN_Y = [i for i in range(NVEL) if velocity_table[i][1] == -1]
SPEED_SCALE = 10.0
UNROLL = 4
UNROLL_F = 1
HIGHEST = lax.Precision.HIGHEST
F32 = jnp.float32
BF16 = jnp.bfloat16
VMEM = pl.BlockSpec(memory_space=pltpu.VMEM)
ANY = pl.BlockSpec(memory_space=pl.ANY)
HBM = pl.BlockSpec(memory_space=pltpu.HBM)


def params(mib=40):
    return pltpu.CompilerParams(vmem_limit_bytes=mib << 20)


def ring_pairs(axis):
    count = lax.axis_size(axis)
    partner = [(s, s ^ 1) for s in range(count)]
    other = [(s, (s + 1 if s % 2 else s - 1) % count) for s in range(count)]
    return partner, other


def swap(values, axis):
    partner, other = ring_pairs(axis)
    return lax.ppermute(values[0], axis, partner), lax.ppermute(values[1], axis, other)


def by_parity(axis, place):
    odd = lax.rem(lax.axis_index(axis), 2)

    @pl.when(odd == 0)
    def _():
        place(0)

    @pl.when(odd == 1)
    def _():
        place(1)


def moments(f):
    plus = [f[a] + f[b] for a, b in PAIRS]
    minus = [f[a] - f[b] for a, b in PAIRS]
    rho = f[0] + plus[0]
    for p in plus[1:]:
        rho = rho + p
    mx, my, mz, m7, m9, m11, m13, m15, m17 = minus
    jx = (mx + m7) + (m9 + m11) + m13
    jy = (my + m7) + (m15 + m17) - m9
    jz = (mz + m11) + (m15 - m13) - m17
    r = 1.0 / rho
    return rho, (jx * r, jy * r, jz * r)


def collide(f, omega, solid):
    rho, u = moments(f)
    base = 1.0 - 1.5 * (u[0] * u[0] + u[1] * u[1] + u[2] * u[2])
    keep = 1.0 - omega
    wr = omega * rho
    post = [None] * NVEL
    post[0] = jnp.where(solid, f[0], keep * f[0] + (W_REST * wr) * base)
    w_face, w_edge = W_FACE * wr, W_EDGE * wr
    for a, b in PAIRS:
        vel = velocity_table[a]
        along = None
        for axis in range(3):
            if vel[axis] == 1:
                along = u[axis] if along is None else along + u[axis]
            elif vel[axis] == -1:
                along = along - u[axis]
        w = w_face if a < 7 else w_edge
        even = w * (base + 4.5 * (along * along))
        odd = w * (3.0 * along)
        post[a] = jnp.where(solid, f[b], keep * f[a] + (even + odd))
        post[b] = jnp.where(solid, f[a], keep * f[b] + (even - odd))
    return post


def emit_post(post, x, nx, post_ref, yup_ref, ydn_ref):
    ny = post_ref.shape[2]
    for i in range(NVEL):
        cz = velocity_table[i][2]
        value = post[i] if cz == 0 else pltpu.roll(post[i], cz % post[i].shape[1], 1)
        post_ref[i, x] = value
        cx = velocity_table[i][0]
        row = lax.rem(x + (cx + nx), nx)
        if i in UP_Y:
            yup_ref[pl.ds(UP_Y.index(i) * nx + row, 1), :] = value[ny - 1 : ny, :]
        if i in DOWN_Y:
            ydn_ref[pl.ds(DOWN_Y.index(i) * nx + row, 1), :] = value[0:1, :]


def emit_faces(nx, post_ref, faces):
    def place(odd):
        for k, i in enumerate(UP_X):
            faces[odd][k] = post_ref[i, nx - 1]
        for k, i in enumerate(DOWN_X):
            faces[1 - odd][k] = post_ref[i, 0]

    by_parity("gx", place)


def sort_halos(xa_ref, xb_ref, ya_ref, yb_ref, xup_ref, xdn_ref, yup_ref, ydn_ref):
    def place_x(odd):
        xup_ref[...] = (xb_ref, xa_ref)[odd][...]
        xdn_ref[...] = (xa_ref, xb_ref)[odd][...]

    def place_y(odd):
        yup_ref[...] = (yb_ref, ya_ref)[odd][...]
        ydn_ref[...] = (ya_ref, yb_ref)[odd][...]

    by_parity("gx", place_x)
    by_parity("gy", place_y)


def first_kernel(
    f_hbm, om_hbm, so_hbm, post_ref, xa_ref, xb_ref, yup_ref, ydn_ref, om_ref, so_ref, f_ref, sem
):
    nx = f_ref.shape[1]
    parts = sem.shape[0] - 2
    rows = nx // parts

    def load(k):
        at = pl.ds(k * rows, rows)
        return pltpu.make_async_copy(f_hbm.at[:, at], f_ref.at[:, at], sem.at[k])

    loads = [load(k) for k in range(parts)]
    omega = pltpu.make_async_copy(om_hbm, om_ref, sem.at[parts])
    solid = pltpu.make_async_copy(so_hbm, so_ref, sem.at[parts + 1])
    omega.start()
    solid.start()
    for k in range(parts):
        loads[k].start()

    def step(x, carry):
        post = collide([f_ref[i, x] for i in range(NVEL)], om_ref[x], so_ref[x] > 0)
        emit_post(post, x, nx, post_ref, yup_ref, ydn_ref)
        return carry

    for k in range(parts):
        loads[k].wait()
        if k == 0:
            omega.wait()
            solid.wait()
        lax.fori_loop(k * rows, (k + 1) * rows, step, 0, unroll=UNROLL)
    emit_faces(nx, post_ref, (xa_ref, xb_ref))


def streamed(x, nx, post_ref, xup_ref, xdn_ref, yup_ref, ydn_ref):
    ny = post_ref.shape[2]
    row_id = lax.broadcasted_iota(jnp.int32, (ny, post_ref.shape[3]), 0)
    f = []
    for i in range(NVEL):
        cx, cy, _ = velocity_table[i]
        if cx == 1:
            value = jnp.where(x == 0, xup_ref[UP_X.index(i)], post_ref[i, lax.rem(x + nx - 1, nx)])
        elif cx == -1:
            value = jnp.where(
                x == nx - 1, xdn_ref[DOWN_X.index(i)], post_ref[i, lax.rem(x + 1, nx)]
            )
        else:
            value = post_ref[i, x]
        if cy == 1:
            edge = yup_ref[pl.ds(UP_Y.index(i) * nx + x, 1), :]
            value = jnp.where(row_id == 0, edge, pltpu.roll(value, 1, 0))
        elif cy == -1:
            edge = ydn_ref[pl.ds(DOWN_Y.index(i) * nx + x, 1), :]
            value = jnp.where(row_id == ny - 1, edge, pltpu.roll(value, ny - 1, 0))
        f.append(value)
    return f


def second_kernel(
    p_ref,
    ra_ref,
    rb_ref,
    sa_ref,
    sb_ref,
    om_ref,
    so_ref,
    gate_ref,
    post_ref,
    xa_ref,
    xb_ref,
    yup_ref,
    ydn_ref,
    *halos,
):
    nx = p_ref.shape[1]
    sort_halos(ra_ref, rb_ref, sa_ref, sb_ref, *halos)

    def step(x, carry):
        f = streamed(x, nx, p_ref, *halos)
        post = collide(f, om_ref[x], so_ref[x] > 0)
        emit_post(post, x, nx, post_ref, yup_ref, ydn_ref)
        return carry

    lax.fori_loop(0, nx, step, 0, unroll=UNROLL)
    emit_faces(nx, post_ref, (xa_ref, xb_ref))


def pack_kernel(xa_ref, xb_ref, yup_ref, ydn_ref, gate_ref, oa_ref, ob_ref):
    nx = yup_ref.shape[0] // len(UP_Y)
    ny = xa_ref.shape[1]

    def corners(ids, out, row, odd):
        xu_ref, xd_ref = ((xb_ref, xa_ref), (xa_ref, xb_ref))[odd]
        for k, i in enumerate(ids):
            if velocity_table[i][0] == 1:
                out[k * nx : k * nx + 1, :] = xu_ref[UP_X.index(i), row : row + 1, :]
            elif velocity_table[i][0] == -1:
                at = k * nx + nx - 1
                out[at : at + 1, :] = xd_ref[DOWN_X.index(i), row : row + 1, :]

    def place(odd):
        up, down = (oa_ref, ob_ref)[odd], (ob_ref, oa_ref)[odd]
        up[...] = yup_ref[...]
        down[...] = ydn_ref[...]
        by_parity("gx", lambda x_odd: corners(UP_Y, up, ny - 1, x_odd))
        by_parity("gx", lambda x_odd: corners(DOWN_Y, down, 0, x_odd))

    by_parity("gy", place)


def gram_kernel(
    s_hbm, basis_hbm, snap_hbm, gate_ref, a_ref, h_hbm, g_ref, t_ref, s_ref, basis_ref, snap_ref, h_ref, ins, outs
):
    rank = basis_ref.shape[0]
    depth = basis_ref.shape[1]
    extra = snap_ref.shape[0]
    cols = a_ref.shape[1]
    weights = pltpu.make_async_copy(s_hbm, s_ref, outs.at[depth // 8])
    weights.start()
    zero = jnp.zeros((cols - rank - extra, 8, 128), F32)

    def load(q):
        at = pl.ds(pl.multiple_of(q * 8, 8), 8)
        return (
            pltpu.make_async_copy(basis_hbm.at[:, at], basis_ref.at[:, at], ins.at[0, q]),
            pltpu.make_async_copy(snap_hbm.at[:, at], snap_ref.at[:, at], ins.at[1, q]),
        )

    def save(q):
        at = pl.ds(pl.multiple_of(q * 1024, 1024), 1024)
        return pltpu.make_async_copy(h_ref.at[:, at], h_hbm.at[:, at], outs.at[q])

    def begin(q, carry):
        for copy in load(q):
            copy.start()
        return carry

    def finish(q, carry):
        save(q).wait()
        return carry

    lax.fori_loop(0, depth // 8, begin, 0)
    weights.wait()
    same = lax.broadcasted_iota(jnp.int32, (rank, rank), 0) == lax.broadcasted_iota(
        jnp.int32, (rank, rank), 1
    )
    scale = jnp.sum(jnp.where(same, s_ref[...], 0.0), axis=1, keepdims=True)
    scale = jnp.broadcast_to(scale, (rank, 128))
    t_ref[...] = jnp.concatenate([scale, jnp.ones((cols - rank, 128), F32)], axis=0)

    def step(q, carry):
        for copy in load(q):
            copy.wait()
        r = pl.multiple_of(q * 8, 8)
        top = jnp.swapaxes(basis_ref[:, pl.ds(r, 8), :], 0, 1)
        low = jnp.concatenate([snap_ref[:, pl.ds(r, 8), :], zero], axis=0)
        low = jnp.swapaxes(low, 0, 1)
        for t in range(8):
            rows = jnp.concatenate([top[t] * scale, low[t]], axis=0)
            a_ref[r + t] = rows
            at = pl.ds(pl.multiple_of((r + t) * 128, 128), 128)
            high = rows.astype(BF16)
            h_ref[0:cols, at] = high
            h_ref[cols : 2 * cols, at] = (rows - high.astype(F32)).astype(BF16)
        save(q).start()
        return carry

    lax.fori_loop(0, depth // 8, step, 0)
    acc = lax.dot_general(
        h_ref[...], h_ref[0:cols, :], (((1,), (1,)), ((), ())), preferred_element_type=F32
    )
    cross = acc[cols:, :]
    eye = (
        lax.broadcasted_iota(jnp.int32, (cols, cols), 0)
        == lax.broadcasted_iota(jnp.int32, (cols, cols), 1)
    ).astype(F32)
    flipped = lax.dot_general(
        eye, cross, (((1,), (1,)), ((), ())), precision=HIGHEST, preferred_element_type=F32
    )
    g_ref[...] = acc[:cols, :] + cross + flipped
    lax.fori_loop(0, depth // 8, finish, 0)


def factor_kernel(inv_rows, g_ref, u_ref, li_ref, w_ref):
    cols = g_ref.shape[0]
    known = cols - 1
    blocks = cols // 8
    pad = jnp.zeros((8, 128 - cols), F32)
    sub = lax.broadcasted_iota(jnp.int32, (8, 128), 0)
    lane = lax.broadcasted_iota(jnp.int32, (8, 128), 1)
    left = [
        jnp.concatenate([g_ref[8 * b : 8 * b + 8, :] * inv_rows, pad], axis=1) for b in range(blocks)
    ]
    right = [(sub + 8 * b == lane).astype(F32) for b in range(blocks)]
    for p in range(blocks):
        live = range(p, blocks)
        width = min(8, known - 8 * p)
        col = [
            {
                b: jnp.broadcast_to(left[b][:, 8 * p + t : 8 * p + t + 1], (8, 128))
                for b in live
            }
            for t in range(width)
        ]
        for t in range(width):
            pivot = lax.rsqrt(jnp.broadcast_to(col[t][p][t : t + 1, :], (8, 128)))
            lcol = {b: col[t][b] * pivot for b in live}
            lcol[p] = jnp.where(sub > t, lcol[p], 0.0)
            for v in range(t + 1, width):
                m = jnp.broadcast_to(lcol[p][v : v + 1, :], (8, 128))
                for b in live:
                    col[v][b] = col[v][b] - lcol[b] * m
            top = jnp.broadcast_to(left[p][t : t + 1, :], (8, 128)) * pivot
            aug = jnp.broadcast_to(right[p][t : t + 1, :], (8, 128)) * pivot
            for b in live:
                left[b] = left[b] - lcol[b] * top
                right[b] = right[b] - lcol[b] * aug
            left[p] = jnp.where(sub == t, top, left[p])
            right[p] = jnp.where(sub == t, aug, right[p])
    fill = jnp.zeros((8, 128), F32)
    for b in range(blocks):
        row = sub + 8 * b
        upper = jnp.where(jnp.logical_and(row <= lane, lane < known), left[b], 0.0)
        inverse = jnp.where(jnp.logical_and(row >= lane, row < known), right[b], 0.0)
        u_ref[8 * b : 8 * b + 8, :] = upper[:, :cols]
        li_ref[8 * b : 8 * b + 8, :] = inverse[:, :cols]
        high = inverse.astype(BF16).astype(F32)
        wide = jnp.concatenate([high, fill], axis=1)
        rest = jnp.concatenate([inverse - high, fill], axis=1)
        wide = wide + pltpu.roll(rest, cols, 1) + pltpu.roll(wide, 2 * cols, 1)
        w_ref[8 * b : 8 * b + 8, :] = wide[:, : 3 * cols]


def rotate_kernel(w_ref, h_hbm, o_ref, h_ref, out_ref, ins, sem):
    cols = w_ref.shape[0]
    depth = out_ref.shape[1]
    weight = w_ref[...].astype(BF16)

    def copy(q):
        at = pl.ds(pl.multiple_of(q * 8, 8), 8)
        return pltpu.make_async_copy(out_ref.at[:, at, :], o_ref.at[:, at, :], sem.at[q])

    def load(q):
        at = pl.ds(pl.multiple_of(q * 1024, 1024), 1024)
        return pltpu.make_async_copy(h_hbm.at[:, at], h_ref.at[:, at], ins.at[q])

    def begin(q, carry):
        load(q).start()
        return carry

    lax.fori_loop(0, depth // 8, begin, 0)

    def step(q, carry):
        load(q).wait()
        at = pl.ds(pl.multiple_of(q * 1024, 1024), 1024)
        high = h_ref[0:cols, at]
        low = h_ref[cols : 2 * cols, at]
        res = lax.dot_general(
            weight,
            jnp.concatenate([high, high, low], axis=0),
            (((1,), (0,)), ((), ())),
            preferred_element_type=F32,
        )
        res = jnp.stack([res[:, t * 128 : (t + 1) * 128] for t in range(8)], axis=0)
        out_ref[:, pl.ds(pl.multiple_of(q * 8, 8), 8), :] = jnp.swapaxes(res, 0, 1)
        copy(q).start()
        return carry

    lax.fori_loop(0, depth // 8, step, 0)

    def finish(q, carry):
        copy(q).wait()
        return carry

    lax.fori_loop(0, depth // 8, finish, 0)


def final_kernel(
    p_ref, ra_ref, rb_ref, sa_ref, sb_ref, so_ref, a_ref, gate_ref, f_hbm, c_ref, v_ref, vel_ref, f_ref, sem, *halos
):
    nx, ny, nz = p_ref.shape[1:]
    nxc, nyc = nx // 2, ny // 2
    sort_halos(ra_ref, rb_ref, sa_ref, sb_ref, *halos)

    def copy(xc):
        at = pl.ds(2 * xc, 2)
        return pltpu.make_async_copy(f_ref.at[:, at], f_hbm.at[:, at], sem.at[xc])

    def finish(xc, carry):
        copy(xc).wait()
        return carry

    def step(xc, carry):
        total = [None] * 3
        for t in range(2):
            x = 2 * xc + t
            f = streamed(x, nx, p_ref, *halos)
            for i in range(NVEL):
                f_ref[i, x] = f[i]
            _, u = moments(f)
            fluid = (so_ref[x] == 0).astype(F32)
            for k in range(3):
                part = u[k] * fluid
                total[k] = part if t == 0 else total[k] + part
        for k in range(3):
            at = pl.multiple_of((k * nxc + xc) * ny, ny)
            for t in range(nz // 128):
                vel_ref[t, pl.ds(at, ny), :] = total[k][:, t * 128 : (t + 1) * 128]
        copy(xc).start()
        return carry

    lax.fori_loop(0, nxc, step, 0, unroll=UNROLL_F)
    depth = 3 * nxc * nyc
    pairs = []
    for t in range(nz // 128):
        half = vel_ref.at[t]
        pairs.append(half[pl.ds(0, depth, stride=2), :] + half[pl.ds(1, depth, stride=2), :])
    pairs = jnp.concatenate(pairs, axis=1)
    pick = (
        lax.broadcasted_iota(jnp.int32, (nz, nz // 2), 0) // 2
        == lax.broadcasted_iota(jnp.int32, (nz, nz // 2), 1)
    ).astype(F32)
    coarse = lax.dot_general(
        pairs, pick, (((1,), (0,)), ((), ())), precision=HIGHEST, preferred_element_type=F32
    )
    c_ref[...] = coarse * (SPEED_SCALE / 8.0)
    cols = a_ref.shape[1]

    def inner(r, acc):
        return acc + a_ref[r] * c_ref[pl.ds(r, 1), :]

    acc = lax.fori_loop(0, depth, inner, jnp.zeros((cols, 128), F32), unroll=8)
    dots = jnp.sum(acc, axis=1, keepdims=True)
    own = jnp.sum(c_ref[...] * c_ref[...])
    down = lax.broadcasted_iota(jnp.int32, (cols, 1), 0)
    dots = jnp.where(down == cols - 1, own, dots)
    across = lax.broadcasted_iota(jnp.int32, (cols, 128), 1)
    diag = jnp.where(across == lax.broadcasted_iota(jnp.int32, (cols, 128), 0), dots, 0.0)
    line = jnp.sum(diag, axis=0, keepdims=True)
    v_ref[...] = jnp.broadcast_to(line, v_ref.shape)
    lax.fori_loop(0, nxc, finish, 0)


def last_kernel(
    inv_rows,
    v_ref,
    li_ref,
    u_ref,
    s_ref,
    c_ref,
    basis_hbm,
    snap_hbm,
    q_ref,
    uo_hbm,
    o_ref,
    uo_ref,
    basis_ref,
    snap_ref,
    tall_ref,
    row_ref,
    ins,
    sem,
):
    cols = li_ref.shape[0]
    known = cols - 1
    rank, depth = basis_ref.shape[:2]
    extra = snap_ref.shape[0]
    parts = ins.shape[1] - 1
    size = depth // parts
    loads = []
    for k in range(parts):
        at = pl.ds(k * size, size)
        loads.append(
            (
                pltpu.make_async_copy(basis_hbm.at[:, at], basis_ref.at[:, at], ins.at[0, k]),
                pltpu.make_async_copy(snap_hbm.at[:, at], snap_ref.at[:, at], ins.at[1, k]),
            )
        )
        for copy in loads[-1]:
            copy.start()
    line = jnp.sum(v_ref[...], axis=0, keepdims=True)[:, :cols] * inv_rows
    across = lax.broadcasted_iota(jnp.int32, (1, cols), 1)
    norm = jnp.sum(jnp.where(across == known, line, 0.0), axis=1, keepdims=True)
    inverse = li_ref[...]
    coef = jnp.sum(inverse * jnp.where(across == known, 0.0, line), axis=1, keepdims=True)
    left = norm - jnp.sum(coef * coef, axis=0, keepdims=True)
    pivot = lax.rsqrt(left)
    col_id = lax.broadcasted_iota(jnp.int32, (cols, cols), 1)
    row_id = lax.broadcasted_iota(jnp.int32, (cols, cols), 0)
    edge = jnp.where(row_id == known, left * pivot, coef)
    uo_ref[...] = jnp.where(col_id == known, edge, u_ref[...])
    factor = pltpu.make_async_copy(uo_ref, uo_hbm, ins.at[0, parts])
    factor.start()
    weight = jnp.sum(inverse * coef, axis=0, keepdims=True) * (-pivot)
    diag = jnp.where(row_id == col_id, weight, 0.0)
    tall_ref[...] = jnp.sum(diag, axis=1, keepdims=True) * s_ref[...]

    def step(q, carry):
        at = pl.ds(pl.multiple_of(q * 16, 16), 16)
        total = [c_ref[at, :] * pivot] + [None] * 3
        for k in range(rank + extra):
            value = basis_ref[k, at, :] if k < rank else snap_ref[k - rank, at, :]
            value = value * tall_ref[k : k + 1, :]
            total[k % 4] = value if total[k % 4] is None else total[k % 4] + value
        row_ref[at, :] = (total[0] + total[1]) + (total[2] + total[3])
        return carry

    for k in range(parts):
        for copy in loads[k]:
            copy.wait()
        lax.fori_loop(k * size // 16, (k + 1) * size // 16, step, 0)
    copy = pltpu.make_async_copy(row_ref, o_ref.at[known], sem)
    copy.start()
    factor.wait()
    copy.wait()


def in_hbm(value):
    return pltpu.with_memory_space_constraint(value, pltpu.HBM)


def shape(dims, dtype=F32):
    return jax.ShapeDtypeStruct(dims, dtype)


def halo_y(xa, xb, yup, ydn, gate):
    sends = pl.pallas_call(
        pack_kernel,
        out_shape=(shape(yup.shape), shape(ydn.shape)),
        in_specs=[VMEM] * 4 + [ANY],
        name="pack",
        compiler_params=params(2),
    )(xa, xb, yup, ydn, gate)
    return swap(sends, "gy")


def rounds():
    steps = []
    for axis in ("gx", "gy"):
        bit = 1
        while bit < lax.axis_size(axis):
            steps.append((axis, bit))
            bit *= 2
    return steps


def exchange(value, steps):
    for axis, bit in steps:
        pairs = [(s, s ^ bit) for s in range(lax.axis_size(axis))]
        value = value + lax.ppermute(value, axis, pairs)
    return value


def on_device(populations, relax_rate, solid_mask, singular_values, basis, snapshots):
    _, nx, ny, nz = populations.shape
    rank, extra = basis.shape[0], snapshots.shape[0]
    cols = rank + extra + 1
    tail = basis.shape[1:]
    depth = tail[0] * tail[1] * tail[2]
    n_dev = lax.axis_size("gx") * lax.axis_size("gy")
    inv_rows = 1.0 / (depth * tail[3] * n_dev)
    edges = len(UP_Y) * nx
    post_shapes = (
        shape((NVEL, nx, ny, nz)),
        shape((len(UP_X), ny, nz)),
        shape((len(DOWN_X), ny, nz)),
        shape((edges, nz)),
        shape((edges, nz)),
    )
    halos = [pltpu.VMEM(post_shapes[k].shape, F32) for k in range(1, 5)]
    post, xa, xb, yup, ydn, omega, solid = pl.pallas_call(
        first_kernel,
        out_shape=post_shapes + (shape((nx, ny, nz)), shape((nx, ny, nz), jnp.int32)),
        in_specs=[HBM] * 3,
        scratch_shapes=[pltpu.VMEM((NVEL, nx, ny, nz), F32), pltpu.SemaphoreType.DMA((6,))],
        name="first",
        compiler_params=params(6),
    )(*[in_hbm(value) for value in (populations, relax_rate, solid_mask)])
    xa, xb = swap((xa, xb), "gx")
    weights = in_hbm(singular_values.reshape(1, rank))
    modes = in_hbm(basis.reshape(rank, depth, 128))
    earlier = in_hbm(snapshots.reshape(extra, depth, 128))
    blocks = depth // 8
    rows, halves, gram, scale = pl.pallas_call(
        gram_kernel,
        out_shape=(
            shape((depth, cols, 128)),
            pltpu.HBM((2 * cols, depth * 128), BF16),
            shape((cols, cols)),
            shape((cols, 128)),
        ),
        in_specs=[HBM, HBM, HBM, ANY],
        out_specs=(VMEM, HBM, VMEM, VMEM),
        scratch_shapes=[
            pltpu.VMEM((1, rank), F32),
            pltpu.VMEM((rank, depth, 128), F32),
            pltpu.VMEM((extra, depth, 128), F32),
            pltpu.VMEM((2 * cols, depth * 128), BF16),
            pltpu.SemaphoreType.DMA((2, blocks)),
            pltpu.SemaphoreType.DMA((blocks + 1,)),
        ],
        name="gram",
        compiler_params=params(12),
    )(weights, modes, earlier, omega)
    ya, yb = halo_y(xa, xb, yup, ydn, gram)
    steps = rounds()
    gram = exchange(gram, steps[:2])
    post, xa, xb, yup, ydn = pl.pallas_call(
        second_kernel,
        out_shape=post_shapes,
        in_specs=[VMEM] * 7 + [ANY],
        scratch_shapes=halos,
        name="second",
        compiler_params=params(4),
    )(post, xa, xb, ya, yb, omega, solid, gram)
    xa, xb = swap((xa, xb), "gx")
    gram = exchange(gram, steps[2:-1])
    ya, yb = halo_y(xa, xb, yup, ydn, gram)
    gram = exchange(gram, steps[-1:])
    upper, inverse, split = pl.pallas_call(
        lambda *refs: factor_kernel(inv_rows, *refs),
        out_shape=(shape((cols, cols)), shape((cols, cols)), shape((cols, 3 * cols))),
        name="factor",
        compiler_params=params(4),
    )(gram)
    field, coarse, line = pl.pallas_call(
        final_kernel,
        out_shape=(shape((NVEL, nx, ny, nz)), shape((depth, 128)), pltpu.VMEM((n_dev, 128), F32)),
        in_specs=[VMEM] * 7 + [ANY],
        out_specs=(ANY, VMEM, VMEM),
        scratch_shapes=[
            pltpu.VMEM((nz // 128, 3 * (nx // 2) * ny, 128), F32),
            pltpu.VMEM((NVEL, nx, ny, nz), F32),
            pltpu.SemaphoreType.DMA((nx // 2,)),
        ]
        + halos,
        name="final",
        compiler_params=params(6),
    )(post, xa, xb, ya, yb, solid, rows, inverse)
    lines = lax.all_to_all(line, ("gx", "gy"), 0, 0, tiled=True)
    rotated = pl.pallas_call(
        rotate_kernel,
        out_shape=shape((cols, depth, 128)),
        in_specs=[VMEM, HBM],
        out_specs=ANY,
        scratch_shapes=[
            pltpu.VMEM((2 * cols, depth * 128), BF16),
            pltpu.VMEM((cols, depth, 128), F32),
            pltpu.SemaphoreType.DMA((blocks,)),
            pltpu.SemaphoreType.DMA((blocks,)),
        ],
        name="rotate",
        compiler_params=params(12),
    )(split, in_hbm(halves))
    upper, rotated = pl.pallas_call(
        lambda *refs: last_kernel(inv_rows, *refs),
        out_shape=(shape((cols, cols)), shape((cols, depth, 128))),
        in_specs=[VMEM] * 5 + [HBM] * 2 + [ANY],
        out_specs=(ANY, ANY),
        scratch_shapes=[
            pltpu.VMEM((cols, cols), F32),
            pltpu.VMEM((rank, depth, 128), F32),
            pltpu.VMEM((extra, depth, 128), F32),
            pltpu.VMEM((cols, 128), F32),
            pltpu.VMEM((depth, 128), F32),
            pltpu.SemaphoreType.DMA((2, 4)),
            pltpu.SemaphoreType.DMA,
        ],
        input_output_aliases={7: 1},
        name="last",
        compiler_params=params(8),
    )(lines, inverse, upper, scale, coarse, modes, earlier, rotated)
    return field, upper, rotated.reshape((cols,) + tail)


def solution(mesh):
    return jax.shard_map(
        on_device,
        mesh=mesh,
        in_specs=(
            P(None, "gx", "gy", None),
            P("gx", "gy", None),
            P("gx", "gy", None),
            P(),
            P(None, None, "gx", "gy", None),
            P(None, None, "gx", "gy", None),
        ),
        out_specs=(P(None, "gx", "gy", None), P(), P(None, None, "gx", "gy", None)),
        check_vma=False,
    )
```

```python
import jax
import jax.numpy as jnp
from jax import lax
from jax.experimental import pallas as pl
from jax.experimental.pallas import tpu as pltpu
from jax.sharding import PartitionSpec as P


velocity_table = [
    (0, 0, 0),
    (1, 0, 0),
    (-1, 0, 0),
    (0, 1, 0),
    (0, -1, 0),
    (0, 0, 1),
    (0, 0, -1),
    (1, 1, 0),
    (-1, -1, 0),
    (1, -1, 0),
    (-1, 1, 0),
    (1, 0, 1),
    (-1, 0, -1),
    (1, 0, -1),
    (-1, 0, 1),
    (0, 1, 1),
    (0, -1, -1),
    (0, 1, -1),
    (0, -1, 1),
]
NVEL = 19
PAIRS = [(i, i + 1) for i in range(1, NVEL, 2)]
W_REST, W_FACE, W_EDGE = 1.0 / 3.0, 1.0 / 18.0, 1.0 / 36.0
UP_X = [i for i in range(NVEL) if velocity_table[i][0] == 1]
DOWN_X = [i for i in range(NVEL) if velocity_table[i][0] == -1]
UP_Y = [i for i in range(NVEL) if velocity_table[i][1] == 1]
DOWN_Y = [i for i in range(NVEL) if velocity_table[i][1] == -1]
SPEED_SCALE = 10.0
UNROLL = 4
ROUND_AXES = ("gy", "gx")
CUTS = (1, 3, 4)


def cuts(count):
    return tuple(count * cut // 5 for cut in CUTS)


UNROLL_F = 1
HIGHEST = lax.Precision.HIGHEST
F32 = jnp.float32
BF16 = jnp.bfloat16
VMEM = pl.BlockSpec(memory_space=pltpu.VMEM)
ANY = pl.BlockSpec(memory_space=pl.ANY)
HBM = pl.BlockSpec(memory_space=pltpu.HBM)


def params(mib=40):
    return pltpu.CompilerParams(vmem_limit_bytes=mib << 20)


def ring_pairs(axis):
    count = lax.axis_size(axis)
    partner = [(s, s ^ 1) for s in range(count)]
    other = [(s, (s + 1 if s % 2 else s - 1) % count) for s in range(count)]
    return partner, other


def swap(values, axis):
    partner, other = ring_pairs(axis)
    return lax.ppermute(values[0], axis, partner), lax.ppermute(values[1], axis, other)


def by_parity(axis, place):
    odd = lax.rem(lax.axis_index(axis), 2)

    @pl.when(odd == 0)
    def _():
        place(0)

    @pl.when(odd == 1)
    def _():
        place(1)


def moments(f):
    plus = [f[a] + f[b] for a, b in PAIRS]
    minus = [f[a] - f[b] for a, b in PAIRS]
    rho = f[0] + plus[0]
    for p in plus[1:]:
        rho = rho + p
    mx, my, mz, m7, m9, m11, m13, m15, m17 = minus
    jx = (mx + m7) + (m9 + m11) + m13
    jy = (my + m7) + (m15 + m17) - m9
    jz = (mz + m11) + (m15 - m13) - m17
    r = 1.0 / rho
    return rho, (jx * r, jy * r, jz * r)


def collide(f, omega, solid):
    rho, u = moments(f)
    base = 1.0 - 1.5 * (u[0] * u[0] + u[1] * u[1] + u[2] * u[2])
    keep = 1.0 - omega
    wr = omega * rho
    post = [None] * NVEL
    post[0] = jnp.where(solid, f[0], keep * f[0] + (W_REST * wr) * base)
    w_face, w_edge = W_FACE * wr, W_EDGE * wr
    for a, b in PAIRS:
        vel = velocity_table[a]
        along = None
        for axis in range(3):
            if vel[axis] == 1:
                along = u[axis] if along is None else along + u[axis]
            elif vel[axis] == -1:
                along = along - u[axis]
        w = w_face if a < 7 else w_edge
        even = w * (base + 4.5 * (along * along))
        odd = w * (3.0 * along)
        post[a] = jnp.where(solid, f[b], keep * f[a] + (even + odd))
        post[b] = jnp.where(solid, f[a], keep * f[b] + (even - odd))
    return post


def emit_post(post, x, nx, post_ref, yup_ref, ydn_ref):
    ny = post_ref.shape[2]
    for i in range(NVEL):
        cz = velocity_table[i][2]
        value = post[i] if cz == 0 else pltpu.roll(post[i], cz % post[i].shape[1], 1)
        post_ref[i, x] = value
        if i in UP_Y:
            yup_ref[pl.ds(UP_Y.index(i) * nx + x, 1), :] = value[ny - 1 : ny, :]
        if i in DOWN_Y:
            ydn_ref[pl.ds(DOWN_Y.index(i) * nx + x, 1), :] = value[0:1, :]


def emit_edges(yup_ref, ydn_ref, edges):
    def place(odd):
        edges[odd][...] = yup_ref[...]
        edges[1 - odd][...] = ydn_ref[...]

    by_parity("gy", place)


def sort_halos(xa_ref, xb_ref, ya_ref, yb_ref, xup_ref, xdn_ref, yup_ref, ydn_ref):
    def place_x(odd):
        xup_ref[...] = (xb_ref, xa_ref)[odd][...]
        xdn_ref[...] = (xa_ref, xb_ref)[odd][...]

    def place_y(odd):
        yup_ref[...] = (yb_ref, ya_ref)[odd][...]
        ydn_ref[...] = (ya_ref, yb_ref)[odd][...]

    by_parity("gx", place_x)
    by_parity("gy", place_y)


def first_kernel(
    f_hbm, om_hbm, so_hbm, post_ref, ya_ref, yb_ref, om_ref, so_ref, f_ref, yup_ref, ydn_ref, sem
):
    nx = f_ref.shape[1]
    parts = sem.shape[0] - 2
    rows = nx // parts

    def load(k):
        at = pl.ds(k * rows, rows)
        return pltpu.make_async_copy(f_hbm.at[:, at], f_ref.at[:, at], sem.at[k])

    loads = [load(k) for k in range(parts)]
    omega = pltpu.make_async_copy(om_hbm, om_ref, sem.at[parts])
    solid = pltpu.make_async_copy(so_hbm, so_ref, sem.at[parts + 1])
    omega.start()
    solid.start()
    for k in range(parts):
        loads[k].start()

    def step(x, carry):
        post = collide([f_ref[i, x] for i in range(NVEL)], om_ref[x], so_ref[x] > 0)
        emit_post(post, x, nx, post_ref, yup_ref, ydn_ref)
        return carry

    for k in range(parts):
        loads[k].wait()
        if k == 0:
            omega.wait()
            solid.wait()
        lax.fori_loop(k * rows, (k + 1) * rows, step, 0, unroll=UNROLL)
    emit_edges(yup_ref, ydn_ref, (ya_ref, yb_ref))


def shift_y(i, value, src, nx, yup_ref, ydn_ref):
    ny = value.shape[0]
    cy = velocity_table[i][1]
    if cy == 0:
        return value
    row_id = lax.broadcasted_iota(jnp.int32, value.shape, 0)
    if cy == 1:
        edge = yup_ref[pl.ds(UP_Y.index(i) * nx + src, 1), :]
        return jnp.where(row_id == 0, edge, pltpu.roll(value, 1, 0))
    edge = ydn_ref[pl.ds(DOWN_Y.index(i) * nx + src, 1), :]
    return jnp.where(row_id == ny - 1, edge, pltpu.roll(value, ny - 1, 0))


def streamed(x, nx, post_ref, xup_ref, xdn_ref, yup_ref, ydn_ref):
    f = []
    for i in range(NVEL):
        cx = velocity_table[i][0]
        src = x if cx == 0 else lax.rem(x + (nx - cx), nx)
        value = shift_y(i, post_ref[i, src], src, nx, yup_ref, ydn_ref)
        if cx == 1:
            value = jnp.where(x == 0, xup_ref[UP_X.index(i)], value)
        elif cx == -1:
            value = jnp.where(x == nx - 1, xdn_ref[DOWN_X.index(i)], value)
        f.append(value)
    return f


def second_kernel(
    p_ref,
    ra_ref,
    rb_ref,
    sa_ref,
    sb_ref,
    om_ref,
    so_ref,
    gate_ref,
    post_ref,
    ya_ref,
    yb_ref,
    yup_ref,
    ydn_ref,
    *halos,
):
    nx = p_ref.shape[1]
    sort_halos(ra_ref, rb_ref, sa_ref, sb_ref, *halos)

    def step(x, carry):
        f = streamed(x, nx, p_ref, *halos)
        post = collide(f, om_ref[x], so_ref[x] > 0)
        emit_post(post, x, nx, post_ref, yup_ref, ydn_ref)
        return carry

    lax.fori_loop(0, nx, step, 0, unroll=UNROLL)
    emit_edges(yup_ref, ydn_ref, (ya_ref, yb_ref))


def pack_kernel(ya_ref, yb_ref, post_ref, gate_ref, xa_ref, xb_ref):
    nx = post_ref.shape[1]

    def place(odd_y):
        yup_ref, ydn_ref = ((yb_ref, ya_ref), (ya_ref, yb_ref))[odd_y]

        def faces(odd_x):
            up_ref, down_ref = ((xa_ref, xb_ref), (xb_ref, xa_ref))[odd_x]
            for k, i in enumerate(UP_X):
                up_ref[k] = shift_y(i, post_ref[i, nx - 1], nx - 1, nx, yup_ref, ydn_ref)
            for k, i in enumerate(DOWN_X):
                down_ref[k] = shift_y(i, post_ref[i, 0], 0, nx, yup_ref, ydn_ref)

        by_parity("gx", faces)

    by_parity("gy", place)


def gram_kernel(
    s_hbm, basis_hbm, snap_hbm, gate_ref, a_ref, h_hbm, g_ref, t_ref, s_ref, basis_ref, snap_ref, h_ref, ins, outs
):
    rank = basis_ref.shape[0]
    depth = basis_ref.shape[1]
    extra = snap_ref.shape[0]
    cols = a_ref.shape[1]
    weights = pltpu.make_async_copy(s_hbm, s_ref, outs.at[depth // 8])
    weights.start()
    zero = jnp.zeros((cols - rank - extra, 8, 128), F32)

    def load(q):
        at = pl.ds(pl.multiple_of(q * 8, 8), 8)
        return (
            pltpu.make_async_copy(basis_hbm.at[:, at], basis_ref.at[:, at], ins.at[0, q]),
            pltpu.make_async_copy(snap_hbm.at[:, at], snap_ref.at[:, at], ins.at[1, q]),
        )

    def save(q):
        at = pl.ds(pl.multiple_of(q * 1024, 1024), 1024)
        return pltpu.make_async_copy(h_ref.at[:, at], h_hbm.at[:, at], outs.at[q])

    def begin(q, carry):
        for copy in load(q):
            copy.start()
        return carry

    def finish(q, carry):
        save(q).wait()
        return carry

    lax.fori_loop(0, depth // 8, begin, 0)
    weights.wait()
    same = lax.broadcasted_iota(jnp.int32, (rank, rank), 0) == lax.broadcasted_iota(
        jnp.int32, (rank, rank), 1
    )
    scale = jnp.sum(jnp.where(same, s_ref[...], 0.0), axis=1, keepdims=True)
    scale = jnp.broadcast_to(scale, (rank, 128))
    t_ref[...] = jnp.concatenate([scale, jnp.ones((cols - rank, 128), F32)], axis=0)

    def step(q, carry):
        for copy in load(q):
            copy.wait()
        r = pl.multiple_of(q * 8, 8)
        top = jnp.swapaxes(basis_ref[:, pl.ds(r, 8), :], 0, 1)
        low = jnp.concatenate([snap_ref[:, pl.ds(r, 8), :], zero], axis=0)
        low = jnp.swapaxes(low, 0, 1)
        for t in range(8):
            rows = jnp.concatenate([top[t] * scale, low[t]], axis=0)
            a_ref[r + t] = rows
            at = pl.ds(pl.multiple_of((r + t) * 128, 128), 128)
            high = rows.astype(BF16)
            h_ref[0:cols, at] = high
            h_ref[cols : 2 * cols, at] = (rows - high.astype(F32)).astype(BF16)
        save(q).start()
        return carry

    lax.fori_loop(0, depth // 8, step, 0)
    acc = lax.dot_general(
        h_ref[...], h_ref[0:cols, :], (((1,), (1,)), ((), ())), preferred_element_type=F32
    )
    cross = acc[cols:, :]
    eye = (
        lax.broadcasted_iota(jnp.int32, (cols, cols), 0)
        == lax.broadcasted_iota(jnp.int32, (cols, cols), 1)
    ).astype(F32)
    flipped = lax.dot_general(
        eye, cross, (((1,), (1,)), ((), ())), precision=HIGHEST, preferred_element_type=F32
    )
    g_ref[...] = acc[:cols, :] + cross + flipped
    lax.fori_loop(0, depth // 8, finish, 0)


def factor_kernel(inv_rows, g_ref, u_ref, li_ref, w_ref):
    cols = g_ref.shape[0]
    known = cols - 1
    blocks = cols // 8
    pad = jnp.zeros((8, 128 - cols), F32)
    sub = lax.broadcasted_iota(jnp.int32, (8, 128), 0)
    lane = lax.broadcasted_iota(jnp.int32, (8, 128), 1)
    left = [
        jnp.concatenate([g_ref[8 * b : 8 * b + 8, :] * inv_rows, pad], axis=1) for b in range(blocks)
    ]
    right = [(sub + 8 * b == lane).astype(F32) for b in range(blocks)]
    for p in range(blocks):
        live = range(p, blocks)
        width = min(8, known - 8 * p)
        col = [
            {
                b: jnp.broadcast_to(left[b][:, 8 * p + t : 8 * p + t + 1], (8, 128))
                for b in live
            }
            for t in range(width)
        ]
        for t in range(width):
            pivot = lax.rsqrt(jnp.broadcast_to(col[t][p][t : t + 1, :], (8, 128)))
            lcol = {b: col[t][b] * pivot for b in live}
            lcol[p] = jnp.where(sub > t, lcol[p], 0.0)
            for v in range(t + 1, width):
                m = jnp.broadcast_to(lcol[p][v : v + 1, :], (8, 128))
                for b in live:
                    col[v][b] = col[v][b] - lcol[b] * m
            top = jnp.broadcast_to(left[p][t : t + 1, :], (8, 128)) * pivot
            aug = jnp.broadcast_to(right[p][t : t + 1, :], (8, 128)) * pivot
            for b in live:
                left[b] = left[b] - lcol[b] * top
                right[b] = right[b] - lcol[b] * aug
            left[p] = jnp.where(sub == t, top, left[p])
            right[p] = jnp.where(sub == t, aug, right[p])
    fill = jnp.zeros((8, 128), F32)
    for b in range(blocks):
        row = sub + 8 * b
        upper = jnp.where(jnp.logical_and(row <= lane, lane < known), left[b], 0.0)
        inverse = jnp.where(jnp.logical_and(row >= lane, row < known), right[b], 0.0)
        u_ref[8 * b : 8 * b + 8, :] = upper[:, :cols]
        li_ref[8 * b : 8 * b + 8, :] = inverse[:, :cols]
        high = inverse.astype(BF16).astype(F32)
        wide = jnp.concatenate([high, fill], axis=1)
        rest = jnp.concatenate([inverse - high, fill], axis=1)
        wide = wide + pltpu.roll(rest, cols, 1) + pltpu.roll(wide, 2 * cols, 1)
        w_ref[8 * b : 8 * b + 8, :] = wide[:, : 3 * cols]


def rotate_kernel(w_ref, h_hbm, o_ref, h_ref, out_ref, ins, sem):
    cols = w_ref.shape[0]
    depth = out_ref.shape[1]
    weight = w_ref[...].astype(BF16)

    def copy(q):
        at = pl.ds(pl.multiple_of(q * 8, 8), 8)
        return pltpu.make_async_copy(out_ref.at[:, at, :], o_ref.at[:, at, :], sem.at[q])

    def load(q):
        at = pl.ds(pl.multiple_of(q * 1024, 1024), 1024)
        return pltpu.make_async_copy(h_hbm.at[:, at], h_ref.at[:, at], ins.at[q])

    def begin(q, carry):
        load(q).start()
        return carry

    lax.fori_loop(0, depth // 8, begin, 0)

    def step(q, carry):
        load(q).wait()
        at = pl.ds(pl.multiple_of(q * 1024, 1024), 1024)
        high = h_ref[0:cols, at]
        low = h_ref[cols : 2 * cols, at]
        res = lax.dot_general(
            weight,
            jnp.concatenate([high, high, low], axis=0),
            (((1,), (0,)), ((), ())),
            preferred_element_type=F32,
        )
        res = jnp.stack([res[:, t * 128 : (t + 1) * 128] for t in range(8)], axis=0)
        out_ref[:, pl.ds(pl.multiple_of(q * 8, 8), 8), :] = jnp.swapaxes(res, 0, 1)
        copy(q).start()
        return carry

    lax.fori_loop(0, depth // 8, step, 0)

    def finish(q, carry):
        copy(q).wait()
        return carry

    lax.fori_loop(0, depth // 8, finish, 0)


def final_kernel(
    p_ref, ra_ref, rb_ref, sa_ref, sb_ref, so_ref, a_ref, gate_ref, f_hbm, c_ref, v_ref, vel_ref, f_ref, sem, *halos
):
    nx, ny, nz = p_ref.shape[1:]
    nxc, nyc = nx // 2, ny // 2
    sort_halos(ra_ref, rb_ref, sa_ref, sb_ref, *halos)

    def copy(xc):
        at = pl.ds(2 * xc, 2)
        return pltpu.make_async_copy(f_ref.at[:, at], f_hbm.at[:, at], sem.at[xc])

    def finish(xc, carry):
        copy(xc).wait()
        return carry

    def step(xc, carry):
        total = [None] * 3
        for t in range(2):
            x = 2 * xc + t
            f = streamed(x, nx, p_ref, *halos)
            for i in range(NVEL):
                f_ref[i, x] = f[i]
            _, u = moments(f)
            fluid = (so_ref[x] == 0).astype(F32)
            for k in range(3):
                part = u[k] * fluid
                total[k] = part if t == 0 else total[k] + part
        for k in range(3):
            at = pl.multiple_of((k * nxc + xc) * ny, ny)
            for t in range(nz // 128):
                vel_ref[t, pl.ds(at, ny), :] = total[k][:, t * 128 : (t + 1) * 128]
        copy(xc).start()
        return carry

    lax.fori_loop(0, nxc, step, 0, unroll=UNROLL_F)
    depth = 3 * nxc * nyc
    pairs = []
    for t in range(nz // 128):
        half = vel_ref.at[t]
        pairs.append(half[pl.ds(0, depth, stride=2), :] + half[pl.ds(1, depth, stride=2), :])
    pairs = jnp.concatenate(pairs, axis=1)
    pick = (
        lax.broadcasted_iota(jnp.int32, (nz, nz // 2), 0) // 2
        == lax.broadcasted_iota(jnp.int32, (nz, nz // 2), 1)
    ).astype(F32)
    coarse = lax.dot_general(
        pairs, pick, (((1,), (0,)), ((), ())), precision=HIGHEST, preferred_element_type=F32
    )
    c_ref[...] = coarse * (SPEED_SCALE / 8.0)
    cols = a_ref.shape[1]

    def inner(r, acc):
        return acc + a_ref[r] * c_ref[pl.ds(r, 1), :]

    acc = lax.fori_loop(0, depth, inner, jnp.zeros((cols, 128), F32), unroll=8)
    dots = jnp.sum(acc, axis=1, keepdims=True)
    own = jnp.sum(c_ref[...] * c_ref[...])
    down = lax.broadcasted_iota(jnp.int32, (cols, 1), 0)
    dots = jnp.where(down == cols - 1, own, dots)
    across = lax.broadcasted_iota(jnp.int32, (cols, 128), 1)
    diag = jnp.where(across == lax.broadcasted_iota(jnp.int32, (cols, 128), 0), dots, 0.0)
    line = jnp.sum(diag, axis=0, keepdims=True)
    v_ref[...] = jnp.broadcast_to(line, v_ref.shape)
    lax.fori_loop(0, nxc, finish, 0)


def last_kernel(
    inv_rows,
    v_ref,
    li_ref,
    u_ref,
    s_ref,
    c_ref,
    basis_ref,
    snap_hbm,
    q_ref,
    uo_hbm,
    o_ref,
    uo_ref,
    snap_ref,
    tall_ref,
    row_ref,
    ins,
    sem,
):
    cols = li_ref.shape[0]
    known = cols - 1
    rank, depth = basis_ref.shape[:2]
    extra = snap_ref.shape[0]
    load = pltpu.make_async_copy(snap_hbm, snap_ref, ins.at[0])
    load.start()
    line = jnp.sum(v_ref[...], axis=0, keepdims=True)[:, :cols] * inv_rows
    across = lax.broadcasted_iota(jnp.int32, (1, cols), 1)
    norm = jnp.sum(jnp.where(across == known, line, 0.0), axis=1, keepdims=True)
    inverse = li_ref[...]
    coef = jnp.sum(inverse * jnp.where(across == known, 0.0, line), axis=1, keepdims=True)
    left = norm - jnp.sum(coef * coef, axis=0, keepdims=True)
    pivot = lax.rsqrt(left)
    col_id = lax.broadcasted_iota(jnp.int32, (cols, cols), 1)
    row_id = lax.broadcasted_iota(jnp.int32, (cols, cols), 0)
    edge = jnp.where(row_id == known, left * pivot, coef)
    uo_ref[...] = jnp.where(col_id == known, edge, u_ref[...])
    factor = pltpu.make_async_copy(uo_ref, uo_hbm, ins.at[1])
    factor.start()
    weight = jnp.sum(inverse * coef, axis=0, keepdims=True) * (-pivot)
    diag = jnp.where(row_id == col_id, weight, 0.0)
    tall_ref[...] = jnp.sum(diag, axis=1, keepdims=True) * s_ref[...]

    def step(q, carry):
        at = pl.ds(pl.multiple_of(q * 16, 16), 16)
        total = [c_ref[at, :] * pivot] + [None] * 3
        for k in range(rank + extra):
            value = basis_ref[k, at, :] if k < rank else snap_ref[k - rank, at, :]
            value = value * tall_ref[k : k + 1, :]
            total[k % 4] = value if total[k % 4] is None else total[k % 4] + value
        row_ref[at, :] = (total[0] + total[1]) + (total[2] + total[3])
        return carry

    load.wait()
    lax.fori_loop(0, depth // 16, step, 0)
    copy = pltpu.make_async_copy(row_ref, o_ref.at[known], sem)
    copy.start()
    factor.wait()
    copy.wait()


def in_hbm(value):
    return pltpu.with_memory_space_constraint(value, pltpu.HBM)


def in_vmem(value):
    return pltpu.with_memory_space_constraint(value, pltpu.VMEM)


def shape(dims, dtype=F32):
    return jax.ShapeDtypeStruct(dims, dtype)


def halo_x(ya, yb, post, gate):
    _, _, ny, nz = post.shape
    pack_call = pl.pallas_call(
        pack_kernel,
        out_shape=(shape((len(UP_X), ny, nz)), shape((len(DOWN_X), ny, nz))),
        in_specs=[VMEM] * 3 + [ANY],
        name="pack",
        compiler_params=params(4),
    )
    faces = pack_call(ya, yb, post, gate)
    return swap(faces, "gx")


def rounds():
    steps = []
    for axis in ROUND_AXES:
        bit = 1
        while bit < lax.axis_size(axis):
            steps.append((axis, bit))
            bit *= 2
    return steps


def exchange(value, steps, begin, end):
    for k in range(begin, end):
        axis, bit = steps[k]
        pairs = [(s, s ^ bit) for s in range(lax.axis_size(axis))]
        other = lax.ppermute(value, axis, pairs)
        value = value + other
    return value


def on_device(populations, relax_rate, solid_mask, singular_values, basis, snapshots):
    _, nx, ny, nz = populations.shape
    rank, extra = basis.shape[0], snapshots.shape[0]
    cols = rank + extra + 1
    tail = basis.shape[1:]
    depth = tail[0] * tail[1] * tail[2]
    n_dev = lax.axis_size("gx") * lax.axis_size("gy")
    inv_rows = 1.0 / (depth * tail[3] * n_dev)
    edges = len(UP_Y) * nx
    post_shapes = (shape((NVEL, nx, ny, nz)), shape((edges, nz)), shape((edges, nz)))
    edge_rows = [pltpu.VMEM((edges, nz), F32)] * 2
    halos = [pltpu.VMEM((len(UP_X), ny, nz), F32)] * 2 + edge_rows
    post, ya, yb, omega, solid = pl.pallas_call(
        first_kernel,
        out_shape=post_shapes + (shape((nx, ny, nz)), shape((nx, ny, nz), jnp.int32)),
        in_specs=[HBM] * 3,
        scratch_shapes=[pltpu.VMEM((NVEL, nx, ny, nz), F32)]
        + edge_rows
        + [pltpu.SemaphoreType.DMA((6,))],
        name="first",
        compiler_params=params(6),
    )(*[in_hbm(value) for value in (populations, relax_rate, solid_mask)])
    ya, yb = swap((ya, yb), "gy")
    weights = in_hbm(singular_values.reshape(1, rank))
    modes = in_hbm(basis.reshape(rank, depth, 128))
    earlier = in_hbm(snapshots.reshape(extra, depth, 128))
    blocks = depth // 8
    rows, halves, gram, scale = pl.pallas_call(
        gram_kernel,
        out_shape=(
            shape((depth, cols, 128)),
            pltpu.HBM((2 * cols, depth * 128), BF16),
            shape((cols, cols)),
            shape((cols, 128)),
        ),
        in_specs=[HBM, HBM, HBM, ANY],
        out_specs=(VMEM, HBM, VMEM, VMEM),
        scratch_shapes=[
            pltpu.VMEM((1, rank), F32),
            pltpu.VMEM((rank, depth, 128), F32),
            pltpu.VMEM((extra, depth, 128), F32),
            pltpu.VMEM((2 * cols, depth * 128), BF16),
            pltpu.SemaphoreType.DMA((2, blocks)),
            pltpu.SemaphoreType.DMA((blocks + 1,)),
        ],
        name="gram",
        compiler_params=params(12),
    )(weights, modes, earlier, omega)
    xa, xb = halo_x(ya, yb, post, gram)
    steps = rounds()
    first, second, third = cuts(len(steps))
    gram = exchange(gram, steps, 0, first)
    second_call = pl.pallas_call(
        second_kernel,
        out_shape=post_shapes,
        in_specs=[VMEM] * 7 + [ANY],
        scratch_shapes=edge_rows + halos,
        name="second",
        compiler_params=params(4),
    )
    post, ya, yb = second_call(post, xa, xb, ya, yb, omega, solid, gram)
    ya, yb = swap((ya, yb), "gy")
    gram = exchange(gram, steps, first, second)
    xa, xb = halo_x(ya, yb, post, gram)
    gram = exchange(gram, steps, second, third)
    final_call = pl.pallas_call(
        final_kernel,
        out_shape=(shape((NVEL, nx, ny, nz)), shape((depth, 128)), pltpu.VMEM((n_dev, 128), F32)),
        in_specs=[VMEM] * 7 + [ANY],
        out_specs=(ANY, VMEM, VMEM),
        scratch_shapes=[
            pltpu.VMEM((nz // 128, 3 * (nx // 2) * ny, 128), F32),
            pltpu.VMEM((NVEL, nx, ny, nz), F32),
            pltpu.SemaphoreType.DMA((nx // 2,)),
        ]
        + halos,
        name="final",
        compiler_params=params(6),
    )
    field, coarse, line = final_call(post, xa, xb, ya, yb, solid, rows, gram)
    lines = lax.all_to_all(line, ("gx", "gy"), 0, 0, tiled=True)
    gram = exchange(gram, steps, third, len(steps))
    upper, inverse, split = pl.pallas_call(
        lambda *refs: factor_kernel(inv_rows, *refs),
        out_shape=(shape((cols, cols)), shape((cols, cols)), shape((cols, 3 * cols))),
        name="factor",
        compiler_params=params(4),
    )(gram)
    rotated = pl.pallas_call(
        rotate_kernel,
        out_shape=shape((cols, depth, 128)),
        in_specs=[VMEM, HBM],
        out_specs=ANY,
        scratch_shapes=[
            pltpu.VMEM((2 * cols, depth * 128), BF16),
            pltpu.VMEM((cols, depth, 128), F32),
            pltpu.SemaphoreType.DMA((blocks,)),
            pltpu.SemaphoreType.DMA((blocks,)),
        ],
        name="rotate",
        compiler_params=params(12),
    )(split, in_hbm(halves))
    upper, rotated = pl.pallas_call(
        lambda *refs: last_kernel(inv_rows, *refs),
        out_shape=(shape((cols, cols)), shape((cols, depth, 128))),
        in_specs=[VMEM] * 6 + [HBM, ANY],
        out_specs=(ANY, ANY),
        scratch_shapes=[
            pltpu.VMEM((cols, cols), F32),
            pltpu.VMEM((extra, depth, 128), F32),
            pltpu.VMEM((cols, 128), F32),
            pltpu.VMEM((depth, 128), F32),
            pltpu.SemaphoreType.DMA((2,)),
            pltpu.SemaphoreType.DMA,
        ],
        input_output_aliases={7: 1},
        name="last",
        compiler_params=params(2),
    )(lines, inverse, upper, scale, coarse, in_vmem(basis.reshape(rank, depth, 128)), earlier, rotated)
    return field, upper, rotated.reshape((cols,) + tail)


def solution(mesh):
    return jax.shard_map(
        on_device,
        mesh=mesh,
        in_specs=(
            P(None, "gx", "gy", None),
            P("gx", "gy", None),
            P("gx", "gy", None),
            P(),
            P(None, None, "gx", "gy", None),
            P(None, None, "gx", "gy", None),
        ),
        out_specs=(P(None, "gx", "gy", None), P(), P(None, None, "gx", "gy", None)),
        check_vma=False,
    )
```

```python
import jax
import jax.numpy as jnp
from jax import lax
from jax.experimental import pallas as pl
from jax.experimental.pallas import tpu as pltpu
from jax.sharding import PartitionSpec as P


velocity_table = [
    (0, 0, 0),
    (1, 0, 0),
    (-1, 0, 0),
    (0, 1, 0),
    (0, -1, 0),
    (0, 0, 1),
    (0, 0, -1),
    (1, 1, 0),
    (-1, -1, 0),
    (1, -1, 0),
    (-1, 1, 0),
    (1, 0, 1),
    (-1, 0, -1),
    (1, 0, -1),
    (-1, 0, 1),
    (0, 1, 1),
    (0, -1, -1),
    (0, 1, -1),
    (0, -1, 1),
]
NVEL = 19
PAIRS = [(i, i + 1) for i in range(1, NVEL, 2)]
W_REST, W_FACE, W_EDGE = 1.0 / 3.0, 1.0 / 18.0, 1.0 / 36.0
UP_X = [i for i in range(NVEL) if velocity_table[i][0] == 1]
DOWN_X = [i for i in range(NVEL) if velocity_table[i][0] == -1]
UP_Y = [i for i in range(NVEL) if velocity_table[i][1] == 1]
DOWN_Y = [i for i in range(NVEL) if velocity_table[i][1] == -1]
SPEED_SCALE = 10.0
UNROLL = 4
CUTS = (1, 3, 4)


def cuts(count):
    return tuple(count * cut // 5 for cut in CUTS)


UNROLL_F = 1
HIGHEST = lax.Precision.HIGHEST
F32 = jnp.float32
BF16 = jnp.bfloat16
VMEM = pl.BlockSpec(memory_space=pltpu.VMEM)
ANY = pl.BlockSpec(memory_space=pl.ANY)
HBM = pl.BlockSpec(memory_space=pltpu.HBM)


def params(mib=40):
    return pltpu.CompilerParams(vmem_limit_bytes=mib << 20)


def ring_pairs(axis):
    count = lax.axis_size(axis)
    partner = [(s, s ^ 1) for s in range(count)]
    other = [(s, (s + 1 if s % 2 else s - 1) % count) for s in range(count)]
    return partner, other


def swap(values, axis):
    partner, other = ring_pairs(axis)
    return lax.ppermute(values[0], axis, partner), lax.ppermute(values[1], axis, other)


def by_parity(axis, place):
    odd = lax.rem(lax.axis_index(axis), 2)

    @pl.when(odd == 0)
    def _():
        place(0)

    @pl.when(odd == 1)
    def _():
        place(1)


def moments(f):
    plus = [f[a] + f[b] for a, b in PAIRS]
    minus = [f[a] - f[b] for a, b in PAIRS]
    rho = f[0] + plus[0]
    for p in plus[1:]:
        rho = rho + p
    mx, my, mz, m7, m9, m11, m13, m15, m17 = minus
    jx = (mx + m7) + (m9 + m11) + m13
    jy = (my + m7) + (m15 + m17) - m9
    jz = (mz + m11) + (m15 - m13) - m17
    r = 1.0 / rho
    return rho, (jx * r, jy * r, jz * r)


def collide(f, omega, solid):
    rho, u = moments(f)
    base = 1.0 - 1.5 * (u[0] * u[0] + u[1] * u[1] + u[2] * u[2])
    keep = 1.0 - omega
    wr = omega * rho
    post = [None] * NVEL
    post[0] = jnp.where(solid, f[0], keep * f[0] + (W_REST * wr) * base)
    w_face, w_edge = W_FACE * wr, W_EDGE * wr
    for a, b in PAIRS:
        vel = velocity_table[a]
        along = None
        for axis in range(3):
            if vel[axis] == 1:
                along = u[axis] if along is None else along + u[axis]
            elif vel[axis] == -1:
                along = along - u[axis]
        w = w_face if a < 7 else w_edge
        even = w * (base + 4.5 * (along * along))
        odd = w * (3.0 * along)
        post[a] = jnp.where(solid, f[b], keep * f[a] + (even + odd))
        post[b] = jnp.where(solid, f[a], keep * f[b] + (even - odd))
    return post


def emit_post(post, x, nx, post_ref, yup_ref, ydn_ref):
    ny = post_ref.shape[2]
    for i in range(NVEL):
        cz = velocity_table[i][2]
        value = post[i] if cz == 0 else pltpu.roll(post[i], cz % post[i].shape[1], 1)
        post_ref[i, x] = value
        if i in UP_Y:
            yup_ref[pl.ds(UP_Y.index(i) * nx + x, 1), :] = value[ny - 1 : ny, :]
        if i in DOWN_Y:
            ydn_ref[pl.ds(DOWN_Y.index(i) * nx + x, 1), :] = value[0:1, :]


def emit_edges(yup_ref, ydn_ref, edges):
    def place(odd):
        edges[odd][...] = yup_ref[...]
        edges[1 - odd][...] = ydn_ref[...]

    by_parity("gy", place)


def sort_halos(xa_ref, xb_ref, ya_ref, yb_ref, xup_ref, xdn_ref, yup_ref, ydn_ref):
    def place_x(odd):
        xup_ref[...] = (xb_ref, xa_ref)[odd][...]
        xdn_ref[...] = (xa_ref, xb_ref)[odd][...]

    def place_y(odd):
        yup_ref[...] = (yb_ref, ya_ref)[odd][...]
        ydn_ref[...] = (ya_ref, yb_ref)[odd][...]

    by_parity("gx", place_x)
    by_parity("gy", place_y)


def first_kernel(
    f_hbm, om_hbm, so_hbm, post_ref, ya_ref, yb_ref, om_ref, so_ref, f_ref, yup_ref, ydn_ref, sem
):
    nx = f_ref.shape[1]
    parts = sem.shape[0] - 2
    rows = nx // parts

    def load(k):
        at = pl.ds(k * rows, rows)
        return pltpu.make_async_copy(f_hbm.at[:, at], f_ref.at[:, at], sem.at[k])

    loads = [load(k) for k in range(parts)]
    omega = pltpu.make_async_copy(om_hbm, om_ref, sem.at[parts])
    solid = pltpu.make_async_copy(so_hbm, so_ref, sem.at[parts + 1])
    omega.start()
    solid.start()
    for k in range(parts):
        loads[k].start()

    def step(x, carry):
        post = collide([f_ref[i, x] for i in range(NVEL)], om_ref[x], so_ref[x] > 0)
        emit_post(post, x, nx, post_ref, yup_ref, ydn_ref)
        return carry

    for k in range(parts):
        loads[k].wait()
        if k == 0:
            omega.wait()
            solid.wait()
        lax.fori_loop(k * rows, (k + 1) * rows, step, 0, unroll=UNROLL)
    emit_edges(yup_ref, ydn_ref, (ya_ref, yb_ref))


def shift_y(i, value, src, nx, yup_ref, ydn_ref):
    ny = value.shape[0]
    cy = velocity_table[i][1]
    if cy == 0:
        return value
    row_id = lax.broadcasted_iota(jnp.int32, value.shape, 0)
    if cy == 1:
        edge = yup_ref[pl.ds(UP_Y.index(i) * nx + src, 1), :]
        return jnp.where(row_id == 0, edge, pltpu.roll(value, 1, 0))
    edge = ydn_ref[pl.ds(DOWN_Y.index(i) * nx + src, 1), :]
    return jnp.where(row_id == ny - 1, edge, pltpu.roll(value, ny - 1, 0))


def streamed(x, nx, post_ref, xup_ref, xdn_ref, yup_ref, ydn_ref):
    f = []
    for i in range(NVEL):
        cx = velocity_table[i][0]
        src = x if cx == 0 else lax.rem(x + (nx - cx), nx)
        value = shift_y(i, post_ref[i, src], src, nx, yup_ref, ydn_ref)
        if cx == 1:
            value = jnp.where(x == 0, xup_ref[UP_X.index(i)], value)
        elif cx == -1:
            value = jnp.where(x == nx - 1, xdn_ref[DOWN_X.index(i)], value)
        f.append(value)
    return f


def second_kernel(
    p_ref,
    ra_ref,
    rb_ref,
    sa_ref,
    sb_ref,
    om_ref,
    so_ref,
    gate_ref,
    post_ref,
    ya_ref,
    yb_ref,
    yup_ref,
    ydn_ref,
    *halos,
):
    nx = p_ref.shape[1]
    sort_halos(ra_ref, rb_ref, sa_ref, sb_ref, *halos)

    def step(x, carry):
        f = streamed(x, nx, p_ref, *halos)
        post = collide(f, om_ref[x], so_ref[x] > 0)
        emit_post(post, x, nx, post_ref, yup_ref, ydn_ref)
        return carry

    lax.fori_loop(0, nx, step, 0, unroll=UNROLL)
    emit_edges(yup_ref, ydn_ref, (ya_ref, yb_ref))


def pack_kernel(ya_ref, yb_ref, post_ref, gate_ref, xa_ref, xb_ref):
    nx = post_ref.shape[1]

    def place(odd_y):
        yup_ref, ydn_ref = ((yb_ref, ya_ref), (ya_ref, yb_ref))[odd_y]

        def faces(odd_x):
            up_ref, down_ref = ((xa_ref, xb_ref), (xb_ref, xa_ref))[odd_x]
            for k, i in enumerate(UP_X):
                up_ref[k] = shift_y(i, post_ref[i, nx - 1], nx - 1, nx, yup_ref, ydn_ref)
            for k, i in enumerate(DOWN_X):
                down_ref[k] = shift_y(i, post_ref[i, 0], 0, nx, yup_ref, ydn_ref)

        by_parity("gx", faces)

    by_parity("gy", place)


def gram_kernel(
    s_hbm, basis_hbm, snap_hbm, gate_ref, a_ref, h_hbm, g_ref, t_ref, s_ref, basis_ref, snap_ref, h_ref, ins, outs
):
    rank = basis_ref.shape[0]
    depth = basis_ref.shape[1]
    extra = snap_ref.shape[0]
    cols = a_ref.shape[1]
    weights = pltpu.make_async_copy(s_hbm, s_ref, outs.at[depth // 8])
    weights.start()
    zero = jnp.zeros((cols - rank - extra, 8, 128), F32)

    def load(q):
        at = pl.ds(pl.multiple_of(q * 8, 8), 8)
        return (
            pltpu.make_async_copy(basis_hbm.at[:, at], basis_ref.at[:, at], ins.at[0, q]),
            pltpu.make_async_copy(snap_hbm.at[:, at], snap_ref.at[:, at], ins.at[1, q]),
        )

    def save(q):
        at = pl.ds(pl.multiple_of(q * 1024, 1024), 1024)
        return pltpu.make_async_copy(h_ref.at[:, at], h_hbm.at[:, at], outs.at[q])

    def begin(q, carry):
        for copy in load(q):
            copy.start()
        return carry

    def finish(q, carry):
        save(q).wait()
        return carry

    lax.fori_loop(0, depth // 8, begin, 0)
    weights.wait()
    same = lax.broadcasted_iota(jnp.int32, (rank, rank), 0) == lax.broadcasted_iota(
        jnp.int32, (rank, rank), 1
    )
    scale = jnp.sum(jnp.where(same, s_ref[...], 0.0), axis=1, keepdims=True)
    scale = jnp.broadcast_to(scale, (rank, 128))
    t_ref[...] = jnp.concatenate([scale, jnp.ones((cols - rank, 128), F32)], axis=0)

    def step(q, carry):
        for copy in load(q):
            copy.wait()
        r = pl.multiple_of(q * 8, 8)
        top = jnp.swapaxes(basis_ref[:, pl.ds(r, 8), :], 0, 1)
        low = jnp.concatenate([snap_ref[:, pl.ds(r, 8), :], zero], axis=0)
        low = jnp.swapaxes(low, 0, 1)
        for t in range(8):
            rows = jnp.concatenate([top[t] * scale, low[t]], axis=0)
            a_ref[r + t] = rows
            at = pl.ds(pl.multiple_of((r + t) * 128, 128), 128)
            high = rows.astype(BF16)
            h_ref[0:cols, at] = high
            h_ref[cols : 2 * cols, at] = (rows - high.astype(F32)).astype(BF16)
        save(q).start()
        return carry

    lax.fori_loop(0, depth // 8, step, 0)
    acc = lax.dot_general(
        h_ref[...], h_ref[0:cols, :], (((1,), (1,)), ((), ())), preferred_element_type=F32
    )
    cross = acc[cols:, :]
    eye = (
        lax.broadcasted_iota(jnp.int32, (cols, cols), 0)
        == lax.broadcasted_iota(jnp.int32, (cols, cols), 1)
    ).astype(F32)
    flipped = lax.dot_general(
        eye, cross, (((1,), (1,)), ((), ())), precision=HIGHEST, preferred_element_type=F32
    )
    g_ref[...] = acc[:cols, :] + cross + flipped
    lax.fori_loop(0, depth // 8, finish, 0)


def factor_kernel(inv_rows, g_ref, u_ref, li_ref, w_ref):
    cols = g_ref.shape[0]
    known = cols - 1
    blocks = cols // 8
    pad = jnp.zeros((8, 128 - cols), F32)
    sub = lax.broadcasted_iota(jnp.int32, (8, 128), 0)
    lane = lax.broadcasted_iota(jnp.int32, (8, 128), 1)
    left = [
        jnp.concatenate([g_ref[8 * b : 8 * b + 8, :] * inv_rows, pad], axis=1) for b in range(blocks)
    ]
    right = [(sub + 8 * b == lane).astype(F32) for b in range(blocks)]
    for p in range(blocks):
        live = range(p, blocks)
        width = min(8, known - 8 * p)
        col = [
            {
                b: jnp.broadcast_to(left[b][:, 8 * p + t : 8 * p + t + 1], (8, 128))
                for b in live
            }
            for t in range(width)
        ]
        for t in range(width):
            pivot = lax.rsqrt(jnp.broadcast_to(col[t][p][t : t + 1, :], (8, 128)))
            lcol = {b: col[t][b] * pivot for b in live}
            lcol[p] = jnp.where(sub > t, lcol[p], 0.0)
            for v in range(t + 1, width):
                m = jnp.broadcast_to(lcol[p][v : v + 1, :], (8, 128))
                for b in live:
                    col[v][b] = col[v][b] - lcol[b] * m
            top = jnp.broadcast_to(left[p][t : t + 1, :], (8, 128)) * pivot
            aug = jnp.broadcast_to(right[p][t : t + 1, :], (8, 128)) * pivot
            for b in live:
                left[b] = left[b] - lcol[b] * top
                right[b] = right[b] - lcol[b] * aug
            left[p] = jnp.where(sub == t, top, left[p])
            right[p] = jnp.where(sub == t, aug, right[p])
    fill = jnp.zeros((8, 128), F32)
    for b in range(blocks):
        row = sub + 8 * b
        upper = jnp.where(jnp.logical_and(row <= lane, lane < known), left[b], 0.0)
        inverse = jnp.where(jnp.logical_and(row >= lane, row < known), right[b], 0.0)
        u_ref[8 * b : 8 * b + 8, :] = upper[:, :cols]
        li_ref[8 * b : 8 * b + 8, :] = inverse[:, :cols]
        high = inverse.astype(BF16).astype(F32)
        wide = jnp.concatenate([high, fill], axis=1)
        rest = jnp.concatenate([inverse - high, fill], axis=1)
        wide = wide + pltpu.roll(rest, cols, 1) + pltpu.roll(wide, 2 * cols, 1)
        w_ref[8 * b : 8 * b + 8, :] = wide[:, : 3 * cols]


def rotate_kernel(w_ref, h_hbm, o_ref, h_ref, out_ref, ins, sem):
    cols = w_ref.shape[0]
    depth = out_ref.shape[1]
    weight = w_ref[...].astype(BF16)

    def copy(q):
        at = pl.ds(pl.multiple_of(q * 16, 16), 16)
        return pltpu.make_async_copy(out_ref.at[:, at, :], o_ref.at[:, at, :], sem.at[q])

    def load(q):
        at = pl.ds(pl.multiple_of(q * 2048, 2048), 2048)
        return pltpu.make_async_copy(h_hbm.at[:, at], h_ref.at[:, at], ins.at[q])

    def begin(q, carry):
        load(q).start()
        return carry

    lax.fori_loop(0, depth // 16, begin, 0)

    def step(q, carry):
        load(q).wait()
        at = pl.ds(pl.multiple_of(q * 2048, 2048), 2048)
        high = h_ref[0:cols, at]
        low = h_ref[cols : 2 * cols, at]
        res = lax.dot_general(
            weight,
            jnp.concatenate([high, high, low], axis=0),
            (((1,), (0,)), ((), ())),
            preferred_element_type=F32,
        )
        res = jnp.stack([res[:, t * 128 : (t + 1) * 128] for t in range(16)], axis=0)
        out_ref[:, pl.ds(pl.multiple_of(q * 16, 16), 16), :] = jnp.swapaxes(res, 0, 1)
        copy(q).start()
        return carry

    lax.fori_loop(0, depth // 16, step, 0)

    def finish(q, carry):
        copy(q).wait()
        return carry

    lax.fori_loop(0, depth // 16, finish, 0)


def final_kernel(
    p_ref, ra_ref, rb_ref, sa_ref, sb_ref, so_ref, a_ref, gate_ref, f_hbm, c_ref, v_hbm, vel_ref, f_ref, v_ref, sem, *halos
):
    nx, ny, nz = p_ref.shape[1:]
    nxc, nyc = nx // 2, ny // 2
    sort_halos(ra_ref, rb_ref, sa_ref, sb_ref, *halos)

    def copy(xc):
        at = pl.ds(2 * xc, 2)
        return pltpu.make_async_copy(f_ref.at[:, at], f_hbm.at[:, at], sem.at[xc])

    def finish(xc, carry):
        copy(xc).wait()
        return carry

    def step(xc, carry):
        total = [None] * 3
        for t in range(2):
            x = 2 * xc + t
            f = streamed(x, nx, p_ref, *halos)
            for i in range(NVEL):
                f_ref[i, x] = f[i]
            _, u = moments(f)
            fluid = (so_ref[x] == 0).astype(F32)
            for k in range(3):
                part = u[k] * fluid
                total[k] = part if t == 0 else total[k] + part
        for k in range(3):
            at = pl.multiple_of((k * nxc + xc) * ny, ny)
            for t in range(nz // 128):
                vel_ref[t, pl.ds(at, ny), :] = total[k][:, t * 128 : (t + 1) * 128]
        copy(xc).start()
        return carry

    lax.fori_loop(0, nxc, step, 0, unroll=UNROLL_F)
    depth = 3 * nxc * nyc
    pairs = []
    for t in range(nz // 128):
        half = vel_ref.at[t]
        pairs.append(half[pl.ds(0, depth, stride=2), :] + half[pl.ds(1, depth, stride=2), :])
    pairs = jnp.concatenate(pairs, axis=1)
    pick = (
        lax.broadcasted_iota(jnp.int32, (nz, nz // 2), 0) // 2
        == lax.broadcasted_iota(jnp.int32, (nz, nz // 2), 1)
    ).astype(F32)
    coarse = lax.dot_general(
        pairs, pick, (((1,), (0,)), ((), ())), precision=HIGHEST, preferred_element_type=F32
    )
    c_ref[...] = coarse * (SPEED_SCALE / 8.0)
    cols = a_ref.shape[1]

    def inner(r, acc):
        return acc + a_ref[r] * c_ref[pl.ds(r, 1), :]

    acc = lax.fori_loop(0, depth, inner, jnp.zeros((cols, 128), F32), unroll=8)
    dots = jnp.sum(acc, axis=1, keepdims=True)
    own = jnp.sum(c_ref[...] * c_ref[...])
    down = lax.broadcasted_iota(jnp.int32, (cols, 1), 0)
    dots = jnp.where(down == cols - 1, own, dots)
    across = lax.broadcasted_iota(jnp.int32, (cols, 128), 1)
    diag = jnp.where(across == lax.broadcasted_iota(jnp.int32, (cols, 128), 0), dots, 0.0)
    line = jnp.sum(diag, axis=0, keepdims=True)
    v_ref[...] = jnp.broadcast_to(line, v_ref.shape)
    send = pltpu.make_async_copy(v_ref, v_hbm, sem.at[nxc])
    send.start()
    lax.fori_loop(0, nxc, finish, 0)
    send.wait()


def last_kernel(
    inv_rows,
    v_ref,
    li_ref,
    u_ref,
    s_ref,
    c_ref,
    basis_ref,
    snap_hbm,
    q_ref,
    uo_hbm,
    o_ref,
    uo_ref,
    snap_ref,
    tall_ref,
    row_ref,
    ins,
    sem,
):
    cols = li_ref.shape[0]
    known = cols - 1
    rank, depth = basis_ref.shape[:2]
    extra = snap_ref.shape[0]
    parts = ins.shape[0] - 1
    size = extra // parts
    loads = []
    for k in range(parts):
        at = pl.ds(k * size, size if k < parts - 1 else extra - k * size)
        loads.append(pltpu.make_async_copy(snap_hbm.at[at], snap_ref.at[at], ins.at[k]))
        loads[k].start()
    line = jnp.sum(v_ref[...], axis=0, keepdims=True)[:, :cols] * inv_rows
    across = lax.broadcasted_iota(jnp.int32, (1, cols), 1)
    norm = jnp.sum(jnp.where(across == known, line, 0.0), axis=1, keepdims=True)
    inverse = li_ref[...]
    coef = jnp.sum(inverse * jnp.where(across == known, 0.0, line), axis=1, keepdims=True)
    left = norm - jnp.sum(coef * coef, axis=0, keepdims=True)
    pivot = lax.rsqrt(left)
    col_id = lax.broadcasted_iota(jnp.int32, (cols, cols), 1)
    row_id = lax.broadcasted_iota(jnp.int32, (cols, cols), 0)
    edge = jnp.where(row_id == known, left * pivot, coef)
    uo_ref[...] = jnp.where(col_id == known, edge, u_ref[...])
    factor = pltpu.make_async_copy(uo_ref, uo_hbm, ins.at[parts])
    factor.start()
    weight = jnp.sum(inverse * coef, axis=0, keepdims=True) * (-pivot)
    diag = jnp.where(row_id == col_id, weight, 0.0)
    tall_ref[...] = jnp.sum(diag, axis=1, keepdims=True) * s_ref[...]

    def weighted(source, first, count, total, at):
        for k in range(count):
            value = source[k, at, :] * tall_ref[first + k : first + k + 1, :]
            total[k % 4] = value if total[k % 4] is None else total[k % 4] + value
        return (total[0] + total[1]) + (total[2] + total[3])

    def begin(q, carry):
        at = pl.ds(pl.multiple_of(q * 16, 16), 16)
        row_ref[at, :] = weighted(basis_ref, 0, rank, [c_ref[at, :] * pivot] + [None] * 3, at)
        return carry

    def finish(q, carry):
        at = pl.ds(pl.multiple_of(q * 16, 16), 16)
        row_ref[at, :] = weighted(snap_ref, rank, extra, [row_ref[at, :]] + [None] * 3, at)
        return carry

    lax.fori_loop(0, depth // 16, begin, 0)
    for load in loads:
        load.wait()
    lax.fori_loop(0, depth // 16, finish, 0)
    copy = pltpu.make_async_copy(row_ref, o_ref.at[known], sem)
    copy.start()
    factor.wait()
    copy.wait()


def in_hbm(value):
    return pltpu.with_memory_space_constraint(value, pltpu.HBM)


def in_vmem(value):
    return pltpu.with_memory_space_constraint(value, pltpu.VMEM)


def shape(dims, dtype=F32):
    return jax.ShapeDtypeStruct(dims, dtype)


def halo_x(ya, yb, post, gate):
    _, _, ny, nz = post.shape
    pack_call = pl.pallas_call(
        pack_kernel,
        out_shape=(shape((len(UP_X), ny, nz)), shape((len(DOWN_X), ny, nz))),
        in_specs=[VMEM] * 3 + [ANY],
        name="pack",
        compiler_params=params(4),
    )
    faces = pack_call(ya, yb, post, gate)
    return swap(faces, "gx")


def rounds():
    bits = {axis: [] for axis in ("gx", "gy")}
    for axis, steps in bits.items():
        bit = 1
        while bit < lax.axis_size(axis):
            steps.append((axis, bit))
            bit *= 2
    gx, gy = bits["gx"], bits["gy"]
    return gx[:1] + gy[:1] + gx[1:] + gy[1:]


def exchange(value, steps, begin, end):
    for k in range(begin, end):
        axis, bit = steps[k]
        pairs = [(s, s ^ bit) for s in range(lax.axis_size(axis))]
        other = lax.ppermute(value, axis, pairs)
        value = value + other
    return value


def on_device(populations, relax_rate, solid_mask, singular_values, basis, snapshots):
    _, nx, ny, nz = populations.shape
    rank, extra = basis.shape[0], snapshots.shape[0]
    cols = rank + extra + 1
    tail = basis.shape[1:]
    depth = tail[0] * tail[1] * tail[2]
    n_dev = lax.axis_size("gx") * lax.axis_size("gy")
    inv_rows = 1.0 / (depth * tail[3] * n_dev)
    edges = len(UP_Y) * nx
    post_shapes = (shape((NVEL, nx, ny, nz)), shape((edges, nz)), shape((edges, nz)))
    edge_rows = [pltpu.VMEM((edges, nz), F32)] * 2
    halos = [pltpu.VMEM((len(UP_X), ny, nz), F32)] * 2 + edge_rows
    post, ya, yb, omega, solid = pl.pallas_call(
        first_kernel,
        out_shape=post_shapes + (shape((nx, ny, nz)), shape((nx, ny, nz), jnp.int32)),
        in_specs=[HBM] * 3,
        scratch_shapes=[pltpu.VMEM((NVEL, nx, ny, nz), F32)]
        + edge_rows
        + [pltpu.SemaphoreType.DMA((6,))],
        name="first",
        compiler_params=params(6),
    )(*[in_hbm(value) for value in (populations, relax_rate, solid_mask)])
    ya, yb = swap((ya, yb), "gy")
    weights = in_hbm(singular_values.reshape(1, rank))
    modes = in_hbm(basis.reshape(rank, depth, 128))
    earlier = in_hbm(snapshots.reshape(extra, depth, 128))
    blocks = depth // 8
    rows, halves, gram, scale = pl.pallas_call(
        gram_kernel,
        out_shape=(
            shape((depth, cols, 128)),
            pltpu.HBM((2 * cols, depth * 128), BF16),
            shape((cols, cols)),
            shape((cols, 128)),
        ),
        in_specs=[HBM, HBM, HBM, ANY],
        out_specs=(VMEM, HBM, VMEM, VMEM),
        scratch_shapes=[
            pltpu.VMEM((1, rank), F32),
            pltpu.VMEM((rank, depth, 128), F32),
            pltpu.VMEM((extra, depth, 128), F32),
            pltpu.VMEM((2 * cols, depth * 128), BF16),
            pltpu.SemaphoreType.DMA((2, blocks)),
            pltpu.SemaphoreType.DMA((blocks + 1,)),
        ],
        name="gram",
        compiler_params=params(12),
    )(weights, modes, earlier, omega)
    xa, xb = halo_x(ya, yb, post, gram)
    steps = rounds()
    first, second, third = cuts(len(steps))
    gram = exchange(gram, steps, 0, first)
    second_call = pl.pallas_call(
        second_kernel,
        out_shape=post_shapes,
        in_specs=[VMEM] * 7 + [ANY],
        scratch_shapes=edge_rows + halos,
        name="second",
        compiler_params=params(4),
    )
    post, ya, yb = second_call(post, xa, xb, ya, yb, omega, solid, gram)
    ya, yb = swap((ya, yb), "gy")
    gram = exchange(gram, steps, first, second)
    xa, xb = halo_x(ya, yb, post, gram)
    gram = exchange(gram, steps, second, third)
    final_call = pl.pallas_call(
        final_kernel,
        out_shape=(shape((NVEL, nx, ny, nz)), shape((depth, 128)), shape((n_dev, 128))),
        in_specs=[VMEM] * 7 + [ANY],
        out_specs=(ANY, VMEM, ANY),
        scratch_shapes=[
            pltpu.VMEM((nz // 128, 3 * (nx // 2) * ny, 128), F32),
            pltpu.VMEM((NVEL, nx, ny, nz), F32),
            pltpu.VMEM((n_dev, 128), F32),
            pltpu.SemaphoreType.DMA((nx // 2 + 1,)),
        ]
        + halos,
        name="final",
        compiler_params=params(6),
    )
    field, coarse, line = final_call(post, xa, xb, ya, yb, solid, rows, gram)
    lines = lax.all_to_all(line, ("gx", "gy"), 0, 0, tiled=True)
    gram = exchange(gram, steps, third, len(steps))
    upper, inverse, split = pl.pallas_call(
        lambda *refs: factor_kernel(inv_rows, *refs),
        out_shape=(shape((cols, cols)), shape((cols, cols)), shape((cols, 3 * cols))),
        name="factor",
        compiler_params=params(4),
    )(gram)
    rotated = pl.pallas_call(
        rotate_kernel,
        out_shape=shape((cols, depth, 128)),
        in_specs=[VMEM, HBM],
        out_specs=ANY,
        scratch_shapes=[
            pltpu.VMEM((2 * cols, depth * 128), BF16),
            pltpu.VMEM((cols, depth, 128), F32),
            pltpu.SemaphoreType.DMA((blocks,)),
            pltpu.SemaphoreType.DMA((blocks,)),
        ],
        name="rotate",
        compiler_params=params(12),
    )(split, in_hbm(halves))
    upper, rotated = pl.pallas_call(
        lambda *refs: last_kernel(inv_rows, *refs),
        out_shape=(shape((cols, cols)), shape((cols, depth, 128))),
        in_specs=[VMEM] * 6 + [HBM, ANY],
        out_specs=(ANY, ANY),
        scratch_shapes=[
            pltpu.VMEM((cols, cols), F32),
            pltpu.VMEM((extra, depth, 128), F32),
            pltpu.VMEM((cols, 128), F32),
            pltpu.VMEM((depth, 128), F32),
            pltpu.SemaphoreType.DMA((2,)),
            pltpu.SemaphoreType.DMA,
        ],
        input_output_aliases={7: 1},
        name="last",
        compiler_params=params(2),
    )(lines, inverse, upper, scale, coarse, in_vmem(basis.reshape(rank, depth, 128)), earlier, rotated)
    return field, upper, rotated.reshape((cols,) + tail)


def solution(mesh):
    return jax.shard_map(
        on_device,
        mesh=mesh,
        in_specs=(
            P(None, "gx", "gy", None),
            P("gx", "gy", None),
            P("gx", "gy", None),
            P(),
            P(None, None, "gx", "gy", None),
            P(None, None, "gx", "gy", None),
        ),
        out_specs=(P(None, "gx", "gy", None), P(), P(None, None, "gx", "gy", None)),
        check_vma=False,
    )
```

```python
import jax
import jax.numpy as jnp
from jax import lax
from jax.experimental import pallas as pl
from jax.experimental.pallas import tpu as pltpu
from jax.sharding import PartitionSpec as P


velocity_table = [
    (0, 0, 0),
    (1, 0, 0),
    (-1, 0, 0),
    (0, 1, 0),
    (0, -1, 0),
    (0, 0, 1),
    (0, 0, -1),
    (1, 1, 0),
    (-1, -1, 0),
    (1, -1, 0),
    (-1, 1, 0),
    (1, 0, 1),
    (-1, 0, -1),
    (1, 0, -1),
    (-1, 0, 1),
    (0, 1, 1),
    (0, -1, -1),
    (0, 1, -1),
    (0, -1, 1),
]
NVEL = 19
PAIRS = [(i, i + 1) for i in range(1, NVEL, 2)]
W_REST, W_FACE, W_EDGE = 1.0 / 3.0, 1.0 / 18.0, 1.0 / 36.0
UP_X = [i for i in range(NVEL) if velocity_table[i][0] == 1]
DOWN_X = [i for i in range(NVEL) if velocity_table[i][0] == -1]
UP_Y = [i for i in range(NVEL) if velocity_table[i][1] == 1]
DOWN_Y = [i for i in range(NVEL) if velocity_table[i][1] == -1]
SPEED_SCALE = 10.0
UNROLL = 4
CUTS = (1, 3, 4)


def cuts(count):
    return tuple(count * cut // 5 for cut in CUTS)


UNROLL_F = 1
HIGHEST = lax.Precision.HIGHEST
F32 = jnp.float32
BF16 = jnp.bfloat16
VMEM = pl.BlockSpec(memory_space=pltpu.VMEM)
ANY = pl.BlockSpec(memory_space=pl.ANY)
HBM = pl.BlockSpec(memory_space=pltpu.HBM)


def params(mib=40):
    return pltpu.CompilerParams(vmem_limit_bytes=mib << 20)


def ring_pairs(axis):
    count = lax.axis_size(axis)
    partner = [(s, s ^ 1) for s in range(count)]
    other = [(s, (s + 1 if s % 2 else s - 1) % count) for s in range(count)]
    return partner, other


def swap(values, axis):
    partner, other = ring_pairs(axis)
    return lax.ppermute(values[0], axis, partner), lax.ppermute(values[1], axis, other)


def by_parity(axis, place):
    odd = lax.rem(lax.axis_index(axis), 2)

    @pl.when(odd == 0)
    def _():
        place(0)

    @pl.when(odd == 1)
    def _():
        place(1)


def moments(f):
    plus = [f[a] + f[b] for a, b in PAIRS]
    minus = [f[a] - f[b] for a, b in PAIRS]
    rho = f[0] + plus[0]
    for p in plus[1:]:
        rho = rho + p
    mx, my, mz, m7, m9, m11, m13, m15, m17 = minus
    jx = (mx + m7) + (m9 + m11) + m13
    jy = (my + m7) + (m15 + m17) - m9
    jz = (mz + m11) + (m15 - m13) - m17
    r = 1.0 / rho
    return rho, (jx * r, jy * r, jz * r)


def collide(f, omega, solid):
    rho, u = moments(f)
    base = 1.0 - 1.5 * (u[0] * u[0] + u[1] * u[1] + u[2] * u[2])
    keep = 1.0 - omega
    wr = omega * rho
    post = [None] * NVEL
    post[0] = jnp.where(solid, f[0], keep * f[0] + (W_REST * wr) * base)
    w_face, w_edge = W_FACE * wr, W_EDGE * wr
    for a, b in PAIRS:
        vel = velocity_table[a]
        along = None
        for axis in range(3):
            if vel[axis] == 1:
                along = u[axis] if along is None else along + u[axis]
            elif vel[axis] == -1:
                along = along - u[axis]
        w = w_face if a < 7 else w_edge
        even = w * (base + 4.5 * (along * along))
        odd = w * (3.0 * along)
        post[a] = jnp.where(solid, f[b], keep * f[a] + (even + odd))
        post[b] = jnp.where(solid, f[a], keep * f[b] + (even - odd))
    return post


def emit_post(post, x, nx, post_ref, yup_ref, ydn_ref):
    ny = post_ref.shape[2]
    for i in range(NVEL):
        cz = velocity_table[i][2]
        value = post[i] if cz == 0 else pltpu.roll(post[i], cz % post[i].shape[1], 1)
        post_ref[i, x] = value
        if i in UP_Y:
            yup_ref[pl.ds(UP_Y.index(i) * nx + x, 1), :] = value[ny - 1 : ny, :]
        if i in DOWN_Y:
            ydn_ref[pl.ds(DOWN_Y.index(i) * nx + x, 1), :] = value[0:1, :]


def emit_edges(yup_ref, ydn_ref, edges):
    def place(odd):
        edges[odd][...] = yup_ref[...]
        edges[1 - odd][...] = ydn_ref[...]

    by_parity("gy", place)


def sort_halos(xa_ref, xb_ref, ya_ref, yb_ref, xup_ref, xdn_ref, yup_ref, ydn_ref):
    def place_x(odd):
        xup_ref[...] = (xb_ref, xa_ref)[odd][...]
        xdn_ref[...] = (xa_ref, xb_ref)[odd][...]

    def place_y(odd):
        yup_ref[...] = (yb_ref, ya_ref)[odd][...]
        ydn_ref[...] = (ya_ref, yb_ref)[odd][...]

    by_parity("gx", place_x)
    by_parity("gy", place_y)


def first_kernel(
    f_hbm, om_hbm, so_hbm, post_ref, ya_ref, yb_ref, om_ref, so_ref, f_ref, yup_ref, ydn_ref, sem
):
    nx = f_ref.shape[1]
    parts = sem.shape[0] - 2
    rows = nx // parts

    def load(k):
        at = pl.ds(k * rows, rows)
        return pltpu.make_async_copy(f_hbm.at[:, at], f_ref.at[:, at], sem.at[k])

    loads = [load(k) for k in range(parts)]
    omega = pltpu.make_async_copy(om_hbm, om_ref, sem.at[parts])
    solid = pltpu.make_async_copy(so_hbm, so_ref, sem.at[parts + 1])
    omega.start()
    solid.start()
    for k in range(parts):
        loads[k].start()

    def step(x, carry):
        post = collide([f_ref[i, x] for i in range(NVEL)], om_ref[x], so_ref[x] > 0)
        emit_post(post, x, nx, post_ref, yup_ref, ydn_ref)
        return carry

    for k in range(parts):
        loads[k].wait()
        if k == 0:
            omega.wait()
            solid.wait()
        lax.fori_loop(k * rows, (k + 1) * rows, step, 0, unroll=UNROLL)
    emit_edges(yup_ref, ydn_ref, (ya_ref, yb_ref))


def shift_y(i, value, src, nx, yup_ref, ydn_ref):
    ny = value.shape[0]
    cy = velocity_table[i][1]
    if cy == 0:
        return value
    row_id = lax.broadcasted_iota(jnp.int32, value.shape, 0)
    if cy == 1:
        edge = yup_ref[pl.ds(UP_Y.index(i) * nx + src, 1), :]
        return jnp.where(row_id == 0, edge, pltpu.roll(value, 1, 0))
    edge = ydn_ref[pl.ds(DOWN_Y.index(i) * nx + src, 1), :]
    return jnp.where(row_id == ny - 1, edge, pltpu.roll(value, ny - 1, 0))


def streamed(x, nx, post_ref, xup_ref, xdn_ref, yup_ref, ydn_ref):
    f = []
    for i in range(NVEL):
        cx = velocity_table[i][0]
        src = x if cx == 0 else lax.rem(x + (nx - cx), nx)
        value = shift_y(i, post_ref[i, src], src, nx, yup_ref, ydn_ref)
        if cx == 1:
            value = jnp.where(x == 0, xup_ref[UP_X.index(i)], value)
        elif cx == -1:
            value = jnp.where(x == nx - 1, xdn_ref[DOWN_X.index(i)], value)
        f.append(value)
    return f


def second_kernel(
    p_ref,
    ra_ref,
    rb_ref,
    sa_ref,
    sb_ref,
    om_ref,
    so_ref,
    gate_ref,
    post_ref,
    ya_ref,
    yb_ref,
    yup_ref,
    ydn_ref,
    *halos,
):
    nx = p_ref.shape[1]
    sort_halos(ra_ref, rb_ref, sa_ref, sb_ref, *halos)

    def step(x, carry):
        f = streamed(x, nx, p_ref, *halos)
        post = collide(f, om_ref[x], so_ref[x] > 0)
        emit_post(post, x, nx, post_ref, yup_ref, ydn_ref)
        return carry

    lax.fori_loop(0, nx, step, 0, unroll=UNROLL)
    emit_edges(yup_ref, ydn_ref, (ya_ref, yb_ref))


def pack_kernel(ya_ref, yb_ref, post_ref, gate_ref, xa_ref, xb_ref):
    nx = post_ref.shape[1]

    def place(odd_y):
        yup_ref, ydn_ref = ((yb_ref, ya_ref), (ya_ref, yb_ref))[odd_y]

        def faces(odd_x):
            up_ref, down_ref = ((xa_ref, xb_ref), (xb_ref, xa_ref))[odd_x]
            for k, i in enumerate(UP_X):
                up_ref[k] = shift_y(i, post_ref[i, nx - 1], nx - 1, nx, yup_ref, ydn_ref)
            for k, i in enumerate(DOWN_X):
                down_ref[k] = shift_y(i, post_ref[i, 0], 0, nx, yup_ref, ydn_ref)

        by_parity("gx", faces)

    by_parity("gy", place)


def gram_kernel(
    s_hbm, basis_hbm, snap_hbm, gate_ref, a_ref, h_hbm, g_ref, t_ref, s_ref, basis_ref, snap_ref, h_ref, ins, outs
):
    rank = basis_ref.shape[0]
    depth = basis_ref.shape[1]
    extra = snap_ref.shape[0]
    cols = a_ref.shape[1]
    weights = pltpu.make_async_copy(s_hbm, s_ref, outs.at[depth // 8])
    weights.start()
    zero = jnp.zeros((cols - rank - extra, 8, 128), F32)

    def load(q):
        at = pl.ds(pl.multiple_of(q * 8, 8), 8)
        return (
            pltpu.make_async_copy(basis_hbm.at[:, at], basis_ref.at[:, at], ins.at[0, q]),
            pltpu.make_async_copy(snap_hbm.at[:, at], snap_ref.at[:, at], ins.at[1, q]),
        )

    def save(q):
        at = pl.ds(pl.multiple_of(q * 1024, 1024), 1024)
        return pltpu.make_async_copy(h_ref.at[:, at], h_hbm.at[:, at], outs.at[q])

    def begin(q, carry):
        for copy in load(q):
            copy.start()
        return carry

    def finish(q, carry):
        save(q).wait()
        return carry

    lax.fori_loop(0, depth // 8, begin, 0)
    weights.wait()
    same = lax.broadcasted_iota(jnp.int32, (rank, rank), 0) == lax.broadcasted_iota(
        jnp.int32, (rank, rank), 1
    )
    scale = jnp.sum(jnp.where(same, s_ref[...], 0.0), axis=1, keepdims=True)
    scale = jnp.broadcast_to(scale, (rank, 128))
    t_ref[...] = jnp.concatenate([scale, jnp.ones((cols - rank, 128), F32)], axis=0)

    def step(q, carry):
        for copy in load(q):
            copy.wait()
        r = pl.multiple_of(q * 8, 8)
        top = jnp.swapaxes(basis_ref[:, pl.ds(r, 8), :], 0, 1)
        low = jnp.concatenate([snap_ref[:, pl.ds(r, 8), :], zero], axis=0)
        low = jnp.swapaxes(low, 0, 1)
        for t in range(8):
            rows = jnp.concatenate([top[t] * scale, low[t]], axis=0)
            a_ref[r + t] = rows
            at = pl.ds(pl.multiple_of((r + t) * 128, 128), 128)
            high = rows.astype(BF16)
            h_ref[0:cols, at] = high
            h_ref[cols : 2 * cols, at] = (rows - high.astype(F32)).astype(BF16)
        save(q).start()
        return carry

    lax.fori_loop(0, depth // 8, step, 0)
    acc = lax.dot_general(
        h_ref[...], h_ref[0:cols, :], (((1,), (1,)), ((), ())), preferred_element_type=F32
    )
    cross = acc[cols:, :]
    eye = (
        lax.broadcasted_iota(jnp.int32, (cols, cols), 0)
        == lax.broadcasted_iota(jnp.int32, (cols, cols), 1)
    ).astype(F32)
    flipped = lax.dot_general(
        eye, cross, (((1,), (1,)), ((), ())), precision=HIGHEST, preferred_element_type=F32
    )
    total = acc[:cols, :] + cross + flipped
    half, width = g_ref.shape
    total = jnp.concatenate([total, jnp.zeros((cols, width - cols), F32)], axis=1)
    lane = lax.broadcasted_iota(jnp.int32, (half, width), 1)
    g_ref[...] = jnp.where(lane < cols, total[:half], pltpu.roll(total[half:], half, 1))
    lax.fori_loop(0, depth // 8, finish, 0)


def factor_kernel(inv_rows, g_ref, u_ref, li_ref, w_ref):
    half, width = g_ref.shape
    cols = 2 * half
    known = cols - 1
    blocks = cols // 8
    top = g_ref[...] * inv_rows
    pick = (
        lax.broadcasted_iota(jnp.int32, (half, width), 1)
        == lax.broadcasted_iota(jnp.int32, (half, width), 0) + half
    ).astype(F32)
    mirror = lax.dot_general(
        pick, top, (((1,), (1,)), ((), ())), precision=HIGHEST, preferred_element_type=F32
    )
    mirror = jnp.concatenate([mirror, jnp.zeros((half, width - half), F32)], axis=1)
    across = lax.broadcasted_iota(jnp.int32, (half, width), 1)
    bottom = jnp.where(across < half, mirror, pltpu.roll(top, width - half, 1))
    gram = jnp.concatenate([top, bottom], axis=0)
    sub = lax.broadcasted_iota(jnp.int32, (8, 128), 0)
    lane = lax.broadcasted_iota(jnp.int32, (8, 128), 1)
    left = [gram[8 * b : 8 * b + 8, :] for b in range(blocks)]
    right = [(sub + 8 * b == lane).astype(F32) for b in range(blocks)]
    for p in range(blocks):
        live = range(p, blocks)
        width = min(8, known - 8 * p)
        col = [
            {
                b: jnp.broadcast_to(left[b][:, 8 * p + t : 8 * p + t + 1], (8, 128))
                for b in live
            }
            for t in range(width)
        ]
        for t in range(width):
            pivot = lax.rsqrt(jnp.broadcast_to(col[t][p][t : t + 1, :], (8, 128)))
            lcol = {b: col[t][b] * pivot for b in live}
            lcol[p] = jnp.where(sub > t, lcol[p], 0.0)
            for v in range(t + 1, width):
                m = jnp.broadcast_to(lcol[p][v : v + 1, :], (8, 128))
                for b in live:
                    col[v][b] = col[v][b] - lcol[b] * m
            top = jnp.broadcast_to(left[p][t : t + 1, :], (8, 128)) * pivot
            aug = jnp.broadcast_to(right[p][t : t + 1, :], (8, 128)) * pivot
            for b in live:
                left[b] = left[b] - lcol[b] * top
                right[b] = right[b] - lcol[b] * aug
            left[p] = jnp.where(sub == t, top, left[p])
            right[p] = jnp.where(sub == t, aug, right[p])
    fill = jnp.zeros((8, 128), F32)
    for b in range(blocks):
        row = sub + 8 * b
        upper = jnp.where(jnp.logical_and(row <= lane, lane < known), left[b], 0.0)
        inverse = jnp.where(jnp.logical_and(row >= lane, row < known), right[b], 0.0)
        u_ref[8 * b : 8 * b + 8, :] = upper[:, :cols]
        li_ref[8 * b : 8 * b + 8, :] = inverse[:, :cols]
        high = inverse.astype(BF16).astype(F32)
        wide = jnp.concatenate([high, fill], axis=1)
        rest = jnp.concatenate([inverse - high, fill], axis=1)
        wide = wide + pltpu.roll(rest, cols, 1) + pltpu.roll(wide, 2 * cols, 1)
        w_ref[8 * b : 8 * b + 8, :] = wide[:, : 3 * cols]


def rotate_kernel(w_ref, h_hbm, o_ref, h_ref, out_ref, ins, sem):
    cols = w_ref.shape[0]
    depth = out_ref.shape[1]
    weight = w_ref[...].astype(BF16)

    def copy(q):
        at = pl.ds(pl.multiple_of(q * 16, 16), 16)
        return pltpu.make_async_copy(out_ref.at[:, at, :], o_ref.at[:, at, :], sem.at[q])

    def load(q):
        at = pl.ds(pl.multiple_of(q * 2048, 2048), 2048)
        return pltpu.make_async_copy(h_hbm.at[:, at], h_ref.at[:, at], ins.at[q])

    def begin(q, carry):
        load(q).start()
        return carry

    lax.fori_loop(0, depth // 16, begin, 0)

    def step(q, carry):
        load(q).wait()
        at = pl.ds(pl.multiple_of(q * 2048, 2048), 2048)
        high = h_ref[0:cols, at]
        low = h_ref[cols : 2 * cols, at]
        res = lax.dot_general(
            weight,
            jnp.concatenate([high, high, low], axis=0),
            (((1,), (0,)), ((), ())),
            preferred_element_type=F32,
        )
        res = jnp.stack([res[:, t * 128 : (t + 1) * 128] for t in range(16)], axis=0)
        out_ref[:, pl.ds(pl.multiple_of(q * 16, 16), 16), :] = jnp.swapaxes(res, 0, 1)
        copy(q).start()
        return carry

    lax.fori_loop(0, depth // 16, step, 0)

    def finish(q, carry):
        copy(q).wait()
        return carry

    lax.fori_loop(0, depth // 16, finish, 0)


def final_kernel(
    p_ref, ra_ref, rb_ref, sa_ref, sb_ref, so_ref, a_ref, gate_ref, f_hbm, c_ref, v_hbm, vel_ref, f_ref, v_ref, sem, *halos
):
    nx, ny, nz = p_ref.shape[1:]
    nxc, nyc = nx // 2, ny // 2
    sort_halos(ra_ref, rb_ref, sa_ref, sb_ref, *halos)

    def copy(xc):
        at = pl.ds(2 * xc, 2)
        return pltpu.make_async_copy(f_ref.at[:, at], f_hbm.at[:, at], sem.at[xc])

    def finish(xc, carry):
        copy(xc).wait()
        return carry

    def step(xc, carry):
        total = [None] * 3
        for t in range(2):
            x = 2 * xc + t
            f = streamed(x, nx, p_ref, *halos)
            for i in range(NVEL):
                f_ref[i, x] = f[i]
            _, u = moments(f)
            fluid = (so_ref[x] == 0).astype(F32)
            for k in range(3):
                part = u[k] * fluid
                total[k] = part if t == 0 else total[k] + part
        for k in range(3):
            at = pl.multiple_of((k * nxc + xc) * ny, ny)
            for t in range(nz // 128):
                vel_ref[t, pl.ds(at, ny), :] = total[k][:, t * 128 : (t + 1) * 128]
        copy(xc).start()
        return carry

    lax.fori_loop(0, nxc, step, 0, unroll=UNROLL_F)
    depth = 3 * nxc * nyc
    pairs = []
    for t in range(nz // 128):
        half = vel_ref.at[t]
        pairs.append(half[pl.ds(0, depth, stride=2), :] + half[pl.ds(1, depth, stride=2), :])
    pairs = jnp.concatenate(pairs, axis=1)
    pick = (
        lax.broadcasted_iota(jnp.int32, (nz, nz // 2), 0) // 2
        == lax.broadcasted_iota(jnp.int32, (nz, nz // 2), 1)
    ).astype(F32)
    coarse = lax.dot_general(
        pairs, pick, (((1,), (0,)), ((), ())), precision=HIGHEST, preferred_element_type=F32
    )
    c_ref[...] = coarse * (SPEED_SCALE / 8.0)
    cols = a_ref.shape[1]

    def inner(r, acc):
        return acc + a_ref[r] * c_ref[pl.ds(r, 1), :]

    acc = lax.fori_loop(0, depth, inner, jnp.zeros((cols, 128), F32), unroll=8)
    dots = jnp.sum(acc, axis=1, keepdims=True)
    own = jnp.sum(c_ref[...] * c_ref[...])
    down = lax.broadcasted_iota(jnp.int32, (cols, 1), 0)
    dots = jnp.where(down == cols - 1, own, dots)
    across = lax.broadcasted_iota(jnp.int32, (cols, 128), 1)
    diag = jnp.where(across == lax.broadcasted_iota(jnp.int32, (cols, 128), 0), dots, 0.0)
    line = jnp.sum(diag, axis=0, keepdims=True)
    v_ref[...] = jnp.broadcast_to(line, v_ref.shape)
    send = pltpu.make_async_copy(v_ref, v_hbm, sem.at[nxc])
    send.start()
    lax.fori_loop(0, nxc, finish, 0)
    send.wait()


def last_kernel(
    inv_rows,
    v_ref,
    li_ref,
    u_ref,
    s_ref,
    c_ref,
    basis_ref,
    snap_hbm,
    q_ref,
    uo_hbm,
    o_ref,
    uo_ref,
    snap_ref,
    tall_ref,
    row_ref,
    ins,
    sem,
):
    cols = li_ref.shape[0]
    known = cols - 1
    rank, depth = basis_ref.shape[:2]
    extra = snap_ref.shape[0]
    parts = ins.shape[0] - 1
    size = extra // parts
    loads = []
    for k in range(parts):
        at = pl.ds(k * size, size if k < parts - 1 else extra - k * size)
        loads.append(pltpu.make_async_copy(snap_hbm.at[at], snap_ref.at[at], ins.at[k]))
        loads[k].start()
    line = jnp.sum(v_ref[...], axis=0, keepdims=True)[:, :cols] * inv_rows
    across = lax.broadcasted_iota(jnp.int32, (1, cols), 1)
    norm = jnp.sum(jnp.where(across == known, line, 0.0), axis=1, keepdims=True)
    inverse = li_ref[...]
    coef = jnp.sum(inverse * jnp.where(across == known, 0.0, line), axis=1, keepdims=True)
    left = norm - jnp.sum(coef * coef, axis=0, keepdims=True)
    pivot = lax.rsqrt(left)
    col_id = lax.broadcasted_iota(jnp.int32, (cols, cols), 1)
    row_id = lax.broadcasted_iota(jnp.int32, (cols, cols), 0)
    edge = jnp.where(row_id == known, left * pivot, coef)
    uo_ref[...] = jnp.where(col_id == known, edge, u_ref[...])
    factor = pltpu.make_async_copy(uo_ref, uo_hbm, ins.at[parts])
    factor.start()
    weight = jnp.sum(inverse * coef, axis=0, keepdims=True) * (-pivot)
    diag = jnp.where(row_id == col_id, weight, 0.0)
    tall_ref[...] = jnp.sum(diag, axis=1, keepdims=True) * s_ref[...]

    def weighted(source, first, count, total, at):
        for k in range(count):
            value = source[k, at, :] * tall_ref[first + k : first + k + 1, :]
            total[k % 4] = value if total[k % 4] is None else total[k % 4] + value
        return (total[0] + total[1]) + (total[2] + total[3])

    def begin(q, carry):
        at = pl.ds(pl.multiple_of(q * 16, 16), 16)
        row_ref[at, :] = weighted(basis_ref, 0, rank, [c_ref[at, :] * pivot] + [None] * 3, at)
        return carry

    def finish(q, carry):
        at = pl.ds(pl.multiple_of(q * 16, 16), 16)
        row_ref[at, :] = weighted(snap_ref, rank, extra, [row_ref[at, :]] + [None] * 3, at)
        return carry

    lax.fori_loop(0, depth // 16, begin, 0)
    for load in loads:
        load.wait()
    lax.fori_loop(0, depth // 16, finish, 0)
    copy = pltpu.make_async_copy(row_ref, o_ref.at[known], sem)
    copy.start()
    factor.wait()
    copy.wait()


def in_hbm(value):
    return pltpu.with_memory_space_constraint(value, pltpu.HBM)


def in_vmem(value):
    return pltpu.with_memory_space_constraint(value, pltpu.VMEM)


def shape(dims, dtype=F32):
    return jax.ShapeDtypeStruct(dims, dtype)


def halo_x(ya, yb, post, gate):
    _, _, ny, nz = post.shape
    pack_call = pl.pallas_call(
        pack_kernel,
        out_shape=(shape((len(UP_X), ny, nz)), shape((len(DOWN_X), ny, nz))),
        in_specs=[VMEM] * 3 + [ANY],
        name="pack",
        compiler_params=params(4),
    )
    faces = pack_call(ya, yb, post, gate)
    return swap(faces, "gx")


def rounds():
    bits = {axis: [] for axis in ("gx", "gy")}
    for axis, steps in bits.items():
        bit = 1
        while bit < lax.axis_size(axis):
            steps.append((axis, bit))
            bit *= 2
    gx, gy = bits["gx"], bits["gy"]
    return gx[:1] + gy[:1] + gx[1:] + gy[1:]


def exchange(value, steps, begin, end):
    for k in range(begin, end):
        axis, bit = steps[k]
        pairs = [(s, s ^ bit) for s in range(lax.axis_size(axis))]
        other = lax.ppermute(value, axis, pairs)
        value = value + other
    return value


def on_device(populations, relax_rate, solid_mask, singular_values, basis, snapshots):
    _, nx, ny, nz = populations.shape
    rank, extra = basis.shape[0], snapshots.shape[0]
    cols = rank + extra + 1
    tail = basis.shape[1:]
    depth = tail[0] * tail[1] * tail[2]
    n_dev = lax.axis_size("gx") * lax.axis_size("gy")
    inv_rows = 1.0 / (depth * tail[3] * n_dev)
    edges = len(UP_Y) * nx
    post_shapes = (shape((NVEL, nx, ny, nz)), shape((edges, nz)), shape((edges, nz)))
    edge_rows = [pltpu.VMEM((edges, nz), F32)] * 2
    halos = [pltpu.VMEM((len(UP_X), ny, nz), F32)] * 2 + edge_rows
    post, ya, yb, omega, solid = pl.pallas_call(
        first_kernel,
        out_shape=post_shapes + (shape((nx, ny, nz)), shape((nx, ny, nz), jnp.int32)),
        in_specs=[HBM] * 3,
        scratch_shapes=[pltpu.VMEM((NVEL, nx, ny, nz), F32)]
        + edge_rows
        + [pltpu.SemaphoreType.DMA((6,))],
        name="first",
        compiler_params=params(6),
    )(*[in_hbm(value) for value in (populations, relax_rate, solid_mask)])
    ya, yb = swap((ya, yb), "gy")
    weights = in_hbm(singular_values.reshape(1, rank))
    modes = in_hbm(basis.reshape(rank, depth, 128))
    earlier = in_hbm(snapshots.reshape(extra, depth, 128))
    blocks = depth // 8
    rows, halves, gram, scale = pl.pallas_call(
        gram_kernel,
        out_shape=(
            shape((depth, cols, 128)),
            pltpu.HBM((2 * cols, depth * 128), BF16),
            shape((cols // 2, 128)),
            shape((cols, 128)),
        ),
        in_specs=[HBM, HBM, HBM, ANY],
        out_specs=(VMEM, HBM, VMEM, VMEM),
        scratch_shapes=[
            pltpu.VMEM((1, rank), F32),
            pltpu.VMEM((rank, depth, 128), F32),
            pltpu.VMEM((extra, depth, 128), F32),
            pltpu.VMEM((2 * cols, depth * 128), BF16),
            pltpu.SemaphoreType.DMA((2, blocks)),
            pltpu.SemaphoreType.DMA((blocks + 1,)),
        ],
        name="gram",
        compiler_params=params(12),
    )(weights, modes, earlier, omega)
    xa, xb = halo_x(ya, yb, post, gram)
    steps = rounds()
    first, second, third = cuts(len(steps))
    gram = exchange(gram, steps, 0, first)
    second_call = pl.pallas_call(
        second_kernel,
        out_shape=post_shapes,
        in_specs=[VMEM] * 7 + [ANY],
        scratch_shapes=edge_rows + halos,
        name="second",
        compiler_params=params(4),
    )
    post, ya, yb = second_call(post, xa, xb, ya, yb, omega, solid, gram)
    ya, yb = swap((ya, yb), "gy")
    gram = exchange(gram, steps, first, second)
    xa, xb = halo_x(ya, yb, post, gram)
    gram = exchange(gram, steps, second, third)
    final_call = pl.pallas_call(
        final_kernel,
        out_shape=(shape((NVEL, nx, ny, nz)), shape((depth, 128)), shape((n_dev, 128))),
        in_specs=[VMEM] * 7 + [ANY],
        out_specs=(ANY, VMEM, ANY),
        scratch_shapes=[
            pltpu.VMEM((nz // 128, 3 * (nx // 2) * ny, 128), F32),
            pltpu.VMEM((NVEL, nx, ny, nz), F32),
            pltpu.VMEM((n_dev, 128), F32),
            pltpu.SemaphoreType.DMA((nx // 2 + 1,)),
        ]
        + halos,
        name="final",
        compiler_params=params(6),
    )
    field, coarse, line = final_call(post, xa, xb, ya, yb, solid, rows, gram)
    lines = lax.all_to_all(line, ("gx", "gy"), 0, 0, tiled=True)
    gram = exchange(gram, steps, third, len(steps))
    upper, inverse, split = pl.pallas_call(
        lambda *refs: factor_kernel(inv_rows, *refs),
        out_shape=(shape((cols, cols)), shape((cols, cols)), shape((cols, 3 * cols))),
        name="factor",
        compiler_params=params(4),
    )(gram)
    rotated = pl.pallas_call(
        rotate_kernel,
        out_shape=shape((cols, depth, 128)),
        in_specs=[VMEM, HBM],
        out_specs=ANY,
        scratch_shapes=[
            pltpu.VMEM((2 * cols, depth * 128), BF16),
            pltpu.VMEM((cols, depth, 128), F32),
            pltpu.SemaphoreType.DMA((blocks,)),
            pltpu.SemaphoreType.DMA((blocks,)),
        ],
        name="rotate",
        compiler_params=params(12),
    )(split, in_hbm(halves))
    upper, rotated = pl.pallas_call(
        lambda *refs: last_kernel(inv_rows, *refs),
        out_shape=(shape((cols, cols)), shape((cols, depth, 128))),
        in_specs=[VMEM] * 6 + [HBM, ANY],
        out_specs=(ANY, ANY),
        scratch_shapes=[
            pltpu.VMEM((cols, cols), F32),
            pltpu.VMEM((extra, depth, 128), F32),
            pltpu.VMEM((cols, 128), F32),
            pltpu.VMEM((depth, 128), F32),
            pltpu.SemaphoreType.DMA((2,)),
            pltpu.SemaphoreType.DMA,
        ],
        input_output_aliases={7: 1},
        name="last",
        compiler_params=params(2),
    )(lines, inverse, upper, scale, coarse, in_vmem(basis.reshape(rank, depth, 128)), earlier, rotated)
    return field, upper, rotated.reshape((cols,) + tail)


def solution(mesh):
    return jax.shard_map(
        on_device,
        mesh=mesh,
        in_specs=(
            P(None, "gx", "gy", None),
            P("gx", "gy", None),
            P("gx", "gy", None),
            P(),
            P(None, None, "gx", "gy", None),
            P(None, None, "gx", "gy", None),
        ),
        out_specs=(P(None, "gx", "gy", None), P(), P(None, None, "gx", "gy", None)),
        check_vma=False,
    )
```

```python
import jax
import jax.numpy as jnp
from jax import lax
from jax.experimental import pallas as pl
from jax.experimental.pallas import tpu as pltpu
from jax.sharding import PartitionSpec as P


velocity_table = [
    (0, 0, 0),
    (1, 0, 0),
    (-1, 0, 0),
    (0, 1, 0),
    (0, -1, 0),
    (0, 0, 1),
    (0, 0, -1),
    (1, 1, 0),
    (-1, -1, 0),
    (1, -1, 0),
    (-1, 1, 0),
    (1, 0, 1),
    (-1, 0, -1),
    (1, 0, -1),
    (-1, 0, 1),
    (0, 1, 1),
    (0, -1, -1),
    (0, 1, -1),
    (0, -1, 1),
]
NVEL = 19
PAIRS = [(i, i + 1) for i in range(1, NVEL, 2)]
W_REST, W_FACE, W_EDGE = 1.0 / 3.0, 1.0 / 18.0, 1.0 / 36.0
UP_X = [i for i in range(NVEL) if velocity_table[i][0] == 1]
DOWN_X = [i for i in range(NVEL) if velocity_table[i][0] == -1]
UP_Y = [i for i in range(NVEL) if velocity_table[i][1] == 1]
DOWN_Y = [i for i in range(NVEL) if velocity_table[i][1] == -1]
SPEED_SCALE = 10.0
UNROLL = 4
CUTS = (1, 3, 4)


def cuts(count):
    return tuple(count * cut // 5 for cut in CUTS)


UNROLL_F = 2
HIGHEST = lax.Precision.HIGHEST
F32 = jnp.float32
BF16 = jnp.bfloat16
VMEM = pl.BlockSpec(memory_space=pltpu.VMEM)
ANY = pl.BlockSpec(memory_space=pl.ANY)
HBM = pl.BlockSpec(memory_space=pltpu.HBM)


def params(mib=40):
    return pltpu.CompilerParams(vmem_limit_bytes=mib << 20)


def ring_pairs(axis):
    count = lax.axis_size(axis)
    partner = [(s, s ^ 1) for s in range(count)]
    other = [(s, (s + 1 if s % 2 else s - 1) % count) for s in range(count)]
    return partner, other


def swap(values, axis):
    partner, other = ring_pairs(axis)
    near = lax.ppermute(values[0], axis, partner)
    far = lax.ppermute(values[1], axis, other)
    return near, far


def by_parity(axis, place):
    odd = lax.rem(lax.axis_index(axis), 2)

    @pl.when(odd == 0)
    def _():
        place(0)

    @pl.when(odd == 1)
    def _():
        place(1)


def moments(f):
    plus = [f[a] + f[b] for a, b in PAIRS]
    minus = [f[a] - f[b] for a, b in PAIRS]
    rho = f[0] + plus[0]
    for p in plus[1:]:
        rho = rho + p
    mx, my, mz, m7, m9, m11, m13, m15, m17 = minus
    jx = (mx + m7) + (m9 + m11) + m13
    jy = (my + m7) + (m15 + m17) - m9
    jz = (mz + m11) + (m15 - m13) - m17
    r = 1.0 / rho
    return rho, (jx * r, jy * r, jz * r)


def collide(f, omega, solid):
    rho, u = moments(f)
    base = 1.0 - 1.5 * (u[0] * u[0] + u[1] * u[1] + u[2] * u[2])
    keep = 1.0 - omega
    wr = omega * rho
    post = [None] * NVEL
    post[0] = jnp.where(solid, f[0], keep * f[0] + (W_REST * wr) * base)
    w_face, w_edge = W_FACE * wr, W_EDGE * wr
    for a, b in PAIRS:
        vel = velocity_table[a]
        along = None
        for axis in range(3):
            if vel[axis] == 1:
                along = u[axis] if along is None else along + u[axis]
            elif vel[axis] == -1:
                along = along - u[axis]
        w = w_face if a < 7 else w_edge
        even = w * (base + 4.5 * (along * along))
        odd = w * (3.0 * along)
        post[a] = jnp.where(solid, f[b], keep * f[a] + (even + odd))
        post[b] = jnp.where(solid, f[a], keep * f[b] + (even - odd))
    return post


def emit_post(post, x, nx, post_ref, yup_ref, ydn_ref):
    ny = post_ref.shape[2]
    for i in range(NVEL):
        cz = velocity_table[i][2]
        value = post[i] if cz == 0 else pltpu.roll(post[i], cz % post[i].shape[1], 1)
        post_ref[i, x] = value
        if i in UP_Y:
            yup_ref[pl.ds(UP_Y.index(i) * nx + x, 1), :] = value[ny - 1 : ny, :]
        if i in DOWN_Y:
            ydn_ref[pl.ds(DOWN_Y.index(i) * nx + x, 1), :] = value[0:1, :]


def emit_edges(yup_ref, ydn_ref, edges):
    def place(odd):
        edges[odd][...] = yup_ref[...]
        edges[1 - odd][...] = ydn_ref[...]

    by_parity("gy", place)


def sort_halos(xa_ref, xb_ref, ya_ref, yb_ref, xup_ref, xdn_ref, yup_ref, ydn_ref):
    def place_x(odd):
        xup_ref[...] = (xb_ref, xa_ref)[odd][...]
        xdn_ref[...] = (xa_ref, xb_ref)[odd][...]

    def place_y(odd):
        yup_ref[...] = (yb_ref, ya_ref)[odd][...]
        ydn_ref[...] = (ya_ref, yb_ref)[odd][...]

    by_parity("gx", place_x)
    by_parity("gy", place_y)


def first_kernel(
    f_hbm, om_hbm, so_hbm, post_ref, ya_ref, yb_ref, om_ref, so_ref, f_ref, yup_ref, ydn_ref, sem
):
    nx = f_ref.shape[1]
    parts = sem.shape[0] - 2
    rows = nx // parts

    def load(k):
        at = pl.ds(k * rows, rows)
        return pltpu.make_async_copy(f_hbm.at[:, at], f_ref.at[:, at], sem.at[k])

    loads = [load(k) for k in range(parts)]
    omega = pltpu.make_async_copy(om_hbm, om_ref, sem.at[parts])
    solid = pltpu.make_async_copy(so_hbm, so_ref, sem.at[parts + 1])
    omega.start()
    solid.start()
    for k in range(parts):
        loads[k].start()

    def step(x, carry):
        post = collide([f_ref[i, x] for i in range(NVEL)], om_ref[x], so_ref[x] > 0)
        emit_post(post, x, nx, post_ref, yup_ref, ydn_ref)
        return carry

    for k in range(parts):
        loads[k].wait()
        if k == 0:
            omega.wait()
            solid.wait()
        lax.fori_loop(k * rows, (k + 1) * rows, step, 0, unroll=UNROLL)
    emit_edges(yup_ref, ydn_ref, (ya_ref, yb_ref))


def shift_y(i, value, src, nx, yup_ref, ydn_ref):
    ny = value.shape[0]
    cy = velocity_table[i][1]
    if cy == 0:
        return value
    row_id = lax.broadcasted_iota(jnp.int32, value.shape, 0)
    if cy == 1:
        edge = yup_ref[pl.ds(UP_Y.index(i) * nx + src, 1), :]
        return jnp.where(row_id == 0, edge, pltpu.roll(value, 1, 0))
    edge = ydn_ref[pl.ds(DOWN_Y.index(i) * nx + src, 1), :]
    return jnp.where(row_id == ny - 1, edge, pltpu.roll(value, ny - 1, 0))


def streamed(x, nx, post_ref, xup_ref, xdn_ref, yup_ref, ydn_ref):
    f = []
    for i in range(NVEL):
        cx = velocity_table[i][0]
        src = x if cx == 0 else lax.rem(x + (nx - cx), nx)
        value = shift_y(i, post_ref[i, src], src, nx, yup_ref, ydn_ref)
        if cx == 1:
            value = jnp.where(x == 0, xup_ref[UP_X.index(i)], value)
        elif cx == -1:
            value = jnp.where(x == nx - 1, xdn_ref[DOWN_X.index(i)], value)
        f.append(value)
    return f


def second_kernel(
    p_ref,
    ra_ref,
    rb_ref,
    sa_ref,
    sb_ref,
    om_ref,
    so_ref,
    gate_ref,
    post_ref,
    ya_ref,
    yb_ref,
    yup_ref,
    ydn_ref,
    *halos,
):
    nx = p_ref.shape[1]
    sort_halos(ra_ref, rb_ref, sa_ref, sb_ref, *halos)

    def step(x, carry):
        f = streamed(x, nx, p_ref, *halos)
        post = collide(f, om_ref[x], so_ref[x] > 0)
        emit_post(post, x, nx, post_ref, yup_ref, ydn_ref)
        return carry

    lax.fori_loop(0, nx, step, 0, unroll=2 * UNROLL)
    emit_edges(yup_ref, ydn_ref, (ya_ref, yb_ref))


def pack_kernel(ya_ref, yb_ref, post_ref, gate_ref, xa_ref, xb_ref):
    nx = post_ref.shape[1]

    def place(odd_y):
        yup_ref, ydn_ref = ((yb_ref, ya_ref), (ya_ref, yb_ref))[odd_y]

        def faces(odd_x):
            up_ref, down_ref = ((xa_ref, xb_ref), (xb_ref, xa_ref))[odd_x]
            for k, i in enumerate(UP_X):
                up_ref[k] = shift_y(i, post_ref[i, nx - 1], nx - 1, nx, yup_ref, ydn_ref)
            for k, i in enumerate(DOWN_X):
                down_ref[k] = shift_y(i, post_ref[i, 0], 0, nx, yup_ref, ydn_ref)

        by_parity("gx", faces)

    by_parity("gy", place)


def gram_kernel(
    s_hbm, basis_hbm, snap_hbm, gate_ref, a_ref, h_hbm, g_ref, t_ref, s_ref, basis_ref, snap_ref, h_ref, ins, outs
):
    rank = basis_ref.shape[0]
    depth = basis_ref.shape[1]
    extra = snap_ref.shape[0]
    cols = a_ref.shape[1]
    weights = pltpu.make_async_copy(s_hbm, s_ref, outs.at[depth // 8])
    weights.start()
    zero = jnp.zeros((cols - rank - extra, 8, 128), F32)

    def load(q):
        at = pl.ds(pl.multiple_of(q * 8, 8), 8)
        return (
            pltpu.make_async_copy(basis_hbm.at[:, at], basis_ref.at[:, at], ins.at[0, q]),
            pltpu.make_async_copy(snap_hbm.at[:, at], snap_ref.at[:, at], ins.at[1, q]),
        )

    def save(q):
        at = pl.ds(pl.multiple_of(q * 1024, 1024), 1024)
        return pltpu.make_async_copy(h_ref.at[:, at], h_hbm.at[:, at], outs.at[q])

    def begin(q, carry):
        for copy in load(q):
            copy.start()
        return carry

    def finish(q, carry):
        save(q).wait()
        return carry

    lax.fori_loop(0, depth // 8, begin, 0)
    weights.wait()
    same = lax.broadcasted_iota(jnp.int32, (rank, rank), 0) == lax.broadcasted_iota(
        jnp.int32, (rank, rank), 1
    )
    scale = jnp.sum(jnp.where(same, s_ref[...], 0.0), axis=1, keepdims=True)
    scale = jnp.broadcast_to(scale, (rank, 128))
    t_ref[...] = jnp.concatenate([scale, jnp.ones((cols - rank, 128), F32)], axis=0)

    def step(q, carry):
        for copy in load(q):
            copy.wait()
        r = pl.multiple_of(q * 8, 8)
        top = jnp.swapaxes(basis_ref[:, pl.ds(r, 8), :], 0, 1)
        low = jnp.concatenate([snap_ref[:, pl.ds(r, 8), :], zero], axis=0)
        low = jnp.swapaxes(low, 0, 1)
        for t in range(8):
            rows = jnp.concatenate([top[t] * scale, low[t]], axis=0)
            a_ref[r + t] = rows
            at = pl.ds(pl.multiple_of((r + t) * 128, 128), 128)
            high = rows.astype(BF16)
            h_ref[0:cols, at] = high
            h_ref[cols : 2 * cols, at] = (rows - high.astype(F32)).astype(BF16)
        save(q).start()
        return carry

    lax.fori_loop(0, depth // 8, step, 0)
    acc = lax.dot_general(
        h_ref[...], h_ref[0:cols, :], (((1,), (1,)), ((), ())), preferred_element_type=F32
    )
    cross = acc[cols:, :]
    eye = (
        lax.broadcasted_iota(jnp.int32, (cols, cols), 0)
        == lax.broadcasted_iota(jnp.int32, (cols, cols), 1)
    ).astype(F32)
    flipped = lax.dot_general(
        eye, cross, (((1,), (1,)), ((), ())), precision=HIGHEST, preferred_element_type=F32
    )
    total = acc[:cols, :] + cross + flipped
    half, width = g_ref.shape
    total = jnp.concatenate([total, jnp.zeros((cols, width - cols), F32)], axis=1)
    lane = lax.broadcasted_iota(jnp.int32, (half, width), 1)
    g_ref[...] = jnp.where(lane < cols, total[:half], pltpu.roll(total[half:], half, 1))
    lax.fori_loop(0, depth // 8, finish, 0)


def factor_kernel(inv_rows, g_ref, u_ref, li_ref, w_ref):
    half, width = g_ref.shape
    cols = 2 * half
    known = cols - 1
    blocks = cols // 8
    top = g_ref[...] * inv_rows
    pick = (
        lax.broadcasted_iota(jnp.int32, (half, width), 1)
        == lax.broadcasted_iota(jnp.int32, (half, width), 0) + half
    ).astype(F32)
    mirror = lax.dot_general(
        pick, top, (((1,), (1,)), ((), ())), precision=HIGHEST, preferred_element_type=F32
    )
    mirror = jnp.concatenate([mirror, jnp.zeros((half, width - half), F32)], axis=1)
    across = lax.broadcasted_iota(jnp.int32, (half, width), 1)
    bottom = jnp.where(across < half, mirror, pltpu.roll(top, width - half, 1))
    gram = jnp.concatenate([top, bottom], axis=0)
    sub = lax.broadcasted_iota(jnp.int32, (8, 128), 0)
    lane = lax.broadcasted_iota(jnp.int32, (8, 128), 1)
    left = [gram[8 * b : 8 * b + 8, :] for b in range(blocks)]
    right = [(sub + 8 * b == lane).astype(F32) for b in range(blocks)]
    for p in range(blocks):
        live = range(p, blocks)
        width = min(8, known - 8 * p)
        col = [
            {
                b: jnp.broadcast_to(left[b][:, 8 * p + t : 8 * p + t + 1], (8, 128))
                for b in live
            }
            for t in range(width)
        ]
        for t in range(width):
            pivot = lax.rsqrt(jnp.broadcast_to(col[t][p][t : t + 1, :], (8, 128)))
            lcol = {b: col[t][b] * pivot for b in live}
            lcol[p] = jnp.where(sub > t, lcol[p], 0.0)
            for v in range(t + 1, width):
                m = jnp.broadcast_to(lcol[p][v : v + 1, :], (8, 128))
                for b in live:
                    col[v][b] = col[v][b] - lcol[b] * m
            top = jnp.broadcast_to(left[p][t : t + 1, :], (8, 128)) * pivot
            aug = jnp.broadcast_to(right[p][t : t + 1, :], (8, 128)) * pivot
            for b in live:
                left[b] = left[b] - lcol[b] * top
                right[b] = right[b] - lcol[b] * aug
            left[p] = jnp.where(sub == t, top, left[p])
            right[p] = jnp.where(sub == t, aug, right[p])
    fill = jnp.zeros((8, 128), F32)
    for b in range(blocks):
        row = sub + 8 * b
        upper = jnp.where(jnp.logical_and(row <= lane, lane < known), left[b], 0.0)
        inverse = jnp.where(jnp.logical_and(row >= lane, row < known), right[b], 0.0)
        u_ref[8 * b : 8 * b + 8, :] = upper[:, :cols]
        li_ref[8 * b : 8 * b + 8, :] = inverse[:, :cols]
        high = inverse.astype(BF16).astype(F32)
        wide = jnp.concatenate([high, fill], axis=1)
        rest = jnp.concatenate([inverse - high, fill], axis=1)
        wide = wide + pltpu.roll(rest, cols, 1) + pltpu.roll(wide, 2 * cols, 1)
        w_ref[8 * b : 8 * b + 8, :] = wide[:, : 3 * cols]


def rotate_kernel(w_ref, h_hbm, o_ref, h_ref, out_ref, ins, sem):
    cols = w_ref.shape[0]
    depth = out_ref.shape[1]
    weight = w_ref[...].astype(BF16)

    def copy(q):
        at = pl.ds(pl.multiple_of(q * 16, 16), 16)
        return pltpu.make_async_copy(out_ref.at[:, at, :], o_ref.at[:, at, :], sem.at[q])

    def load(q):
        at = pl.ds(pl.multiple_of(q * 2048, 2048), 2048)
        return pltpu.make_async_copy(h_hbm.at[:, at], h_ref.at[:, at], ins.at[q])

    def begin(q, carry):
        load(q).start()
        return carry

    lax.fori_loop(0, depth // 16, begin, 0)

    def step(q, carry):
        load(q).wait()
        at = pl.ds(pl.multiple_of(q * 2048, 2048), 2048)
        high = h_ref[0:cols, at]
        low = h_ref[cols : 2 * cols, at]
        res = lax.dot_general(
            weight,
            jnp.concatenate([high, high, low], axis=0),
            (((1,), (0,)), ((), ())),
            preferred_element_type=F32,
        )
        res = jnp.stack([res[:, t * 128 : (t + 1) * 128] for t in range(16)], axis=0)
        out_ref[:, pl.ds(pl.multiple_of(q * 16, 16), 16), :] = jnp.swapaxes(res, 0, 1)
        copy(q).start()
        return carry

    lax.fori_loop(0, depth // 16, step, 0)

    def finish(q, carry):
        copy(q).wait()
        return carry

    lax.fori_loop(0, depth // 16, finish, 0)


def final_kernel(
    p_ref, ra_ref, rb_ref, sa_ref, sb_ref, so_ref, a_ref, gate_ref, f_hbm, c_ref, v_hbm, vel_ref, f_ref, v_ref, sem, *halos
):
    nx, ny, nz = p_ref.shape[1:]
    nxc, nyc = nx // 2, ny // 2
    sort_halos(ra_ref, rb_ref, sa_ref, sb_ref, *halos)

    def copy(xc):
        at = pl.ds(2 * xc, 2)
        return pltpu.make_async_copy(f_ref.at[:, at], f_hbm.at[:, at], sem.at[xc])

    def finish(xc, carry):
        copy(xc).wait()
        return carry

    def step(xc, carry):
        total = [None] * 3
        for t in range(2):
            x = 2 * xc + t
            f = streamed(x, nx, p_ref, *halos)
            for i in range(NVEL):
                f_ref[i, x] = f[i]
            _, u = moments(f)
            fluid = (so_ref[x] == 0).astype(F32)
            for k in range(3):
                part = u[k] * fluid
                total[k] = part if t == 0 else total[k] + part
        for k in range(3):
            at = pl.multiple_of((k * nxc + xc) * ny, ny)
            for t in range(nz // 128):
                vel_ref[t, pl.ds(at, ny), :] = total[k][:, t * 128 : (t + 1) * 128]
        copy(xc).start()
        return carry

    lax.fori_loop(0, nxc, step, 0, unroll=UNROLL_F)
    depth = 3 * nxc * nyc
    pairs = []
    for t in range(nz // 128):
        half = vel_ref.at[t]
        pairs.append(half[pl.ds(0, depth, stride=2), :] + half[pl.ds(1, depth, stride=2), :])
    pairs = jnp.concatenate(pairs, axis=1)
    pick = (
        lax.broadcasted_iota(jnp.int32, (nz, nz // 2), 0) // 2
        == lax.broadcasted_iota(jnp.int32, (nz, nz // 2), 1)
    ).astype(F32)
    coarse = lax.dot_general(
        pairs, pick, (((1,), (0,)), ((), ())), precision=HIGHEST, preferred_element_type=F32
    )
    c_ref[...] = coarse * (SPEED_SCALE / 8.0)
    cols = a_ref.shape[1]

    def inner(r, acc):
        return acc + a_ref[r] * c_ref[pl.ds(r, 1), :]

    acc = lax.fori_loop(0, depth, inner, jnp.zeros((cols, 128), F32), unroll=16)
    dots = jnp.sum(acc, axis=1, keepdims=True)
    own = jnp.sum(c_ref[...] * c_ref[...])
    down = lax.broadcasted_iota(jnp.int32, (cols, 1), 0)
    dots = jnp.where(down == cols - 1, own, dots)
    across = lax.broadcasted_iota(jnp.int32, (cols, 128), 1)
    diag = jnp.where(across == lax.broadcasted_iota(jnp.int32, (cols, 128), 0), dots, 0.0)
    line = jnp.sum(diag, axis=0, keepdims=True)
    v_ref[...] = jnp.broadcast_to(line, v_ref.shape)
    send = pltpu.make_async_copy(v_ref, v_hbm, sem.at[nxc])
    send.start()
    lax.fori_loop(0, nxc, finish, 0)
    send.wait()


def last_kernel(
    inv_rows,
    v_ref,
    li_ref,
    u_ref,
    s_ref,
    c_ref,
    basis_ref,
    snap_hbm,
    q_ref,
    uo_hbm,
    o_ref,
    uo_ref,
    snap_ref,
    tall_ref,
    row_ref,
    ins,
    sem,
):
    cols = li_ref.shape[0]
    known = cols - 1
    rank, depth = basis_ref.shape[:2]
    extra = snap_ref.shape[0]
    parts = ins.shape[0] - 1
    size = extra // parts
    loads = []
    for k in range(parts):
        at = pl.ds(k * size, size if k < parts - 1 else extra - k * size)
        loads.append(pltpu.make_async_copy(snap_hbm.at[at], snap_ref.at[at], ins.at[k]))
        loads[k].start()
    line = jnp.sum(v_ref[...], axis=0, keepdims=True)[:, :cols] * inv_rows
    across = lax.broadcasted_iota(jnp.int32, (1, cols), 1)
    norm = jnp.sum(jnp.where(across == known, line, 0.0), axis=1, keepdims=True)
    inverse = li_ref[...]
    coef = jnp.sum(inverse * jnp.where(across == known, 0.0, line), axis=1, keepdims=True)
    left = norm - jnp.sum(coef * coef, axis=0, keepdims=True)
    pivot = lax.rsqrt(left)
    col_id = lax.broadcasted_iota(jnp.int32, (cols, cols), 1)
    row_id = lax.broadcasted_iota(jnp.int32, (cols, cols), 0)
    edge = jnp.where(row_id == known, left * pivot, coef)
    uo_ref[...] = jnp.where(col_id == known, edge, u_ref[...])
    factor = pltpu.make_async_copy(uo_ref, uo_hbm, ins.at[parts])
    factor.start()
    weight = jnp.sum(inverse * coef, axis=0, keepdims=True) * (-pivot)
    diag = jnp.where(row_id == col_id, weight, 0.0)
    tall_ref[...] = jnp.sum(diag, axis=1, keepdims=True) * s_ref[...]

    def weighted(source, first, count, total, at):
        for k in range(count):
            value = source[k, at, :] * tall_ref[first + k : first + k + 1, :]
            total[k % 4] = value if total[k % 4] is None else total[k % 4] + value
        return (total[0] + total[1]) + (total[2] + total[3])

    def begin(q, carry):
        at = pl.ds(pl.multiple_of(q * 16, 16), 16)
        row_ref[at, :] = weighted(basis_ref, 0, rank, [c_ref[at, :] * pivot] + [None] * 3, at)
        return carry

    def finish(q, carry):
        at = pl.ds(pl.multiple_of(q * 16, 16), 16)
        row_ref[at, :] = weighted(snap_ref, rank, extra, [row_ref[at, :]] + [None] * 3, at)
        return carry

    lax.fori_loop(0, depth // 16, begin, 0)
    for load in loads:
        load.wait()
    lax.fori_loop(0, depth // 16, finish, 0)
    copy = pltpu.make_async_copy(row_ref, o_ref.at[known], sem)
    copy.start()
    factor.wait()
    copy.wait()


def in_hbm(value):
    return pltpu.with_memory_space_constraint(value, pltpu.HBM)


def in_vmem(value):
    return pltpu.with_memory_space_constraint(value, pltpu.VMEM)


def shape(dims, dtype=F32):
    return jax.ShapeDtypeStruct(dims, dtype)


def halo_x(ya, yb, post, gate):
    _, _, ny, nz = post.shape
    pack_call = pl.pallas_call(
        pack_kernel,
        out_shape=(shape((len(UP_X), ny, nz)), shape((len(DOWN_X), ny, nz))),
        in_specs=[VMEM] * 3 + [ANY],
        name="pack",
        compiler_params=params(4),
    )
    faces = pack_call(ya, yb, post, gate)
    return swap(faces, "gx")


def rounds():
    bits = {axis: [] for axis in ("gx", "gy")}
    for axis, steps in bits.items():
        bit = 1
        while bit < lax.axis_size(axis):
            steps.append((axis, bit))
            bit *= 2
    gx, gy = bits["gx"], bits["gy"]
    return gx[:1] + gy[:1] + gx[1:] + gy[1:]


def exchange(value, steps, begin, end):
    for k in range(begin, end):
        axis, bit = steps[k]
        pairs = [(s, s ^ bit) for s in range(lax.axis_size(axis))]
        other = lax.ppermute(value, axis, pairs)
        value = value + other
    return value


def on_device(populations, relax_rate, solid_mask, singular_values, basis, snapshots):
    _, nx, ny, nz = populations.shape
    rank, extra = basis.shape[0], snapshots.shape[0]
    cols = rank + extra + 1
    tail = basis.shape[1:]
    depth = tail[0] * tail[1] * tail[2]
    n_dev = lax.axis_size("gx") * lax.axis_size("gy")
    inv_rows = 1.0 / (depth * tail[3] * n_dev)
    edges = len(UP_Y) * nx
    post_shapes = (shape((NVEL, nx, ny, nz)), shape((edges, nz)), shape((edges, nz)))
    edge_rows = [pltpu.VMEM((edges, nz), F32)] * 2
    halos = [pltpu.VMEM((len(UP_X), ny, nz), F32)] * 2 + edge_rows
    post, ya, yb, omega, solid = pl.pallas_call(
        first_kernel,
        out_shape=post_shapes + (shape((nx, ny, nz)), shape((nx, ny, nz), jnp.int32)),
        in_specs=[HBM] * 3,
        scratch_shapes=[pltpu.VMEM((NVEL, nx, ny, nz), F32)]
        + edge_rows
        + [pltpu.SemaphoreType.DMA((6,))],
        name="first",
        compiler_params=params(6),
    )(*[in_hbm(value) for value in (populations, relax_rate, solid_mask)])
    ya, yb = swap((ya, yb), "gy")
    weights = in_hbm(singular_values.reshape(1, rank))
    modes = in_hbm(basis.reshape(rank, depth, 128))
    earlier = in_hbm(snapshots.reshape(extra, depth, 128))
    blocks = depth // 8
    rows, halves, gram, scale = pl.pallas_call(
        gram_kernel,
        out_shape=(
            shape((depth, cols, 128)),
            pltpu.HBM((2 * cols, depth * 128), BF16),
            shape((cols // 2, 128)),
            shape((cols, 128)),
        ),
        in_specs=[HBM, HBM, HBM, ANY],
        out_specs=(VMEM, HBM, VMEM, VMEM),
        scratch_shapes=[
            pltpu.VMEM((1, rank), F32),
            pltpu.VMEM((rank, depth, 128), F32),
            pltpu.VMEM((extra, depth, 128), F32),
            pltpu.VMEM((2 * cols, depth * 128), BF16),
            pltpu.SemaphoreType.DMA((2, blocks)),
            pltpu.SemaphoreType.DMA((blocks + 1,)),
        ],
        name="gram",
        compiler_params=params(12),
    )(weights, modes, earlier, omega)
    xa, xb = halo_x(ya, yb, post, gram)
    steps = rounds()
    first, second, third = cuts(len(steps))
    gram = exchange(gram, steps, 0, first)
    second_call = pl.pallas_call(
        second_kernel,
        out_shape=post_shapes,
        in_specs=[VMEM] * 7 + [ANY],
        scratch_shapes=edge_rows + halos,
        name="second",
        compiler_params=params(4),
    )
    post, ya, yb = second_call(post, xa, xb, ya, yb, omega, solid, gram)
    ya, yb = swap((ya, yb), "gy")
    gram = exchange(gram, steps, first, second)
    xa, xb = halo_x(ya, yb, post, gram)
    gram = exchange(gram, steps, second, third)
    final_call = pl.pallas_call(
        final_kernel,
        out_shape=(shape((NVEL, nx, ny, nz)), shape((depth, 128)), shape((n_dev, 128))),
        in_specs=[VMEM] * 7 + [ANY],
        out_specs=(ANY, VMEM, ANY),
        scratch_shapes=[
            pltpu.VMEM((nz // 128, 3 * (nx // 2) * ny, 128), F32),
            pltpu.VMEM((NVEL, nx, ny, nz), F32),
            pltpu.VMEM((n_dev, 128), F32),
            pltpu.SemaphoreType.DMA((nx // 2 + 1,)),
        ]
        + halos,
        name="final",
        compiler_params=params(6),
    )
    field, coarse, line = final_call(post, xa, xb, ya, yb, solid, rows, gram)
    lines = lax.all_to_all(line, ("gx", "gy"), 0, 0, tiled=True)
    gram = exchange(gram, steps, third, len(steps))
    upper, inverse, split = pl.pallas_call(
        lambda *refs: factor_kernel(inv_rows, *refs),
        out_shape=(shape((cols, cols)), shape((cols, cols)), shape((cols, 3 * cols))),
        name="factor",
        compiler_params=params(4),
    )(gram)
    rotated = pl.pallas_call(
        rotate_kernel,
        out_shape=shape((cols, depth, 128)),
        in_specs=[VMEM, HBM],
        out_specs=ANY,
        scratch_shapes=[
            pltpu.VMEM((2 * cols, depth * 128), BF16),
            pltpu.VMEM((cols, depth, 128), F32),
            pltpu.SemaphoreType.DMA((blocks,)),
            pltpu.SemaphoreType.DMA((blocks,)),
        ],
        name="rotate",
        compiler_params=params(12),
    )(split, in_hbm(halves))
    upper, rotated = pl.pallas_call(
        lambda *refs: last_kernel(inv_rows, *refs),
        out_shape=(shape((cols, cols)), shape((cols, depth, 128))),
        in_specs=[VMEM] * 6 + [HBM, ANY],
        out_specs=(ANY, ANY),
        scratch_shapes=[
            pltpu.VMEM((cols, cols), F32),
            pltpu.VMEM((extra, depth, 128), F32),
            pltpu.VMEM((cols, 128), F32),
            pltpu.VMEM((depth, 128), F32),
            pltpu.SemaphoreType.DMA((2,)),
            pltpu.SemaphoreType.DMA,
        ],
        input_output_aliases={7: 1},
        name="last",
        compiler_params=params(2),
    )(lines, inverse, upper, scale, coarse, in_vmem(basis.reshape(rank, depth, 128)), earlier, rotated)
    return field, upper, rotated.reshape((cols,) + tail)


def solution(mesh):
    return jax.shard_map(
        on_device,
        mesh=mesh,
        in_specs=(
            P(None, "gx", "gy", None),
            P("gx", "gy", None),
            P("gx", "gy", None),
            P(),
            P(None, None, "gx", "gy", None),
            P(None, None, "gx", "gy", None),
        ),
        out_specs=(P(None, "gx", "gy", None), P(), P(None, None, "gx", "gy", None)),
        check_vma=False,
    )
```
